32 devices in a mesh: dp: 4 (over y, x), seq: 8 (over z, core).
Axes of the slice: x: 2, y: 2, z: 4, core: 2. Of those that a mesh axis runs over, the one named last changes fastest.
Arguments:
- hidden_in: bfloat16 [4, 1024, 2048], P('dp', 'seq'), may hold values from -6 to 6
- segment_ids: int32 [4, 1024], P('dp', 'seq'), may hold values from 0 to 3, never falling along the last dimension, each value on 1 to 512 neighbouring positions
- grad_out: bfloat16 [4, 1024, 2048], P('dp', 'seq'), may hold values from -6 to 6
- attn_gain: float32 [2048], replicated, may hold values from 0.5 to 1.5
- w_query: float32 [2048, 1536], P(('dp', 'seq')), may hold values from -0.125 to 0.125
- w_key: float32 [2048, 1536], P(('dp', 'seq')), may hold values from -0.125 to 0.125
- w_value: float32 [2048, 3072], P(('dp', 'seq')), may hold values from -0.125 to 0.125
- w_decay: float32 [2048, 6], P(('dp', 'seq')), may hold values from -0.125 to 0.125
- w_beta: float32 [2048, 6], P(('dp', 'seq')), may hold values from -0.125 to 0.125
- w_outgate: float32 [2048, 3072], P(('dp', 'seq')), may hold values from -0.125 to 0.125
- a_log: float32 [6], replicated, may hold values from -10 to -3
- conv_query: float32 [4, 1536], replicated, may hold values from -3 to 3
- conv_key: float32 [4, 1536], replicated, may hold values from -3 to 3
- conv_value: float32 [4, 3072], replicated, may hold values from -3 to 3
- out_gain: float32 [512], replicated, may hold values from 0.5 to 1.5
- w_output: float32 [2048, 3072], P(('dp', 'seq')), may hold values from -0.109375 to 0.109375
- mlp_gain: float32 [2048], replicated, may hold values from 0.5 to 1.5
- w_gate: float32 [2048, 5632], P(('dp', 'seq')), may hold values from -0.125 to 0.125
- w_up: float32 [2048, 5632], P(('dp', 'seq')), may hold values from -0.125 to 0.125
- w_down: float32 [2048, 5632], P(('dp', 'seq')), may hold values from -0.078125 to 0.078125
Outputs:
- hidden_out: bfloat16 [4, 1024, 2048], P('dp', 'seq')
- grad_in: bfloat16 [4, 1024, 2048], P('dp', 'seq')
- grad_attn_gain: float32 [2048], replicated
- grad_w_query: float32 [2048, 1536], P(('dp', 'seq'))
- grad_w_key: float32 [2048, 1536], P(('dp', 'seq'))
- grad_w_value: float32 [2048, 3072], P(('dp', 'seq'))
- grad_w_decay: float32 [2048, 6], P(('dp', 'seq'))
- grad_w_beta: float32 [2048, 6], P(('dp', 'seq'))
- grad_w_outgate: float32 [2048, 3072], P(('dp', 'seq'))
- grad_a_log: float32 [6], replicated
- grad_conv_query: float32 [4, 1536], replicated
- grad_conv_key: float32 [4, 1536], replicated
- grad_conv_value: float32 [4, 3072], replicated
- grad_out_gain: float32 [512], replicated
- grad_w_output: float32 [2048, 3072], P(('dp', 'seq'))
- grad_mlp_gain: float32 [2048], replicated
- grad_w_gate: float32 [2048, 5632], P(('dp', 'seq'))
- grad_w_up: float32 [2048, 5632], P(('dp', 'seq'))
- grad_w_down: float32 [2048, 5632], P(('dp', 'seq'))
The draws below stay inside these ranges and needn't reach their ends.
Inputs may be any that keep to these rules, and one draw needn't show every extreme that they name: `segment_ids`: document numbers of a packed row start at 0 and never fall; a document holds at most half of the row's 1024 tokens, and one holds exactly that many.
All inputs are finite; a program needn't handle non-finite values.
Results may differ from the reference program's by a relative error of at most 0.015.
The reference program's roundings to bfloat16 on the way count: a program that leaves them out, or rounds other values in their place, can miss the bound.
Values may be sent and summed in bfloat16 or wider, within the bound.
A program may use at most 768 MiB of HBM per device.

```python
import math
import jax
import jax.numpy as jnp
import numpy as np
from jax import lax

D = 2048
H = 6
DV = 512
FF = 5632
CONV = 4
BLOCK = 64
DOCS = 4
HK = 1536
HV = 3072
ROWS = 4
LENGTH = 1024


def draw_a_log(key, part):
    fraction = jax.random.uniform(key, (H,), jnp.float32)
    lowest = math.log(0.3 / LENGTH)
    highest = math.log(1.0 / 30.0)
    return lowest + fraction * (highest - lowest)


def levels(stream_key, extent, cuts, least, top_value):
    factor_of, own = 1.0, jax.random.fold_in(stream_key, 6)
    for dim, shards_of in cuts:
        heights = jnp.exp(jax.random.uniform(jax.random.fold_in(own, dim), (shards_of,), jnp.float32, least / len(cuts), top_value / len(cuts)))
        factor_of = factor_of * jnp.repeat(heights, extent[dim] // shards_of).reshape([-1 if axis == dim else 1 for axis in range(len(extent))])
    return factor_of


def profile(amount, total, reach, lean):
    weights = [(1 << 20) // math.isqrt(standing ** lean) + 1 for standing in range(2, amount + 1)]
    rest, holding = total - reach - (amount - 1), [1] * (amount - 1)
    while rest > 0:
        free = [i for i in range(amount - 1) if holding[i] < reach]
        pool, remaining = sum([weights[i] for i in free]), rest
        for i in free:
            extra = min(reach - holding[i], max(1, remaining * weights[i] // pool), rest)
            holding[i] = holding[i] + extra
            rest = rest - extra
    return np.array([reach] + holding)


def ragged_sizes(own_key, number_of, total, reach, skew):
    if number_of == 2:
        one = jax.random.randint(own_key, (), max(1, total - reach), min(reach, total - 1) + 1)
        return jnp.stack([one, total - one])
    lengths = jnp.asarray(profile(number_of, total, reach, skew), jnp.int32)
    pairs = (number_of - 1) // 2
    donor, receiver = lengths[1:1 + 2 * pairs:2], lengths[2:2 + 2 * pairs:2]
    room = jnp.minimum(donor - 1, reach - receiver)
    passed = jax.random.randint(jax.random.fold_in(own_key, 1), (pairs,), 0, 1 << 20) % (room + 1)
    lengths = lengths.at[1:1 + 2 * pairs:2].set(donor - passed).at[2:2 + 2 * pairs:2].set(receiver + passed)
    return lengths[jax.random.permutation(jax.random.fold_in(own_key, 2), number_of)]


def bell_draw(key, extent, scale, most, shards=(), dtype=jnp.bfloat16):
    drawn = scale * jax.random.normal(key, extent, jnp.float32)
    if shards:
        drawn = drawn * levels(key, extent, shards, -0.22, 0.18)
    return jnp.clip(drawn, -most, most).astype(dtype)


def setup_inputs(seed: int = 0) -> dict:
    key_of = jax.random.split(jax.random.key(seed), 21)
    return {
        "hidden_in": bell_draw(key_of[0], (ROWS, LENGTH, D), 1.0, 6.0, ((0, 4), (1, 8))),
        "segment_ids": jax.vmap(lambda own: jnp.searchsorted(jnp.cumsum(ragged_sizes(own, DOCS, LENGTH, LENGTH // 2, 0)), jnp.arange(LENGTH), side="right"))(jax.random.split(key_of[1], ROWS)).reshape((ROWS, LENGTH)).astype(jnp.int32),
        "grad_out": bell_draw(key_of[2], (ROWS, LENGTH, D), 1.0, 6.0, ((0, 4), (1, 8))),
        "attn_gain": jnp.clip(1.0 + 0.1 * jax.random.normal(key_of[3], (D,), jnp.float32), 0.5, 1.5),
        "w_query": bell_draw(key_of[4], (D, HK), D ** -0.5, 0.125, ((0, 32),), jnp.float32),
        "w_key": bell_draw(key_of[5], (D, HK), D ** -0.5, 0.125, ((0, 32),), jnp.float32),
        "w_value": bell_draw(key_of[6], (D, HV), D ** -0.5, 0.125, ((0, 32),), jnp.float32),
        "w_decay": bell_draw(key_of[7], (D, H), D ** -0.5, 0.125, ((0, 32),), jnp.float32),
        "w_beta": bell_draw(key_of[8], (D, H), D ** -0.5, 0.125, ((0, 32),), jnp.float32),
        "w_outgate": bell_draw(key_of[9], (D, HV), D ** -0.5, 0.125, ((0, 32),), jnp.float32),
        "a_log": draw_a_log(jax.random.fold_in(key_of[20], 71), 0),
        "conv_query": bell_draw(key_of[11], (CONV, HK), CONV ** -0.5, 3.0, (), jnp.float32),
        "conv_key": bell_draw(key_of[12], (CONV, HK), CONV ** -0.5, 3.0, (), jnp.float32),
        "conv_value": bell_draw(key_of[13], (CONV, HV), CONV ** -0.5, 3.0, (), jnp.float32),
        "out_gain": jnp.clip(1.0 + 0.1 * jax.random.normal(key_of[14], (DV,), jnp.float32), 0.5, 1.5),
        "w_output": bell_draw(key_of[15], (D, HV), HV ** -0.5, 0.109375, ((0, 32),), jnp.float32),
        "mlp_gain": jnp.clip(1.0 + 0.1 * jax.random.normal(key_of[16], (D,), jnp.float32), 0.5, 1.5),
        "w_gate": bell_draw(key_of[17], (D, FF), D ** -0.5, 0.125, ((0, 32),), jnp.float32),
        "w_up": bell_draw(key_of[18], (D, FF), D ** -0.5, 0.125, ((0, 32),), jnp.float32),
        "w_down": bell_draw(key_of[19], (D, FF), FF ** -0.5, 0.078125, ((0, 32),), jnp.float32),
    }


EPSILON = 1e-06
EXACT_PRECISION = lax.Precision.HIGHEST

@jax.custom_vjp
def low(v):
    return lax.optimization_barrier(v.astype(jnp.bfloat16)).astype(jnp.float32)

@jax.custom_vjp
def low_back(v):
    return v

def low_keep(v):
    return (low(v), None)

def low_pass(kept, grad):
    return (grad,)

def back_keep(v):
    return (v, None)

def back_low(kept, grad):
    return (low(grad),)
low.defvjp(low_keep, low_pass)
low_back.defvjp(back_keep, back_low)

def rms_scale(values):
    return values * lax.rsqrt(lax.optimization_barrier(jnp.mean(values * values, axis=-1, keepdims=True)) + EPSILON)

def unit_rows(values):
    return values * lax.rsqrt(lax.optimization_barrier(jnp.sum(values * values, axis=-1, keepdims=True)) + EPSILON)

def project(left, weight):
    return jnp.einsum('rtd,de->rte', left, weight, precision=EXACT_PRECISION)

def project_back(left, weight):
    return jnp.einsum('rte,de->rtd', left, weight, precision=EXACT_PRECISION)

def short_conv(before, segment, kernel):
    length = before.shape[1]
    padded = jnp.pad(before, ((0, 0), (CONV - 1, 0), (0, 0)))
    padded_ids = jnp.pad(segment, ((0, 0), (CONV - 1, 0)))
    mixed = jnp.zeros_like(before)
    for lag in range(CONV):
        offset = CONV - 1 - lag
        same = (segment == padded_ids[:, offset:offset + length]).astype(jnp.float32)
        mixed = mixed + kernel[lag] * padded[:, offset:offset + length] * same[:, :, None]
    return jax.nn.silu(mixed)

def recurrence(queries, key_vecs, value_vecs, beta_gate, alpha):
    rows, length, heads, key_size = queries.shape
    value_size = value_vecs.shape[3]
    blocks = length // BLOCK

    def to_blocks(values):
        return jnp.moveaxis(values.reshape((rows, blocks, BLOCK) + values.shape[2:]), 0, 2)

    def token_step(state, inputs):
        query_now, key_now, value_now, beta_now, alpha_now = inputs
        state = alpha_now[:, :, None, None] * state
        recalled = jnp.einsum('rhk,rhkv->rhv', key_now, state, precision=EXACT_PRECISION)
        state = state + beta_now[:, :, None, None] * key_now[:, :, :, None] * (value_now - recalled)[:, :, None, :]
        output = jnp.einsum('rhk,rhkv->rhv', query_now, state, precision=EXACT_PRECISION)
        return (state, output)

    def block_step(state, inputs):
        return lax.scan(token_step, state, inputs)
    start_state = jnp.zeros((rows, heads, key_size, value_size), jnp.float32)
    inputs = (to_blocks(queries), to_blocks(key_vecs), to_blocks(value_vecs), to_blocks(beta_gate), to_blocks(alpha))
    final, outputs = lax.scan(jax.checkpoint(block_step), start_state, inputs)
    return jnp.moveaxis(outputs, 2, 0).reshape(rows, length, heads, value_size)

def layer(inputs, segment, attn_gain, w_query, w_key, w_value, w_decay, w_beta, w_outgate, a_log, conv_query, conv_key, conv_value, out_gain, w_output, mlp_gain, w_gate, w_up, w_down):
    rows, length = (inputs.shape[0], inputs.shape[1])
    heads = a_log.shape[0]
    key_size = w_query.shape[1] // heads
    value_size = out_gain.shape[0]
    normed = low(rms_scale(inputs) * attn_gain)
    query_pre = low_back(low(project(normed, low(w_query))))
    key_pre = low_back(low(project(normed, low(w_key))))
    value_pre = low_back(low(project(normed, low(w_value))))
    decay_pre = low_back(project(normed, low(w_decay)))
    beta_pre = low_back(project(normed, low(w_beta)))
    gate_pre = low_back(project(normed, low(w_outgate)))
    query_act = short_conv(query_pre, segment, conv_query).reshape(rows, length, heads, key_size)
    key_act = short_conv(key_pre, segment, conv_key).reshape(rows, length, heads, key_size)
    value_vecs = short_conv(value_pre, segment, conv_value).reshape(rows, length, heads, value_size)
    queries = unit_rows(query_act) * key_size ** (-0.5)
    key_vecs = unit_rows(key_act)
    beta_gate = jax.nn.sigmoid(beta_pre)
    decay_log = -jnp.exp(a_log) * jax.nn.softplus(decay_pre)
    previous = jnp.pad(segment, ((0, 0), (1, 0)))[:, :length]
    keep = (segment == previous).astype(jnp.float32)[:, :, None]
    alpha = jnp.exp(decay_log) * keep
    mixed = recurrence(queries, key_vecs, value_vecs, beta_gate, alpha)
    gate = jax.nn.silu(gate_pre).reshape(rows, length, heads, value_size)
    gated = low((rms_scale(mixed) * out_gain * gate).reshape(rows, length, heads * value_size))
    attended = low_back(project_back(gated, low(w_output)))
    middle = inputs + attended
    normed_two = low(rms_scale(middle) * mlp_gain)
    gate_mlp = low_back(project(normed_two, low(w_gate)))
    up_mlp = low_back(project(normed_two, low(w_up)))
    hidden = low(jax.nn.silu(gate_mlp) * up_mlp)
    return middle + low_back(project_back(hidden, low(w_down)))

def reference(hidden_in, segment_ids, grad_out, attn_gain, w_query, w_key, w_value, w_decay, w_beta, w_outgate, a_log, conv_query, conv_key, conv_value, out_gain, w_output, mlp_gain, w_gate, w_up, w_down):
    inputs = hidden_in.astype(jnp.float32)

    def forward(values, gain_one, query_weight, key_weight, value_weight, decay_weight, beta_weight, outgate_weight, scales, conv_one, conv_two, conv_three, gain_out, output_weight, gain_two, gate_weight, up_weight, down_weight):
        return layer(values, segment_ids, gain_one, query_weight, key_weight, value_weight, decay_weight, beta_weight, outgate_weight, scales, conv_one, conv_two, conv_three, gain_out, output_weight, gain_two, gate_weight, up_weight, down_weight)
    result, pullback = jax.vjp(forward, inputs, attn_gain, w_query, w_key, w_value, w_decay, w_beta, w_outgate, a_log, conv_query, conv_key, conv_value, out_gain, w_output, mlp_gain, w_gate, w_up, w_down)
    grads = pullback(grad_out.astype(jnp.float32))
    return (result.astype(jnp.bfloat16), grads[0].astype(jnp.bfloat16), grads[1], grads[2], grads[3], grads[4], grads[5], grads[6], grads[7], grads[8], grads[9], grads[10], grads[11], grads[12], grads[13], grads[14], grads[15], grads[16], grads[17])
```

```python
from functools import partial

import jax
import jax.numpy as jnp
from jax import lax
from jax.experimental import pallas as pl
from jax.experimental.pallas import tpu as pltpu
from jax.sharding import Mesh
from jax.sharding import PartitionSpec as P

CONV = 4
EPSILON = 1e-06
EXACT = lax.Precision.HIGHEST
BF16 = jnp.bfloat16
F32 = jnp.float32
BY_MESH = pl.DeviceIdType.MESH
LANES = 128


def rms_scale(values):
    return values * lax.rsqrt(jnp.mean(values * values, axis=-1, keepdims=True) + EPSILON)


def swiglu(gate_values, up_values):
    return jax.nn.silu(gate_values) * up_values


def mm(left, right, over=(1, 0)):
    return lax.dot_general(
        left, right, (((over[0],), (over[1],)), ((), ())), preferred_element_type=F32
    )


def exact(left, right, over=(1, 0)):
    return lax.dot_general(
        left,
        right,
        (((over[0],), (over[1],)), ((), ())),
        precision=EXACT,
        preferred_element_type=F32,
    )


def place():
    return lax.axis_index("dp"), lax.axis_index("zq"), lax.axis_index("c")


def greet(peers):
    barrier = pltpu.get_barrier_semaphore()
    for peer in peers:
        pl.semaphore_signal(barrier, inc=1, device_id=peer, device_id_type=BY_MESH)
    pl.semaphore_wait(barrier, len(peers))


def remote(source, target, send, recv, peer):
    return pltpu.make_async_remote_copy(
        src_ref=source,
        dst_ref=target,
        send_sem=send,
        recv_sem=recv,
        device_id=peer,
        device_id_type=BY_MESH,
    )


def plane_offsets(rows):
    return [(k, flip) for k in range(rows) for flip in (0, 1) if (k, flip) != (0, 0)]


def plane_peer(offset, rows):
    d, z, c = place()
    k, flip = offset
    return (lax.rem(d + k, rows), z, 1 - c if flip else c)


def swap_kernel(rows, x_ref, o_ref, own, send, recv):
    d, z, c = place()
    me = d * 2 + c
    offsets = plane_offsets(rows)
    greet([plane_peer(offset, rows) for offset in offsets])
    copies = []
    for i, offset in enumerate(offsets):
        peer = plane_peer(offset, rows)
        copy = remote(
            x_ref.at[peer[0] * 2 + peer[2]], o_ref.at[me], send.at[i], recv.at[i], peer
        )
        copy.start()
        copies.append(copy)
    keep = pltpu.make_async_copy(x_ref.at[me], o_ref.at[me], own)
    keep.start()
    keep.wait()
    for copy in copies:
        copy.wait()


def spread_kernel(rows, x_ref, o_ref, own, send, recv, pair_send, pair_recv):
    d, z, c = place()
    me = d * 2 + c
    pair = (d, z, 1 - c)
    others = [(lax.rem(d + k, rows), z, c) for k in range(1, rows)]
    greet(others + [pair])
    copies = []
    for i, peer in enumerate(others):
        copy = remote(x_ref, o_ref.at[me], send.at[i], recv.at[i], peer)
        copy.start()
        copies.append(copy)
    hand = remote(x_ref, o_ref.at[me], pair_send.at[0], pair_recv.at[0], pair)
    hand.start()
    keep = pltpu.make_async_copy(x_ref, o_ref.at[me], own)
    keep.start()
    hands = [hand]
    for i, copy in enumerate(copies):
        copy.wait_recv()
        origin = lax.rem(d + rows - (i + 1), rows) * 2 + c
        hand = remote(
            o_ref.at[origin], o_ref.at[origin], pair_send.at[i + 1], pair_recv.at[i + 1], pair
        )
        hand.start()
        hands.append(hand)
    keep.wait()
    for copy in copies:
        copy.wait_send()
    for hand in hands:
        hand.wait()


def fold_kernel(
    rows, x_ref, o_ref, mine, theirs, load, pair_send, pair_recv, send, recv, own
):
    d, z, c = place()
    pair = (d, z, 1 - c)
    others = [(lax.rem(d + k, rows), z, c) for k in range(1, rows)]
    greet(others + [pair])
    order = [lax.rem(d + k, rows) for k in range(1, rows)] + [d]
    hands, loads = [], []
    for i, to in enumerate(order):
        hand = remote(
            x_ref.at[to * 2 + (1 - c)], theirs.at[i], pair_send.at[i], pair_recv.at[i], pair
        )
        hand.start()
        hands.append(hand)
        copy = pltpu.make_async_copy(x_ref.at[to * 2 + c], mine.at[i], load.at[i])
        copy.start()
        loads.append(copy)
    copies = []
    for i in range(rows):
        loads[i].wait()
        hands[i].wait_recv()
        mine[i] = (mine[i].astype(F32) + theirs[i].astype(F32)).astype(BF16)
        if i < rows - 1:
            copy = remote(mine.at[i], o_ref.at[d], send.at[i], recv.at[i], others[i])
        else:
            copy = pltpu.make_async_copy(mine.at[i], o_ref.at[d], own)
        copy.start()
        copies.append(copy)
    for hand in hands:
        hand.wait_send()
    for copy in copies:
        copy.wait()


def column_kernel(count, x_ref, o_ref, own, send, recv):
    d, z, c = place()
    others = [(d, lax.rem(z + k, count), c) for k in range(1, count)]
    greet(others)
    copies = []
    for i, peer in enumerate(others):
        copy = remote(x_ref, o_ref.at[z], send.at[i], recv.at[i], peer)
        copy.start()
        copies.append(copy)
    keep = pltpu.make_async_copy(x_ref, o_ref.at[z], own)
    keep.start()
    keep.wait()
    for copy in copies:
        copy.wait()


def neighbours(count):
    d, z, c = place()
    after = (d, lax.rem(z + c, count), 1 - c)
    before = (d, lax.rem(z + c - 1 + count, count), 1 - c)
    spot = z * 2 + c
    return spot, before, after


def greet_chain(count):
    spot, before, after = neighbours(count)
    barrier = pltpu.get_barrier_semaphore()

    @pl.when(spot > 0)
    def _():
        pl.semaphore_signal(barrier, inc=1, device_id=before, device_id_type=BY_MESH)

    @pl.when(spot < 2 * count - 1)
    def _():
        pl.semaphore_signal(barrier, inc=1, device_id=after, device_id_type=BY_MESH)

    pl.semaphore_wait(
        barrier,
        (spot > 0).astype(jnp.int32) + (spot < 2 * count - 1).astype(jnp.int32),
    )


def hop_kernel(count, forward, x_ref, o_ref, send, recv):
    spot, before, after = neighbours(count)
    greet_chain(count)
    if forward:
        gives, takes, to = spot < 2 * count - 1, spot > 0, after
    else:
        gives, takes, to = spot > 0, spot < 2 * count - 1, before
    copy = remote(x_ref, o_ref, send, recv, to)

    @pl.when(gives)
    def _():
        copy.start()

    @pl.when(takes)
    def _():
        copy.wait_recv()

    @pl.when(jnp.logical_not(takes))
    def _():
        o_ref[...] = jnp.zeros_like(o_ref)

    @pl.when(gives)
    def _():
        copy.wait_send()


def chain_kernel(
    count, heads, forward, high_ref, low_ref, add_ref, o_ref, land, stage, send, recv
):
    spot, before, after = neighbours(count)
    greet_chain(count)
    if forward:
        gives, takes, to = spot < 2 * count - 1, spot > 0, after
    else:
        gives, takes, to = spot > 0, spot < 2 * count - 1, before
    over = (1, 0) if forward else (0, 0)
    copies = [
        remote(stage.at[h], land.at[h], send.at[h], recv.at[h], to) for h in range(heads)
    ]
    for h in range(heads):

        @pl.when(jnp.logical_not(takes))
        def _():
            land[h] = jnp.zeros_like(land[h])

        @pl.when(takes)
        def _():
            copies[h].wait_recv()

        @pl.when(gives)
        def _():
            state = land[h]
            leaving = add_ref[h] + mm(high_ref[h], state, over) + mm(low_ref[h], state, over)
            stage[h] = leaving.astype(BF16)
            copies[h].start()

    for h in range(heads):

        @pl.when(gives)
        def _():
            copies[h].wait_send()

    o_ref[...] = land[...]


ANY = pl.BlockSpec(memory_space=pl.ANY)
IN_VMEM = pl.BlockSpec(memory_space=pltpu.VMEM)


def dma(*shape):
    return pltpu.SemaphoreType.DMA(shape)


def comm_call(body, out, scratch, ident, operands, spec=ANY, cost=30):
    return pl.pallas_call(
        body,
        out_shape=out,
        in_specs=[spec] * len(operands),
        out_specs=spec,
        scratch_shapes=scratch,
        compiler_params=pltpu.CompilerParams(collective_id=ident, has_side_effects=True),
        cost_estimate=pl.CostEstimate(
            flops=0, bytes_accessed=int(cost * 3.0e6), transcendentals=0
        ),
    )(*operands)


def swap(x, ident):
    rows = lax.axis_size("dp")
    links = 2 * rows - 1
    return comm_call(
        partial(swap_kernel, rows),
        jax.ShapeDtypeStruct(x.shape, x.dtype),
        [pltpu.SemaphoreType.DMA, dma(links), dma(links)],
        ident,
        (x,),
    )


def spread(x, ident):
    rows = lax.axis_size("dp")
    return comm_call(
        partial(spread_kernel, rows),
        jax.ShapeDtypeStruct((2 * rows,) + x.shape, x.dtype),
        [pltpu.SemaphoreType.DMA, dma(rows - 1), dma(rows - 1), dma(rows), dma(rows)],
        ident,
        (x,),
    )


def fold(x, ident):
    rows = lax.axis_size("dp")
    part = (rows,) + x.shape[1:]
    received = comm_call(
        partial(fold_kernel, rows),
        jax.ShapeDtypeStruct(part, x.dtype),
        [
            pltpu.VMEM(part, x.dtype),
            pltpu.VMEM(part, x.dtype),
            dma(rows),
            dma(rows),
            dma(rows),
            dma(rows - 1),
            dma(rows - 1),
            pltpu.SemaphoreType.DMA,
        ],
        ident,
        (x,),
    )
    return jnp.sum(received.astype(F32), axis=0)


def column(x, ident):
    count = lax.axis_size("zq")
    return comm_call(
        partial(column_kernel, count),
        jax.ShapeDtypeStruct((count,) + x.shape, x.dtype),
        [pltpu.SemaphoreType.DMA, dma(count - 1), dma(count - 1)],
        ident,
        (x,),
    )


def hop(x, forward, ident):
    count = lax.axis_size("zq")
    return comm_call(
        partial(hop_kernel, count, forward),
        jax.ShapeDtypeStruct(x.shape, x.dtype),
        [pltpu.SemaphoreType.DMA, pltpu.SemaphoreType.DMA],
        ident,
        (x,),
        IN_VMEM,
    )


def chain(high, low, add, forward, ident):
    count = lax.axis_size("zq")
    heads = add.shape[0]
    return comm_call(
        partial(chain_kernel, count, heads, forward),
        jax.ShapeDtypeStruct(add.shape, BF16),
        [
            pltpu.VMEM(add.shape, BF16),
            pltpu.VMEM(add.shape, BF16),
            dma(heads),
            dma(heads),
        ],
        ident,
        (high, low, add),
        IN_VMEM,
    )


def unit_lower_inverse(low):
    size = low.shape[0]
    row = lax.broadcasted_iota(jnp.int32, low.shape, 0)
    col = lax.broadcasted_iota(jnp.int32, low.shape, 1)

    def same(width):
        shift = width.bit_length() - 1
        return (row >> shift) == (col >> shift)

    eye = (row == col).astype(F32)
    width = 8
    near = jnp.where(same(width), low, 0.0)
    square = exact(near, near)
    inverse = eye - near
    inverse = inverse + exact(inverse, square)
    square = exact(square, square)
    inverse = inverse + exact(inverse, square)
    while width < size:
        cross = jnp.where(same(2 * width) & jnp.logical_not(same(width)), low, 0.0)
        inverse = inverse - exact(inverse, exact(cross, inverse))
        width *= 2
    return inverse


def unit_parts(values):
    scale = lax.rsqrt(jnp.sum(values * values, axis=-1, keepdims=True) + EPSILON)
    return values * scale, scale


def unit_back(unit, scale, grad):
    return scale * (grad - unit * jnp.sum(unit * grad, axis=-1, keepdims=True))


def strict_lower(size):
    row = lax.broadcasted_iota(jnp.int32, (size, size), 0)
    col = lax.broadcasted_iota(jnp.int32, (size, size), 1)
    return (row > col).astype(F32)


def chunk_forward_kernel(
    q_ref,
    k_ref,
    v_ref,
    beta_ref,
    decay_ref,
    start_ref,
    tail_ref,
    inverse_ref,
    scores_ref,
    own_ref,
    effect_ref,
    offset_ref,
    high_ref,
    low_ref,
):
    size, key_size = q_ref.shape
    beta, start, tail = beta_ref[0], start_ref[0], tail_ref[0]
    decay = decay_ref[0]
    query = unit_parts(q_ref[...])[0] * key_size ** (-0.5)
    key = unit_parts(k_ref[...])[0]
    inner = exact(key, key, (1, 1))
    inverse = unit_lower_inverse(beta * inner * (decay * strict_lower(size)))
    scores = exact(query, key, (1, 1)) * decay
    update = exact(inverse, beta * v_ref[...])
    reach = exact(inverse, (beta * start) * key)
    inverse_ref[0] = inverse
    scores_ref[0] = scores
    own_ref[...] = exact(scores, update)
    effect_ref[0] = start * query - exact(scores, reach)
    last = tail * key
    offset_ref[0] = exact(last, update, (0, 0))
    row = lax.broadcasted_iota(jnp.int32, (key_size, key_size), 0)
    col = lax.broadcasted_iota(jnp.int32, (key_size, key_size), 1)
    transfer = jnp.where(row == col, start[size - 1 :, :], 0.0) - exact(last, reach, (0, 0))
    high = transfer.astype(BF16)
    high_ref[0] = high
    low_ref[0] = (transfer - high.astype(F32)).astype(BF16)


def gate_forward_kernel(own_ref, effect_ref, state_ref, gate_ref, gain_ref, mixed_ref, gated_ref):
    mixed = own_ref[...] + exact(effect_ref[0], state_ref[0].astype(F32))
    mixed_ref[...] = mixed
    gate = gate_ref[...].astype(F32)
    gated_ref[...] = (
        rms_scale(mixed) * gain_ref[...] * (gate * jax.nn.sigmoid(gate))
    ).astype(BF16)


def gate_backward_kernel(
    mixed_ref, gate_ref, gain_ref, grad_ref, effect_ref, out_ref, gate_grad_ref, gain_grad_ref, add_ref
):
    mixed = mixed_ref[...]
    gate = gate_ref[...].astype(F32)
    grad = grad_ref[...].astype(F32)
    gain = gain_ref[...]
    scale = lax.rsqrt(jnp.mean(mixed * mixed, axis=-1, keepdims=True) + EPSILON)
    normed = mixed * scale
    sig = jax.nn.sigmoid(gate)
    act = gate * sig
    gain_grad_ref[0] = jnp.sum(grad * normed * act, axis=0, keepdims=True)
    gate_grad_ref[...] = (
        grad * normed * gain * (sig * (1.0 + gate * (1.0 - sig)))
    ).astype(BF16)
    inner = grad * gain * act
    mixed_grad = scale * (inner - normed * jnp.mean(inner * normed, axis=-1, keepdims=True))
    out_ref[...] = mixed_grad
    add_ref[0] = exact(effect_ref[0], mixed_grad, (0, 0))


def chunk_backward_kernel(
    q_ref,
    k_ref,
    v_ref,
    beta_ref,
    decay_ref,
    start_ref,
    tail_ref,
    inverse_ref,
    scores_ref,
    state_ref,
    mixed_ref,
    ending_ref,
    dq_ref,
    dk_ref,
    dv_ref,
    dbeta_ref,
    ddecay_ref,
    dstart_ref,
    dtail_ref,
):
    size, key_size = q_ref.shape
    beta, start, tail = beta_ref[0], start_ref[0], tail_ref[0]
    decay, inverse, scores = decay_ref[0], inverse_ref[0], scores_ref[0]
    state = state_ref[0].astype(F32)
    ending = ending_ref[0].astype(F32)
    mixed_grad = mixed_ref[...]
    unit_q, scale_q = unit_parts(q_ref[...])
    query = unit_q * key_size ** (-0.5)
    key, scale_k = unit_parts(k_ref[...])
    below = strict_lower(size)
    inner = exact(key, key, (1, 1))
    raw = exact(query, key, (1, 1))
    recalled = exact(key, state)
    miss = v_ref[...] - start * recalled
    update = exact(inverse, beta * miss)
    mixed_state = exact(mixed_grad, state, (1, 1))
    last = tail * key
    dupdate = exact(scores, mixed_grad, (0, 0)) + exact(last, ending)
    dscores = exact(mixed_grad, update, (1, 1))
    dlast = exact(update, ending, (1, 1))
    dright = exact(inverse, dupdate, (0, 0))
    dlower = -exact(dright, update, (1, 1)) * below
    dv_ref[...] = beta * dright
    dscaled = dscores * decay
    dquery = start * mixed_state + exact(dscaled, key)
    dinner = beta * dlower * decay
    dkey = (
        tail * dlast
        + exact(dscaled, query, (0, 0))
        - exact((beta * start) * dright, state, (1, 1))
        + exact(dinner, key)
        + exact(dinner, key, (0, 0))
    )
    right_recalled = jnp.sum(dright * recalled, axis=-1, keepdims=True)
    dbeta_ref[0] = jnp.sum(dright * miss, axis=-1, keepdims=True) + jnp.sum(
        dlower * inner * decay, axis=-1, keepdims=True
    )
    final = jnp.sum(jnp.sum(ending * state, axis=-1, keepdims=True), axis=0, keepdims=True)
    row = lax.broadcasted_iota(jnp.int32, (size, 1), 0)
    dstart_ref[0] = (
        jnp.sum(query * mixed_state, axis=-1, keepdims=True)
        - beta * right_recalled
        + jnp.where(row == size - 1, final, 0.0)
    )
    dtail_ref[0] = jnp.sum(key * dlast, axis=-1, keepdims=True)
    ddecay_ref[0] = dscores * raw + beta * dlower * inner
    dq_ref[...] = unit_back(unit_q, scale_q, dquery * key_size ** (-0.5))
    dk_ref[...] = unit_back(key, scale_k, dkey)


def by_head(*shape):
    return pl.BlockSpec((1,) + shape, lambda h: (h, 0, 0))


def by_columns(rows, width, offset=0):
    return pl.BlockSpec((rows, width), lambda h: (0, h + offset))


def head_call(body, heads, in_specs, out_specs, out_shape, operands, flops):
    return pl.pallas_call(
        body,
        grid=(heads,),
        in_specs=in_specs,
        out_specs=out_specs,
        out_shape=out_shape,
        cost_estimate=pl.CostEstimate(flops=flops, bytes_accessed=20_000_000, transcendentals=0),
    )(*operands)


def shaped(*shape, dtype=F32):
    return jax.ShapeDtypeStruct(shape, dtype)


def short_conv(seg_ext, pre_ext, conv_query, conv_key, conv_value):
    kernel = jnp.concatenate([conv_query, conv_key, conv_value], axis=1)
    margin = CONV - 1
    length = pre_ext.shape[0] - margin
    mixed = jnp.zeros((length, kernel.shape[1]), F32)
    for lag in range(CONV):
        offset = margin - lag
        same = (seg_ext[margin:] == seg_ext[offset : offset + length]).astype(F32)
        mixed = mixed + kernel[lag] * pre_ext[offset : offset + length] * same[:, None]
    return jax.nn.silu(mixed)


def decays(segment, before, decay_pre, beta_pre, a_log):
    length = segment.shape[0]
    beta = jax.nn.sigmoid(beta_pre)
    decay_log = -jnp.exp(a_log) * jax.nn.softplus(decay_pre)
    order = jnp.arange(length)
    lower = order[:, None] >= order[None, :]
    running = exact(lower.astype(F32), decay_log).T
    live = (segment[:, None] == segment[None, :]) & lower
    gap = running[:, :, None] - running[:, None, :]
    decay = jnp.where(live, jnp.exp(jnp.where(live, gap, 0.0)), 0.0)
    start = jnp.exp(running) * (segment == before).astype(F32)
    live_last = segment == segment[-1]
    last_gap = running[:, -1:] - running
    tail = jnp.where(live_last, jnp.exp(jnp.where(live_last, last_gap, 0.0)), 0.0)
    return beta.T[:, :, None], decay, start[:, :, None], tail[:, :, None]


def local(
    hidden_in,
    segment_ids,
    grad_out,
    attn_gain,
    w_query,
    w_key,
    w_value,
    w_decay,
    w_beta,
    w_outgate,
    a_log,
    conv_query,
    conv_key,
    conv_value,
    out_gain,
    w_output,
    mlp_gain,
    w_gate,
    w_up,
    w_down,
):
    rows, count = lax.axis_size("dp"), lax.axis_size("zq")
    group = 2 * rows
    inputs = hidden_in[0].astype(F32)
    segment = segment_ids[0]
    grad_low = grad_out[0]
    length, width = inputs.shape
    heads = a_log.shape[0]
    key_width, value_width = w_query.shape[1], w_value.shape[1]
    key_size, value_size = key_width // heads, out_gain.shape[0]
    mixer_width = 2 * key_width + value_width
    hidden_width = w_gate.shape[1]
    owned = w_query.shape[0]
    margin = CONV - 1
    spot = lax.axis_index("zq") * 2 + lax.axis_index("c")
    me = lax.axis_index("dp") * 2 + lax.axis_index("c")
    project_width = (mixer_width + value_width) // group
    ffn_width = hidden_width // group
    back_width = value_width // group

    def shuffled(values):
        return (
            values.reshape(-1, rows, count, 2 * owned).swapaxes(1, 2).reshape(-1, width)
        )

    def unshuffled(values):
        return (
            values.reshape(-1, count, rows, 2 * owned).swapaxes(1, 2).reshape(-1, width)
        )

    def cut(values):
        return values.astype(BF16).reshape(owned, group, -1).swapaxes(0, 1)

    def joined(values):
        return values.swapaxes(0, 1).reshape(values.shape[1], -1)

    small = jnp.concatenate([w_decay, w_beta], axis=1).astype(BF16)
    small = jnp.pad(small, ((0, 0), (0, LANES - 2 * heads)))
    mixer_cut = jnp.concatenate(
        [
            cut(jnp.concatenate([w_query, w_key, w_value, w_outgate], axis=1)),
            jnp.broadcast_to(small[None], (group, owned, LANES)),
        ],
        axis=2,
    )
    ffn_cut = jnp.concatenate([cut(w_output), cut(w_gate), cut(w_up), cut(w_down)], axis=2)
    mixer_own = swap(mixer_cut, 0).reshape(group * owned, -1)
    mixer_weights = lax.all_gather(mixer_own, "zq", axis=0, tiled=True)
    ffn_own = swap(ffn_cut, 1).reshape(group * owned, -1)
    ffn_weights = lax.all_gather(ffn_own, "zq", axis=0, tiled=True)
    project = mixer_weights[:, :project_width]
    small_weights = mixer_weights[:, project_width:]
    output_weights = ffn_weights[:, :back_width]
    gate_up = ffn_weights[:, back_width : back_width + 2 * ffn_width]
    down = ffn_weights[:, back_width + 2 * ffn_width :]

    normed, norm_pull = jax.vjp(rms_scale, inputs)
    normed_low = shuffled((normed * attn_gain).astype(BF16))
    normed_all = spread(normed_low, 2).reshape(-1, width)
    grad_all = spread(shuffled(grad_low), 2).reshape(-1, width)
    projected = mm(normed_all, project).astype(BF16)
    mixed_low = joined(swap(projected.reshape(group, length, project_width), 3))
    pre_low = mixed_low[:, :mixer_width]
    gate_pre = mixed_low[:, mixer_width:]
    small_pre = mm(normed_low, small_weights)
    decay_pre, beta_pre = small_pre[:, :heads], small_pre[:, heads : 2 * heads]

    rim = hop(pre_low[length - 16 :], True, 4)[16 - margin :]
    rim_ids = lax.ppermute(
        segment[-margin:],
        ("zq", "c"),
        [(i, i + 1) for i in range(2 * count - 1)],
    )
    seg_ext = jnp.concatenate([rim_ids, segment])
    pre_ext = jnp.concatenate([rim, pre_low], axis=0).astype(F32)
    active, conv_pull = jax.vjp(
        partial(short_conv, seg_ext), pre_ext, conv_query, conv_key, conv_value
    )
    (beta, decay, start, tail), decay_pull = jax.vjp(
        partial(decays, segment, seg_ext[margin - 1]), decay_pre, beta_pre, a_log
    )
    token_specs = [
        by_columns(length, key_size),
        by_columns(length, key_size, heads),
        by_columns(length, value_size, 2 * key_width // value_size),
        by_head(length, 1),
        by_head(length, length),
        by_head(length, 1),
        by_head(length, 1),
    ]
    token_args = (active, active, active, beta, decay, start, tail)
    values_spec = by_columns(length, value_size)
    state_spec = by_head(key_size, value_size)
    inverse, scores, own, effect, offset, high, low = head_call(
        chunk_forward_kernel,
        heads,
        token_specs,
        [
            by_head(length, length),
            by_head(length, length),
            values_spec,
            by_head(length, key_size),
            state_spec,
            by_head(key_size, key_size),
            by_head(key_size, key_size),
        ],
        [
            shaped(heads, length, length),
            shaped(heads, length, length),
            shaped(length, value_width),
            shaped(heads, length, key_size),
            shaped(heads, key_size, value_size),
            shaped(heads, key_size, key_size, dtype=BF16),
            shaped(heads, key_size, key_size, dtype=BF16),
        ],
        token_args,
        6_000_000_000,
    )
    state = chain(high, low, offset, True, 5)
    gain_spec = pl.BlockSpec((1, value_size), lambda h: (0, 0))
    gain_row = out_gain[None]
    mixed, gated = head_call(
        gate_forward_kernel,
        heads,
        [values_spec, by_head(length, key_size), state_spec, values_spec, gain_spec],
        [values_spec, values_spec],
        [shaped(length, value_width), shaped(length, value_width, dtype=BF16)],
        (own, effect, state, gate_pre, gain_row),
        1_000_000_000,
    )
    gated_cut = gated.reshape(length, group, back_width).swapaxes(0, 1)
    gated_all = swap(gated_cut, 6).reshape(-1, back_width)
    attended = fold(
        mm(gated_all, output_weights, (1, 1)).astype(BF16).reshape(group, length, width), 7
    )
    middle = inputs + unshuffled(attended)

    normed_two, norm_pull_two = jax.vjp(rms_scale, middle)
    normed_two_all = spread(shuffled((normed_two * mlp_gain).astype(BF16)), 2).reshape(-1, width)
    both = mm(normed_two_all, gate_up)
    hidden, swiglu_pull = jax.vjp(swiglu, both[:, :ffn_width], both[:, ffn_width:])
    hidden_low = hidden.astype(BF16)
    grad_gate, grad_up = swiglu_pull(mm(grad_all, down))
    both_grad_low = jnp.concatenate([grad_gate, grad_up], axis=1).astype(BF16)
    grad_normed_two = unshuffled(
        fold(mm(both_grad_low, gate_up, (1, 1)).astype(BF16).reshape(group, length, width), 7)
    )
    mlp_part = fold(mm(hidden_low, down, (1, 1)).astype(BF16).reshape(group, length, width), 7)
    result = (middle + unshuffled(mlp_part)).astype(BF16)
    gate_up_rows = mm(normed_two_all, both_grad_low, (0, 0)).astype(BF16)
    down_rows = mm(grad_all, hidden_low, (0, 0)).astype(BF16)
    grad_mlp_gain = jnp.sum(grad_normed_two * normed_two, axis=0)
    grad_middle = grad_low.astype(F32) + norm_pull_two(grad_normed_two * mlp_gain)[0]

    attended_grad_all = spread(shuffled(grad_middle.astype(BF16)), 2).reshape(-1, width)
    grad_gated_all = mm(attended_grad_all, output_weights).astype(BF16)
    grad_gated = joined(swap(grad_gated_all.reshape(group, length, back_width), 6))
    output_rows = mm(attended_grad_all, gated_all, (0, 0)).astype(BF16)
    ffn_rows = lax.psum_scatter(
        jnp.concatenate([output_rows, gate_up_rows, down_rows], axis=1),
        "zq",
        scatter_dimension=0,
        tiled=True,
    )
    mixed_grad, gate_pre_grad, gain_grad, state_add = head_call(
        gate_backward_kernel,
        heads,
        [values_spec, values_spec, gain_spec, values_spec, by_head(length, key_size)],
        [values_spec, values_spec, by_head(1, value_size), state_spec],
        [
            shaped(length, value_width),
            shaped(length, value_width, dtype=BF16),
            shaped(heads, 1, value_size),
            shaped(heads, key_size, value_size),
        ],
        (mixed, gate_pre, gain_row, grad_gated, effect),
        1_000_000_000,
    )
    grad_out_gain = jnp.sum(gain_grad, axis=(0, 1))
    ending = chain(high, low, state_add, False, 8)
    dq, dk, dv, dbeta, ddecay, dstart, dtail = head_call(
        chunk_backward_kernel,
        heads,
        token_specs
        + [
            by_head(length, length),
            by_head(length, length),
            state_spec,
            values_spec,
            state_spec,
        ],
        [
            values_spec if size == value_size else by_columns(length, size)
            for size in (key_size, key_size, value_size)
        ]
        + [by_head(length, 1), by_head(length, length), by_head(length, 1), by_head(length, 1)],
        [
            shaped(length, key_width),
            shaped(length, key_width),
            shaped(length, value_width),
            shaped(heads, length, 1),
            shaped(heads, length, length),
            shaped(heads, length, 1),
            shaped(heads, length, 1),
        ],
        token_args + (inverse, scores, state, mixed_grad, ending),
        12_000_000_000,
    )
    grad_decay, grad_beta, grad_alog = decay_pull((dbeta, ddecay, dstart, dtail))
    grad_ext, grad_conv_one, grad_conv_two, grad_conv_three = conv_pull(
        jnp.concatenate([dq, dk, dv], axis=1)
    )
    rim_grad = jnp.pad(grad_ext[:margin].astype(BF16), ((16 - margin, 0), (0, 0)))
    returned = hop(rim_grad, False, 9).astype(F32)[16 - margin :]
    grad_pre = grad_ext[margin:].at[length - margin :].add(returned)
    small_grad = jnp.concatenate([grad_decay, grad_beta], axis=1).astype(BF16)
    small_grad = jnp.pad(small_grad, ((0, 0), (0, LANES - 2 * heads)))
    wide_grad = jnp.concatenate([grad_pre.astype(BF16), gate_pre_grad], axis=1)
    grads_cut = jnp.concatenate(
        [
            wide_grad.reshape(length, group, project_width).swapaxes(0, 1),
            jnp.broadcast_to(small_grad[None], (group, length, LANES)),
        ],
        axis=2,
    )
    grads_all = swap(grads_cut, 10).reshape(group * length, -1)
    mixer_rows = lax.psum_scatter(
        mm(normed_all, grads_all, (0, 0)).astype(BF16),
        "zq",
        scatter_dimension=0,
        tiled=True,
    )
    combined = fold(
        mm(grads_all[:, :project_width], project, (1, 1))
        .astype(BF16)
        .reshape(group, length, width),
        7,
    )
    combined = unshuffled(combined + mm(small_grad, small_weights, (1, 1)))
    grad_attn_gain = jnp.sum(combined * normed, axis=0)
    grad_inputs = grad_middle + norm_pull(combined * attn_gain)[0]

    ffn_back = joined_rows(swap(ffn_rows.reshape(group, owned, -1), 1))
    output_grad = joined(ffn_back[:, :, :back_width])
    gate_grad = joined(ffn_back[:, :, back_width : back_width + ffn_width])
    up_grad = joined(ffn_back[:, :, back_width + ffn_width : back_width + 2 * ffn_width])
    down_grad = joined(ffn_back[:, :, back_width + 2 * ffn_width :])
    mixer_parts = mixer_rows.reshape(group, owned, -1)
    mixer_back = joined(joined_rows(swap(mixer_parts, 0))[:, :, :project_width])
    small_rows = lax.dynamic_index_in_dim(mixer_parts, me, 0, keepdims=False)
    small_rows = small_rows[:, project_width:].astype(F32)

    pieces = (
        grad_attn_gain,
        grad_alog,
        grad_conv_one,
        grad_conv_two,
        grad_conv_three,
        grad_out_gain,
        grad_mlp_gain,
    )
    flat = jnp.concatenate([piece.reshape(-1) for piece in pieces])
    lines = -(-flat.shape[0] // (8 * LANES)) * 8
    flat = jnp.pad(flat, (0, lines * LANES - flat.shape[0])).reshape(lines, LANES)
    flat = jnp.sum(spread(flat, 11), axis=0)
    flat = jnp.sum(column(flat, 12), axis=0).reshape(-1)
    summed, at = [], 0
    for piece in pieces:
        summed.append(flat[at : at + piece.size].reshape(piece.shape))
        at += piece.size

    return (
        result[None],
        grad_inputs.astype(BF16)[None],
        summed[0],
        mixer_back[:, :key_width],
        mixer_back[:, key_width : 2 * key_width],
        mixer_back[:, 2 * key_width : mixer_width],
        small_rows[:, :heads],
        small_rows[:, heads : 2 * heads],
        mixer_back[:, mixer_width:],
        summed[1],
        summed[2],
        summed[3],
        summed[4],
        summed[5],
        output_grad,
        summed[6],
        gate_grad,
        up_grad,
        down_grad,
    )


def joined_rows(values):
    return values.astype(F32)


def solution(mesh):
    rows, places = mesh.shape["dp"], mesh.shape["seq"]
    fine = Mesh(mesh.devices.reshape(rows, places // 2, 2), ("dp", "zq", "c"))
    tokens = P("dp", ("zq", "c"), None)
    owned = P(("dp", "zq", "c"), None)
    return jax.shard_map(
        local,
        mesh=fine,
        in_specs=(tokens, P("dp", ("zq", "c")), tokens, P())
        + (owned,) * 6
        + (P(),) * 5
        + (owned, P(), owned, owned, owned),
        out_specs=(tokens, tokens, P())
        + (owned,) * 6
        + (P(),) * 5
        + (owned, P(), owned, owned, owned),
        check_vma=False,
    )
```

```python
from functools import partial

import jax
import jax.numpy as jnp
from jax import lax
from jax.experimental import pallas as pl
from jax.experimental.pallas import tpu as pltpu
from jax.sharding import Mesh
from jax.sharding import PartitionSpec as P

CONV = 4
EPSILON = 1e-06
EXACT = lax.Precision.HIGHEST
BF16 = jnp.bfloat16
F32 = jnp.float32
BY_MESH = pl.DeviceIdType.MESH
LANES = 128
PIECES = 2
CHUNKS = 2
RIM = 16


def rms_scale(values):
    return values * lax.rsqrt(jnp.mean(values * values, axis=-1, keepdims=True) + EPSILON)


def swiglu(gate_values, up_values):
    return jax.nn.silu(gate_values) * up_values


def mm(left, right, over=(1, 0)):
    return lax.dot_general(
        left, right, (((over[0],), (over[1],)), ((), ())), preferred_element_type=F32
    )


def exact(left, right, over=(1, 0)):
    return lax.dot_general(
        left,
        right,
        (((over[0],), (over[1],)), ((), ())),
        precision=EXACT,
        preferred_element_type=F32,
    )


def place():
    return lax.axis_index("dp"), lax.axis_index("zq"), lax.axis_index("c")


def greet(peers):
    barrier = pltpu.get_barrier_semaphore()
    for peer in peers:
        pl.semaphore_signal(barrier, inc=1, device_id=peer, device_id_type=BY_MESH)
    pl.semaphore_wait(barrier, len(peers))


def remote(source, target, send, recv, peer):
    return pltpu.make_async_remote_copy(
        src_ref=source,
        dst_ref=target,
        send_sem=send,
        recv_sem=recv,
        device_id=peer,
        device_id_type=BY_MESH,
    )


def plane_offsets(rows):
    return [(k, flip) for k in range(rows) for flip in (0, 1) if (k, flip) != (0, 0)]


def plane_peer(offset, rows):
    d, z, c = place()
    k, flip = offset
    return (lax.rem(d + k, rows), z, 1 - c if flip else c)


def swap_kernel(rows, x_ref, o_ref, own, send, recv):
    d, z, c = place()
    me = d * 2 + c
    offsets = plane_offsets(rows)
    greet([plane_peer(offset, rows) for offset in offsets])
    copies = []
    for i, offset in enumerate(offsets):
        peer = plane_peer(offset, rows)
        copy = remote(
            x_ref.at[peer[0] * 2 + peer[2]], o_ref.at[me], send.at[i], recv.at[i], peer
        )
        copy.start()
        copies.append(copy)
    keep = pltpu.make_async_copy(x_ref.at[me], o_ref.at[me], own)
    keep.start()
    keep.wait()
    for copy in copies:
        copy.wait()


def spread_kernel(rows, x_ref, o_ref, own, send, recv, pair_send, pair_recv):
    d, z, c = place()
    me = d * 2 + c
    pair = (d, z, 1 - c)
    others = [(lax.rem(d + k, rows), z, c) for k in range(1, rows)]
    greet(others + [pair])
    copies = []
    for i, peer in enumerate(others):
        copy = remote(x_ref, o_ref.at[me], send.at[i], recv.at[i], peer)
        copy.start()
        copies.append(copy)
    hand = remote(x_ref, o_ref.at[me], pair_send.at[0], pair_recv.at[0], pair)
    hand.start()
    keep = pltpu.make_async_copy(x_ref, o_ref.at[me], own)
    keep.start()
    hands = [hand]
    for i, copy in enumerate(copies):
        copy.wait_recv()
        origin = lax.rem(d + rows - (i + 1), rows) * 2 + c
        hand = remote(
            o_ref.at[origin], o_ref.at[origin], pair_send.at[i + 1], pair_recv.at[i + 1], pair
        )
        hand.start()
        hands.append(hand)
    keep.wait()
    for copy in copies:
        copy.wait_send()
    for hand in hands:
        hand.wait()


def fold_kernel(
    rows, x_ref, o_ref, mine, theirs, load, pair_send, pair_recv, send, recv, own
):
    d, z, c = place()
    pair = (d, z, 1 - c)
    others = [(lax.rem(d + k, rows), z, c) for k in range(1, rows)]
    greet(others + [pair])
    order = [lax.rem(d + k, rows) for k in range(1, rows)] + [d]
    hands, loads = [], []
    for i, to in enumerate(order):
        hand = remote(
            x_ref.at[to * 2 + (1 - c)], theirs.at[i], pair_send.at[i], pair_recv.at[i], pair
        )
        hand.start()
        hands.append(hand)
        copy = pltpu.make_async_copy(x_ref.at[to * 2 + c], mine.at[i], load.at[i])
        copy.start()
        loads.append(copy)
    copies = []
    for i in range(rows):
        loads[i].wait()
        hands[i].wait_recv()
        mine[i] = (mine[i].astype(F32) + theirs[i].astype(F32)).astype(BF16)
        if i < rows - 1:
            copy = remote(mine.at[i], o_ref.at[d], send.at[i], recv.at[i], others[i])
        else:
            copy = pltpu.make_async_copy(mine.at[i], o_ref.at[d], own)
        copy.start()
        copies.append(copy)
    for hand in hands:
        hand.wait_send()
    for copy in copies:
        copy.wait()


def slab_pieces(widths, slab, t):
    at, end, base = t * slab, (t + 1) * slab, 0
    for source, width in enumerate(widths):
        low, high = max(at, base), min(end, base + width)
        if low < high:
            yield source, low - base, low - at, high - low
        base += width


def start_kernel(rows, count, hidden_ref, grad_ref, gain_ref, decay_ref, beta_ref, *refs):
    weight_refs = refs[:8]
    all_ref, *side_outs = refs[8:11]
    one_out_ref, two_out_ref, hidden_out_ref, one_ref, two_ref = refs[11:16]
    raws, cut_ref, sides = refs[16:24], refs[24], refs[25:27]
    (
        load,
        own,
        deal_send,
        deal_recv,
        side_send,
        side_recv,
        round_send,
        round_recv,
        pair_send,
        pair_recv,
        up_send,
        up_recv,
        down_send,
        down_recv,
    ) = refs[27:]
    loads = [
        pltpu.make_async_copy(weight, raw, load.at[i])
        for i, (weight, raw) in enumerate(zip(weight_refs, raws))
    ]
    for copy in loads:
        copy.start()
    d, z, c = place()
    me = d * 2 + c
    group = 2 * rows
    pair = (d, z, 1 - c)
    others = [(lax.rem(d + k, rows), z, c) for k in range(1, rows)]
    above = (d, lax.rem(z + 1, count), c)
    below = (d, lax.rem(z + count - 1, count), c)
    has_above, has_below = z < count - 1, z > 0
    offsets = plane_offsets(rows)
    barrier = pltpu.get_barrier_semaphore()
    for offset in offsets:
        pl.semaphore_signal(
            barrier, inc=1, device_id=plane_peer(offset, rows), device_id_type=BY_MESH
        )

    @pl.when(has_above)
    def _():
        pl.semaphore_signal(barrier, inc=1, device_id=above, device_id_type=BY_MESH)

    @pl.when(has_below)
    def _():
        pl.semaphore_signal(barrier, inc=1, device_id=below, device_id_type=BY_MESH)

    owned = raws[0].shape[0]
    wide = cut_ref.shape[2]
    heads = decay_ref.shape[1]
    back = raws[3].shape[1] // group
    slab = wide - LANES - back
    for copy in loads[:4]:
        copy.wait()
    widths = [raw.shape[1] for raw in raws[:3]]
    for t in range(group):
        for source, at, to, size in slab_pieces(widths, slab, t):
            cut_ref[t, :, to : to + size] = raws[source][:, at : at + size].astype(BF16)
        cut_ref[t, :, slab : slab + back] = raws[3][:, t * back : (t + 1) * back].astype(BF16)
        cut_ref[t, :, slab + back :] = jnp.concatenate(
            [decay_ref[...], beta_ref[...], jnp.zeros((owned, LANES - 2 * heads), F32)], axis=1
        ).astype(BF16)
    pl.semaphore_wait(
        barrier, len(offsets) + has_above.astype(jnp.int32) + has_below.astype(jnp.int32)
    )

    def deal(source, target, send, recv):
        copies = []
        for i, offset in enumerate(offsets):
            peer = plane_peer(offset, rows)
            copy = remote(
                source.at[peer[0] * 2 + peer[2]], target.at[me], send.at[i], recv.at[i], peer
            )
            copy.start()
            copies.append(copy)
        return copies

    def origin(offset):
        k, flip = offset
        return lax.rem(d + rows - k, rows) * 2 + (1 - c if flip else c)

    def passed(k, i, block, upward):
        at = z - k if upward else z + k
        at = lax.rem(at + count, count)
        send, recv = (up_send, up_recv) if upward else (down_send, down_recv)
        return remote(
            all_ref.at[at, block],
            all_ref.at[at, block],
            send.at[k, i],
            recv.at[k, i],
            above if upward else below,
        )

    def give(k, i, block):
        @pl.when(has_above & (z - k >= 0))
        def _():
            passed(k, i, block, True).start()

        @pl.when(has_below & (z + k <= count - 1))
        def _():
            passed(k, i, block, False).start()

    def take(k, i, block):
        @pl.when(z - k - 1 >= 0)
        def _():
            passed(k, i, block, True).wait_recv()

        @pl.when(z + k + 1 <= count - 1)
        def _():
            passed(k, i, block, False).wait_recv()

    def given(k, i, block):
        @pl.when(has_above & (z - k >= 0))
        def _():
            passed(k, i, block, True).wait_send()

        @pl.when(has_below & (z + k <= count - 1))
        def _():
            passed(k, i, block, False).wait_send()

    dealt = deal(cut_ref, all_ref.at[z], deal_send, deal_recv)
    keep = pltpu.make_async_copy(cut_ref.at[me], all_ref.at[z, me], own.at[0])
    keep.start()
    keep.wait()
    blocks = [me] + [origin(offset) for offset in offsets]
    give(0, 0, me)
    run = 2 * owned
    width = hidden_ref.shape[1]

    def moved(values):
        return jnp.concatenate(
            [
                values[:, (b * count + a) * run : (b * count + a + 1) * run]
                for a in range(count)
                for b in range(rows)
            ],
            axis=1,
        )

    hidden = moved(hidden_ref[...])
    hidden_out_ref[...] = hidden
    one_ref[...] = (rms_scale(hidden.astype(F32)) * moved(gain_ref[...])).astype(BF16)
    two_ref[...] = moved(grad_ref[...])
    rounds = []
    for j, (source, target) in enumerate(((one_ref, one_out_ref), (two_ref, two_out_ref))):
        copies = []
        for i, peer in enumerate(others):
            copies.append(
                remote(source, target.at[me], round_send.at[j, i], round_recv.at[j, i], peer)
            )
        copies.append(
            remote(source, target.at[me], pair_send.at[j, 0], pair_recv.at[j, 0], pair)
        )
        rounds.append(copies)
    for i, copy in enumerate(dealt):
        copy.wait_recv()
        give(0, i + 1, blocks[i + 1])
    keeps = [
        pltpu.make_async_copy(one_ref, one_out_ref.at[me], own.at[1]),
        pltpu.make_async_copy(two_ref, two_out_ref.at[me], own.at[2]),
    ]
    for copy in rounds[0] + keeps:
        copy.start()
    for copy in loads[4:]:
        copy.wait()
    deals = []
    for j, (laid, side, side_out) in enumerate(zip((raws[4:6], raws[6:]), sides, side_outs)):
        for t in range(group):
            at = 0
            for raw in laid:
                size = raw.shape[1] // group
                side[t, :, at : at + size] = raw[:, t * size : (t + 1) * size].astype(BF16)
                at += size
        deals += deal(side, side_out, side_send.at[j], side_recv.at[j])
        keep = pltpu.make_async_copy(side.at[me], side_out.at[me], own.at[3 + j])
        keep.start()
        keeps.append(keep)
    for copy in rounds[1]:
        copy.start()
    hands = []
    for k in range(count - 1):
        for i, block in enumerate(blocks):
            take(k, i, block)
            if k < count - 2:
                give(k + 1, i, block)
        if k < 2:
            target = (one_out_ref, two_out_ref)[k]
            for i, copy in enumerate(rounds[k][:-1]):
                copy.wait_recv()
                at = lax.rem(d + rows - (i + 1), rows) * 2 + c
                hand = remote(
                    target.at[at], target.at[at], pair_send.at[k, i + 1], pair_recv.at[k, i + 1], pair
                )
                hand.start()
                hands.append(hand)
    for copy in keeps:
        copy.wait()
    for copy in dealt:
        copy.wait_send()
    for copies in rounds:
        for copy in copies[:-1]:
            copy.wait_send()
        copies[-1].wait()
    for copy in hands + deals:
        copy.wait()
    for k in range(count - 1):
        for i, block in enumerate(blocks):
            given(k, i, block)


def turn_kernel(rows, backward, x_ref, gain_ref, base_ref, *refs):
    if backward:
        out_ref, all_ref, sums_ref = refs[1:4]
        gain_grad_ref, middle_ref = sums_ref, refs[0]
        scratch = refs[4:]
    else:
        out_ref, all_ref = refs[:2]
        scratch = refs[2:]
    (
        mine,
        theirs,
        land,
        low,
        load,
        fold_pair_send,
        fold_pair_recv,
        fold_send,
        fold_recv,
        own,
        send,
        recv,
        pair_send,
        pair_recv,
    ) = scratch
    d, z, c = place()
    me = d * 2 + c
    pair = (d, z, 1 - c)
    others = [(lax.rem(d + k, rows), z, c) for k in range(1, rows)]
    greet(others + [pair])
    order = [lax.rem(d + k, rows) for k in range(1, rows)] + [d]
    step = x_ref.shape[1] // CHUNKS
    parts = [pl.ds(j * step, step) for j in range(CHUNKS)]
    hands, loads = {}, {}
    for j, part in enumerate(parts):
        for i, to in enumerate(order):
            hands[j, i] = remote(
                x_ref.at[to * 2 + (1 - c), part],
                theirs.at[i, part],
                fold_pair_send.at[j, i],
                fold_pair_recv.at[j, i],
                pair,
            )
            hands[j, i].start()
            loads[j, i] = pltpu.make_async_copy(
                x_ref.at[to * 2 + c, part], mine.at[i, part], load.at[j, i]
            )
            loads[j, i].start()
    folds = {}
    for j, part in enumerate(parts):
        for i in range(rows):
            loads[j, i].wait()
            hands[j, i].wait_recv()
            if i < rows - 1:
                mine[i, part] = (mine[i, part].astype(F32) + theirs[i, part].astype(F32)).astype(
                    BF16
                )
                folds[j, i] = remote(
                    mine.at[i, part],
                    land.at[i, part],
                    fold_send.at[j, i],
                    fold_recv.at[j, i],
                    others[i],
                )
                folds[j, i].start()
    gain = gain_ref[...]
    sends, keeps = {}, []
    if backward:
        sums_ref[...] = jnp.zeros_like(sums_ref)
    for j, part in enumerate(parts):
        total = mine[rows - 1, part].astype(F32) + theirs[rows - 1, part].astype(F32)
        for i in range(rows - 1):
            folds[j, i].wait_recv()
            total = total + land[i, part].astype(F32)
        if backward:
            middle = middle_ref[part, :]
            scale = lax.rsqrt(jnp.mean(middle * middle, axis=-1, keepdims=True) + EPSILON)
            normed = middle * scale
            sums_ref[...] += jnp.sum(total * normed, axis=0, keepdims=True)
            inner = total * gain
            result = base_ref[part, :].astype(F32) + scale * (
                inner - normed * jnp.mean(inner * normed, axis=-1, keepdims=True)
            )
            out_ref[part, :] = result
            low[part, :] = result.astype(BF16)
        else:
            result = base_ref[part, :].astype(F32) + total
            out_ref[part, :] = result
            low[part, :] = (rms_scale(result) * gain).astype(BF16)
        for i, peer in enumerate(others + [pair]):
            at = (send.at[j, i], recv.at[j, i])
            if i == rows - 1:
                at = (pair_send.at[j, rows - 1], pair_recv.at[j, rows - 1])
            sends[j, i] = remote(low.at[part], all_ref.at[me, part], *at, peer)
            sends[j, i].start()
        keep = pltpu.make_async_copy(low.at[part], all_ref.at[me, part], own.at[j])
        keep.start()
        keeps.append(keep)
    for j, part in enumerate(parts):
        for i in range(rows - 1):
            sends[j, i].wait_recv()
            at = lax.rem(d + rows - (i + 1), rows) * 2 + c
            hand = remote(
                all_ref.at[at, part],
                all_ref.at[at, part],
                pair_send.at[j, i],
                pair_recv.at[j, i],
                pair,
            )
            hand.start()
            hands[j, rows + i] = hand
    for keep in keeps:
        keep.wait()
    for (j, i), hand in hands.items():
        hand.wait_send()
        if i >= rows:
            hand.wait_recv()
    for copy in folds.values():
        copy.wait_send()
    for (j, i), copy in sends.items():
        copy.wait_send()
        if i == rows - 1:
            copy.wait_recv()


def greet_plane_and_line(rows, count):
    d, z, c = place()
    spot, before, after = neighbours(count)
    offsets = plane_offsets(rows)
    lower, upper = (c == 0) & (z > 0), (c == 1) & (z < count - 1)
    barrier = pltpu.get_barrier_semaphore()
    for offset in offsets:
        pl.semaphore_signal(
            barrier, inc=1, device_id=plane_peer(offset, rows), device_id_type=BY_MESH
        )

    @pl.when(lower)
    def _():
        pl.semaphore_signal(barrier, inc=1, device_id=before, device_id_type=BY_MESH)

    @pl.when(upper)
    def _():
        pl.semaphore_signal(barrier, inc=1, device_id=after, device_id_type=BY_MESH)

    pl.semaphore_wait(
        barrier, len(offsets) + lower.astype(jnp.int32) + upper.astype(jnp.int32)
    )


def swap_on_kernel(rows, count, x_ref, o_ref, rim_ref, land, own, send, recv, rim_send, rim_recv):
    d, z, c = place()
    me = d * 2 + c
    spot, before, after = neighbours(count)
    greet_plane_and_line(rows, count)
    copies = []
    for i, offset in enumerate(plane_offsets(rows)):
        peer = plane_peer(offset, rows)
        copy = remote(
            x_ref.at[peer[0] * 2 + peer[2]], o_ref.at[me], send.at[i], recv.at[i], peer
        )
        copy.start()
        copies.append(copy)
    keep = pltpu.make_async_copy(x_ref.at[me], o_ref.at[me], own)
    keep.start()
    keep.wait()
    for copy in copies:
        copy.wait_recv()
    size = x_ref.shape[1]
    rim = remote(o_ref.at[:, pl.ds(size - RIM, RIM)], land, rim_send, rim_recv, after)
    gives, takes = spot < 2 * count - 1, spot > 0

    @pl.when(gives)
    def _():
        rim.start()

    @pl.when(takes)
    def _():
        rim.wait_recv()

    @pl.when(jnp.logical_not(takes))
    def _():
        land[...] = jnp.zeros_like(land)

    rim_ref[...] = land[...]
    for copy in copies:
        copy.wait_send()

    @pl.when(gives)
    def _():
        rim.wait_send()


def swap_back_kernel(
    rows,
    count,
    x_ref,
    tail_ref,
    rim_ref,
    small_ref,
    o_ref,
    land,
    fixed,
    own,
    send,
    recv,
    rim_send,
    rim_recv,
):
    d, z, c = place()
    me = d * 2 + c
    spot, before, after = neighbours(count)
    greet_plane_and_line(rows, count)
    size, part = x_ref.shape[1:]
    wide = o_ref.shape[2]
    rim = remote(rim_ref, land, rim_send, rim_recv, before)
    gives, takes = spot > 0, spot < 2 * count - 1

    @pl.when(gives)
    def _():
        rim.start()

    body, end = pl.ds(0, size - RIM), pl.ds(size - RIM, RIM)
    left, right = pl.ds(0, part), pl.ds(part, wide - part)
    copies = []
    for i, offset in enumerate(plane_offsets(rows)):
        peer = plane_peer(offset, rows)
        to = peer[0] * 2 + peer[2]
        copies.append(
            (
                remote(
                    x_ref.at[to, body], o_ref.at[me, body, left], send.at[0, i], recv.at[0, i], peer
                ),
                remote(small_ref, o_ref.at[me, :, right], send.at[1, i], recv.at[1, i], peer),
                remote(fixed.at[to], o_ref.at[me, end, left], send.at[2, i], recv.at[2, i], peer),
            )
        )
        copies[-1][0].start()
        copies[-1][1].start()
    keeps = [
        pltpu.make_async_copy(x_ref.at[me, body], o_ref.at[me, body, left], own.at[0]),
        pltpu.make_async_copy(small_ref, o_ref.at[me, :, right], own.at[1]),
        pltpu.make_async_copy(fixed.at[me], o_ref.at[me, end, left], own.at[2]),
    ]
    keeps[0].start()
    keeps[1].start()

    @pl.when(takes)
    def _():
        rim.wait_recv()

    @pl.when(jnp.logical_not(takes))
    def _():
        land[...] = jnp.zeros_like(land)

    fixed[...] = (tail_ref[...] + land[...].astype(F32)).astype(BF16)
    keeps[2].start()
    for group in copies:
        group[2].start()
    for keep in keeps:
        keep.wait()
    for group in copies:
        for copy in group:
            copy.wait()

    @pl.when(gives)
    def _():
        rim.wait_send()


def column_kernel(count, x_ref, o_ref, own, send, recv):
    d, z, c = place()
    others = [(d, lax.rem(z + k, count), c) for k in range(1, count)]
    greet(others)
    copies = []
    for i, peer in enumerate(others):
        copy = remote(x_ref, o_ref.at[z], send.at[i], recv.at[i], peer)
        copy.start()
        copies.append(copy)
    keep = pltpu.make_async_copy(x_ref, o_ref.at[z], own)
    keep.start()
    keep.wait()
    for copy in copies:
        copy.wait()


def neighbours(count):
    d, z, c = place()
    after = (d, lax.rem(z + c, count), 1 - c)
    before = (d, lax.rem(z + c - 1 + count, count), 1 - c)
    spot = z * 2 + c
    return spot, before, after


def greet_chain(count):
    spot, before, after = neighbours(count)
    barrier = pltpu.get_barrier_semaphore()

    @pl.when(spot > 0)
    def _():
        pl.semaphore_signal(barrier, inc=1, device_id=before, device_id_type=BY_MESH)

    @pl.when(spot < 2 * count - 1)
    def _():
        pl.semaphore_signal(barrier, inc=1, device_id=after, device_id_type=BY_MESH)

    pl.semaphore_wait(
        barrier,
        (spot > 0).astype(jnp.int32) + (spot < 2 * count - 1).astype(jnp.int32),
    )


def hop_kernel(count, forward, x_ref, o_ref, send, recv):
    spot, before, after = neighbours(count)
    greet_chain(count)
    if forward:
        gives, takes, to = spot < 2 * count - 1, spot > 0, after
    else:
        gives, takes, to = spot > 0, spot < 2 * count - 1, before
    copy = remote(x_ref, o_ref, send, recv, to)

    @pl.when(gives)
    def _():
        copy.start()

    @pl.when(takes)
    def _():
        copy.wait_recv()

    @pl.when(jnp.logical_not(takes))
    def _():
        o_ref[...] = jnp.zeros_like(o_ref)

    @pl.when(gives)
    def _():
        copy.wait_send()


def chain_kernel(
    count,
    rows,
    heads,
    sides,
    forward,
    high_ref,
    low_ref,
    add_ref,
    *refs,
):
    side_refs, (o_ref, *side_out_refs) = refs[:sides], refs[sides : 2 * sides + 1]
    land, stage, send, recv, own, side_send, side_recv = refs[2 * sides + 1 :]
    d, z, c = place()
    me = d * 2 + c
    spot, before, after = neighbours(count)
    offsets = plane_offsets(rows)
    barrier = pltpu.get_barrier_semaphore()
    for offset in offsets:
        pl.semaphore_signal(
            barrier, inc=1, device_id=plane_peer(offset, rows), device_id_type=BY_MESH
        )

    @pl.when((c == 0) & (z > 0))
    def _():
        pl.semaphore_signal(barrier, inc=1, device_id=before, device_id_type=BY_MESH)

    @pl.when((c == 1) & (z < count - 1))
    def _():
        pl.semaphore_signal(barrier, inc=1, device_id=after, device_id_type=BY_MESH)

    pl.semaphore_wait(
        barrier,
        len(offsets)
        + ((c == 0) & (z > 0)).astype(jnp.int32)
        + ((c == 1) & (z < count - 1)).astype(jnp.int32),
    )
    waits = []
    for j in range(sides):
        for i, offset in enumerate(offsets):
            peer = plane_peer(offset, rows)
            waits.append(
                remote(
                    side_refs[j].at[peer[0] * 2 + peer[2]],
                    side_out_refs[j].at[me],
                    side_send.at[j, i],
                    side_recv.at[j, i],
                    peer,
                )
            )
        waits.append(
            pltpu.make_async_copy(side_refs[j].at[me], side_out_refs[j].at[me], own.at[j])
        )
    for copy in waits:
        copy.start()
    if forward:
        gives, takes, to = spot < 2 * count - 1, spot > 0, after
    else:
        gives, takes, to = spot > 0, spot < 2 * count - 1, before
    part = o_ref.shape[2] // PIECES
    copies = [
        remote(stage.at[i], land.at[i], send.at[i], recv.at[i], to)
        for i in range(heads * PIECES)
    ]
    for h in range(heads):
        for j in range(PIECES):
            i = h * PIECES + j
            columns = slice(j * part, (j + 1) * part)

            @pl.when(jnp.logical_not(takes))
            def _():
                land[i] = jnp.zeros_like(land[i])

            @pl.when(takes)
            def _():
                copies[i].wait_recv()

            @pl.when(gives)
            def _():
                state = land[i]
                leaving = add_ref[h, :, columns] + mm(high_ref[h], state) + mm(low_ref[h], state)
                stage[i] = leaving.astype(BF16)
                copies[i].start()

    for copy in copies:

        @pl.when(gives)
        def _():
            copy.wait_send()

    for h in range(heads):
        for j in range(PIECES):
            o_ref[h, :, j * part : (j + 1) * part] = land[h * PIECES + j]
    for copy in waits:
        copy.wait()


ANY = pl.BlockSpec(memory_space=pl.ANY)
IN_VMEM = pl.BlockSpec(memory_space=pltpu.VMEM)
IN_HBM = pl.BlockSpec(memory_space=pltpu.HBM)


def dma(*shape):
    return pltpu.SemaphoreType.DMA(shape)


def comm_call(body, out, scratch, ident, operands, spec=ANY, cost=30):
    return pl.pallas_call(
        body,
        out_shape=out,
        in_specs=[spec] * len(operands),
        out_specs=spec,
        scratch_shapes=scratch,
        compiler_params=pltpu.CompilerParams(collective_id=ident, has_side_effects=True),
        cost_estimate=pl.CostEstimate(
            flops=0, bytes_accessed=int(cost * 3.0e6), transcendentals=0
        ),
    )(*operands)


def swap(x, ident):
    rows = lax.axis_size("dp")
    links = 2 * rows - 1
    return comm_call(
        partial(swap_kernel, rows),
        jax.ShapeDtypeStruct(x.shape, x.dtype),
        [pltpu.SemaphoreType.DMA, dma(links), dma(links)],
        ident,
        (x,),
    )


def spread(x, ident):
    rows = lax.axis_size("dp")
    return comm_call(
        partial(spread_kernel, rows),
        jax.ShapeDtypeStruct((2 * rows,) + x.shape, x.dtype),
        [pltpu.SemaphoreType.DMA, dma(rows - 1), dma(rows - 1), dma(rows), dma(rows)],
        ident,
        (x,),
    )


def fold(x, ident):
    rows = lax.axis_size("dp")
    part = (rows,) + x.shape[1:]
    received = comm_call(
        partial(fold_kernel, rows),
        jax.ShapeDtypeStruct(part, x.dtype),
        [
            pltpu.VMEM(part, x.dtype),
            pltpu.VMEM(part, x.dtype),
            dma(rows),
            dma(rows),
            dma(rows),
            dma(rows - 1),
            dma(rows - 1),
            pltpu.SemaphoreType.DMA,
        ],
        ident,
        (x,),
    )
    return jnp.sum(received.astype(F32), axis=0)


def turn(x, gain, base, middle, ident):
    rows = lax.axis_size("dp")
    group, length, width = x.shape
    backward = middle is not None
    part = (rows, length, width)
    return pl.pallas_call(
        partial(turn_kernel, rows, backward),
        out_shape=[
            jax.ShapeDtypeStruct((length, width), F32),
            jax.ShapeDtypeStruct((group, length, width), BF16),
        ]
        + ([jax.ShapeDtypeStruct((1, width), F32)] if backward else []),
        in_specs=[ANY, IN_VMEM, IN_VMEM] + ([IN_VMEM] if backward else []),
        out_specs=[IN_VMEM, ANY] + ([IN_VMEM] if backward else []),
        scratch_shapes=[
            pltpu.VMEM(part, BF16),
            pltpu.VMEM(part, BF16),
            pltpu.VMEM((rows - 1, length, width), BF16),
            pltpu.VMEM((length, width), BF16),
        ]
        + [dma(CHUNKS, rows)] * 3
        + [dma(CHUNKS, rows - 1)] * 2
        + [dma(CHUNKS)]
        + [dma(CHUNKS, rows - 1)] * 2
        + [dma(CHUNKS, rows)] * 2,
        compiler_params=pltpu.CompilerParams(collective_id=ident, has_side_effects=True),
        cost_estimate=pl.CostEstimate(
            flops=0, bytes_accessed=150_000_000, transcendentals=0
        ),
    )(x, gain, base, *([middle] if backward else []))


def swap_on(x, ident):
    rows, count = lax.axis_size("dp"), lax.axis_size("zq")
    group, length, part = x.shape
    links = 2 * rows - 1
    return pl.pallas_call(
        partial(swap_on_kernel, rows, count),
        out_shape=[
            jax.ShapeDtypeStruct(x.shape, x.dtype),
            jax.ShapeDtypeStruct((group, RIM, part), x.dtype),
        ],
        in_specs=[ANY],
        out_specs=[ANY, IN_VMEM],
        scratch_shapes=[
            pltpu.VMEM((group, RIM, part), x.dtype),
            pltpu.SemaphoreType.DMA,
            dma(links),
            dma(links),
            pltpu.SemaphoreType.DMA,
            pltpu.SemaphoreType.DMA,
        ],
        compiler_params=pltpu.CompilerParams(collective_id=ident, has_side_effects=True),
        cost_estimate=pl.CostEstimate(flops=0, bytes_accessed=90_000_000, transcendentals=0),
    )(x)


def swap_back(x, tail, rim, small, ident):
    rows, count = lax.axis_size("dp"), lax.axis_size("zq")
    group, length, part = x.shape
    links = 2 * rows - 1
    return pl.pallas_call(
        partial(swap_back_kernel, rows, count),
        out_shape=jax.ShapeDtypeStruct((group, length, part + small.shape[1]), x.dtype),
        in_specs=[ANY, IN_VMEM, ANY, ANY],
        out_specs=ANY,
        scratch_shapes=[
            pltpu.VMEM((group, RIM, part), x.dtype),
            pltpu.VMEM((group, RIM, part), x.dtype),
            dma(3),
            dma(3, links),
            dma(3, links),
            pltpu.SemaphoreType.DMA,
            pltpu.SemaphoreType.DMA,
        ],
        compiler_params=pltpu.CompilerParams(collective_id=ident, has_side_effects=True),
        cost_estimate=pl.CostEstimate(flops=0, bytes_accessed=90_000_000, transcendentals=0),
    )(x, tail, rim, small)


def begin(hidden, grad, gain, decay, beta, weights, ident):
    rows, count = lax.axis_size("dp"), lax.axis_size("zq")
    group, links = 2 * rows, 2 * rows - 1
    owned = decay.shape[0]
    parts = [weight.shape[1] // group for weight in weights]
    wide = sum(parts[:4]) + LANES
    cut = (group, owned, wide)
    side_shapes = [(group, owned, sum(parts[4:6])), (group, owned, sum(parts[6:]))]
    assert count > 2
    tokens = jax.ShapeDtypeStruct(hidden.shape, BF16)
    everyone = jax.ShapeDtypeStruct((group,) + hidden.shape, BF16)
    return pl.pallas_call(
        partial(start_kernel, rows, count),
        out_shape=[jax.ShapeDtypeStruct((count,) + cut, BF16)]
        + [jax.ShapeDtypeStruct(shape, BF16) for shape in side_shapes]
        + [everyone] * 2
        + [tokens] * 3,
        in_specs=[IN_VMEM] * 5 + [IN_HBM] * 8,
        out_specs=[ANY] * 5 + [IN_VMEM] * 3,
        scratch_shapes=[pltpu.VMEM(weight.shape, F32) for weight in weights]
        + [pltpu.VMEM(cut, BF16)]
        + [pltpu.VMEM(shape, BF16) for shape in side_shapes]
        + [
            dma(8),
            dma(5),
            dma(links),
            dma(links),
            dma(2, links),
            dma(2, links),
            dma(2, rows - 1),
            dma(2, rows - 1),
            dma(2, rows),
            dma(2, rows),
        ]
        + [dma(count - 1, group)] * 4,
        compiler_params=pltpu.CompilerParams(
            collective_id=ident, has_side_effects=True, vmem_limit_bytes=40 << 20
        ),
        cost_estimate=pl.CostEstimate(
            flops=0, bytes_accessed=300_000_000, transcendentals=0
        ),
    )(hidden, grad, gain, decay, beta, *weights)


def column(x, ident):
    count = lax.axis_size("zq")
    return comm_call(
        partial(column_kernel, count),
        jax.ShapeDtypeStruct((count,) + x.shape, x.dtype),
        [pltpu.SemaphoreType.DMA, dma(count - 1), dma(count - 1)],
        ident,
        (x,),
    )


def hop(x, forward, ident):
    count = lax.axis_size("zq")
    return comm_call(
        partial(hop_kernel, count, forward),
        jax.ShapeDtypeStruct(x.shape, x.dtype),
        [pltpu.SemaphoreType.DMA, pltpu.SemaphoreType.DMA],
        ident,
        (x,),
        IN_VMEM,
    )


def chain(high, low, add, sides, forward, ident):
    rows, count = lax.axis_size("dp"), lax.axis_size("zq")
    heads, key_size, value_size = add.shape
    links = 2 * rows - 1
    pieces = (heads * PIECES, key_size, value_size // PIECES)
    return pl.pallas_call(
        partial(chain_kernel, count, rows, heads, len(sides), forward),
        out_shape=[jax.ShapeDtypeStruct(add.shape, BF16)]
        + [jax.ShapeDtypeStruct(side.shape, side.dtype) for side in sides],
        in_specs=[IN_VMEM] * 3 + [ANY] * len(sides),
        out_specs=[IN_VMEM] + [ANY] * len(sides),
        scratch_shapes=[
            pltpu.VMEM(pieces, BF16),
            pltpu.VMEM(pieces, BF16),
            dma(heads * PIECES),
            dma(heads * PIECES),
            dma(len(sides)),
            dma(len(sides), links),
            dma(len(sides), links),
        ],
        compiler_params=pltpu.CompilerParams(collective_id=ident, has_side_effects=True),
        cost_estimate=pl.CostEstimate(
            flops=0, bytes_accessed=200_000_000, transcendentals=0
        ),
    )(high, low, add, *sides)


def unit_lower_inverse(low):
    size = low.shape[0]
    row = lax.broadcasted_iota(jnp.int32, low.shape, 0)
    col = lax.broadcasted_iota(jnp.int32, low.shape, 1)

    def same(width):
        shift = width.bit_length() - 1
        return (row >> shift) == (col >> shift)

    eye = (row == col).astype(F32)
    width = 8
    near = jnp.where(same(width), low, 0.0)
    square = exact(near, near)
    inverse = eye - near
    inverse = inverse + exact(inverse, square)
    square = exact(square, square)
    inverse = inverse + exact(inverse, square)
    while width < size:
        cross = jnp.where(same(2 * width) & jnp.logical_not(same(width)), low, 0.0)
        inverse = inverse - exact(inverse, exact(cross, inverse))
        width *= 2
    return inverse


def unit_parts(values):
    scale = lax.rsqrt(jnp.sum(values * values, axis=-1, keepdims=True) + EPSILON)
    return values * scale, scale


def unit_back(unit, scale, grad):
    return scale * (grad - unit * jnp.sum(unit * grad, axis=-1, keepdims=True))


def strict_lower(size):
    row = lax.broadcasted_iota(jnp.int32, (size, size), 0)
    col = lax.broadcasted_iota(jnp.int32, (size, size), 1)
    return (row > col).astype(F32)


def convolve(x_ref, rim_ref, taps_ref, same_ref, ext):
    size = x_ref.shape[1]
    ext[:RIM] = rim_ref[0].astype(F32)
    ext[RIM:] = x_ref[0].astype(F32)
    mixed = taps_ref[0:1] * ext[RIM:]
    for lag in range(1, CONV):
        mixed = mixed + taps_ref[lag : lag + 1] * ext[RIM - lag : RIM - lag + size] * (
            same_ref[:, lag : lag + 1]
        )
    return mixed


def convolve_back(grad, taps_ref, same_ref, ext, back):
    size = grad.shape[0]
    back[:RIM] = jnp.zeros((RIM, grad.shape[1]), F32)
    back[RIM:] = taps_ref[0:1] * grad
    sums = [jnp.sum(grad * ext[RIM:], axis=0, keepdims=True)]
    for lag in range(1, CONV):
        kept = grad * same_ref[:, lag : lag + 1]
        sums.append(
            jnp.sum(kept * ext[RIM - lag : RIM - lag + size], axis=0, keepdims=True)
        )
        back[RIM - lag : RIM - lag + size] += taps_ref[lag : lag + 1] * kept
    return jnp.concatenate(sums, axis=0)


def silu_parts(values):
    sig = jax.nn.sigmoid(values)
    return values * sig, sig * (1.0 + values * (1.0 - sig))


def chunk_forward_kernel(
    *refs,
):
    pre_refs, rim_refs, tap_refs = refs[:4], refs[4:8], refs[8:12]
    same_ref, beta_ref, decay_ref, start_ref, tail_ref = refs[12:17]
    (
        inverse_ref,
        scores_ref,
        own_ref,
        effect_ref,
        offset_ref,
        high_ref,
        low_ref,
        back_high_ref,
        back_low_ref,
    ) = refs[17:26]
    ext = refs[26]
    active = []
    for i in range(4):
        mixed = convolve(pre_refs[i], rim_refs[i], tap_refs[i], same_ref, ext.at[i])
        active.append(silu_parts(mixed)[0])
    size, key_size = active[0].shape
    beta, start, tail = beta_ref[0], start_ref[0], tail_ref[0]
    decay = decay_ref[0]
    query = unit_parts(active[0])[0] * key_size ** (-0.5)
    key = unit_parts(active[1])[0]
    values = jnp.concatenate(active[2:], axis=1)
    inner = exact(key, key, (1, 1))
    inverse = unit_lower_inverse(beta * inner * (decay * strict_lower(size)))
    scores = exact(query, key, (1, 1)) * decay
    update = exact(inverse, beta * values)
    reach = exact(inverse, (beta * start) * key)
    inverse_ref[0] = inverse
    scores_ref[0] = scores
    own_ref[...] = exact(scores, update)
    effect_ref[0] = start * query - exact(scores, reach)
    last = tail * key
    offset_ref[0] = exact(last, update, (0, 0))
    row = lax.broadcasted_iota(jnp.int32, (key_size, key_size), 0)
    col = lax.broadcasted_iota(jnp.int32, (key_size, key_size), 1)
    transfer = jnp.where(row == col, start[size - 1 :, :], 0.0) - exact(last, reach, (0, 0))
    for matrix, top_ref, rest_ref in (
        (transfer, high_ref, low_ref),
        (transfer.T, back_high_ref, back_low_ref),
    ):
        top = matrix.astype(BF16)
        top_ref[0] = top
        rest_ref[0] = (matrix - top.astype(F32)).astype(BF16)


def gate_forward_kernel(own_ref, effect_ref, state_ref, gate_ref, gain_ref, mixed_ref, gated_ref):
    mixed = own_ref[...] + exact(effect_ref[0], state_ref[0].astype(F32))
    mixed_ref[...] = mixed
    gate = gate_ref[...].astype(F32)
    gated_ref[...] = (
        rms_scale(mixed) * gain_ref[...] * (gate * jax.nn.sigmoid(gate))
    ).astype(BF16)


def gate_backward_kernel(
    mixed_ref, gate_ref, gain_ref, grad_ref, effect_ref, out_ref, gate_grad_ref, gain_grad_ref, add_ref
):
    mixed = mixed_ref[...]
    gate = gate_ref[...].astype(F32)
    grad = grad_ref[...].astype(F32)
    gain = gain_ref[...]
    scale = lax.rsqrt(jnp.mean(mixed * mixed, axis=-1, keepdims=True) + EPSILON)
    normed = mixed * scale
    sig = jax.nn.sigmoid(gate)
    act = gate * sig
    gain_grad_ref[0] = jnp.sum(grad * normed * act, axis=0, keepdims=True)
    gate_grad_ref[...] = (
        grad * normed * gain * (sig * (1.0 + gate * (1.0 - sig)))
    ).astype(BF16)
    inner = grad * gain * act
    mixed_grad = scale * (inner - normed * jnp.mean(inner * normed, axis=-1, keepdims=True))
    out_ref[...] = mixed_grad
    add_ref[0] = exact(effect_ref[0], mixed_grad, (0, 0))


def chunk_backward_kernel(heads, *refs):
    pre_refs, rim_refs, tap_refs = refs[:4], refs[4:8], refs[8:12]
    same_ref, beta_ref, decay_ref, start_ref, tail_ref = refs[12:17]
    inverse_ref, scores_ref, state_ref, mixed_ref, ending_ref = refs[17:22]
    (
        grad_ref,
        grad_tail_ref,
        grad_rim_ref,
        taps_grad_ref,
        dbeta_ref,
        ddecay_ref,
        dstart_ref,
        dtail_ref,
    ) = refs[22:30]
    ext, back = refs[30:]
    active, slopes = [], []
    for i in range(4):
        mixed = convolve(pre_refs[i], rim_refs[i], tap_refs[i], same_ref, ext.at[i])
        value, slope = silu_parts(mixed)
        active.append(value)
        slopes.append(slope)
    size, key_size = active[0].shape
    values = jnp.concatenate(active[2:], axis=1)
    beta, start, tail = beta_ref[0], start_ref[0], tail_ref[0]
    decay, inverse, scores = decay_ref[0], inverse_ref[0], scores_ref[0]
    state = state_ref[0].astype(F32)
    ending = ending_ref[0].astype(F32)
    mixed_grad = mixed_ref[...]
    unit_q, scale_q = unit_parts(active[0])
    query = unit_q * key_size ** (-0.5)
    key, scale_k = unit_parts(active[1])
    below = strict_lower(size)
    inner = exact(key, key, (1, 1))
    raw = exact(query, key, (1, 1))
    recalled = exact(key, state)
    miss = values - start * recalled
    update = exact(inverse, beta * miss)
    mixed_state = exact(mixed_grad, state, (1, 1))
    last = tail * key
    dupdate = exact(scores, mixed_grad, (0, 0)) + exact(last, ending)
    dscores = exact(mixed_grad, update, (1, 1))
    dlast = exact(update, ending, (1, 1))
    dright = exact(inverse, dupdate, (0, 0))
    dlower = -exact(dright, update, (1, 1)) * below
    dscaled = dscores * decay
    dquery = start * mixed_state + exact(dscaled, key)
    dinner = beta * dlower * decay
    dkey = (
        tail * dlast
        + exact(dscaled, query, (0, 0))
        - exact((beta * start) * dright, state, (1, 1))
        + exact(dinner, key)
        + exact(dinner, key, (0, 0))
    )
    right_recalled = jnp.sum(dright * recalled, axis=-1, keepdims=True)
    dbeta_ref[0] = jnp.sum(dright * miss, axis=-1, keepdims=True) + jnp.sum(
        dlower * inner * decay, axis=-1, keepdims=True
    )
    final = jnp.sum(jnp.sum(ending * state, axis=-1, keepdims=True), axis=0, keepdims=True)
    row = lax.broadcasted_iota(jnp.int32, (size, 1), 0)
    dstart_ref[0] = (
        jnp.sum(query * mixed_state, axis=-1, keepdims=True)
        - beta * right_recalled
        + jnp.where(row == size - 1, final, 0.0)
    )
    dtail_ref[0] = jnp.sum(key * dlast, axis=-1, keepdims=True)
    ddecay_ref[0] = dscores * raw + beta * dlower * inner
    dvalues = beta * dright
    grads = [
        unit_back(unit_q, scale_q, dquery * key_size ** (-0.5)),
        unit_back(key, scale_k, dkey),
        dvalues[:, :key_size],
        dvalues[:, key_size:],
    ]
    head = pl.program_id(0)
    per = grad_ref.shape[2] // key_size
    for i, block in enumerate((head, heads + head, 2 * heads + 2 * head, 2 * heads + 2 * head + 1)):
        sums = convolve_back(grads[i] * slopes[i], tap_refs[i], same_ref, ext.at[i], back)
        slab = block // per
        columns = pl.ds(pl.multiple_of((block % per) * key_size, key_size), key_size)
        grad_ref[slab, :, columns] = back[RIM:].astype(BF16)
        grad_tail_ref[slab, :, columns] = back[size:]
        grad_rim_ref[slab, :, columns] = back[:RIM].astype(BF16)
        taps_grad_ref[slab, 0:CONV, columns] = sums


def by_head(*shape):
    return pl.BlockSpec((1,) + shape, lambda h: (h, 0, 0))


def by_columns(rows, width, offset=0):
    return pl.BlockSpec((rows, width), lambda h: (0, h + offset))


def head_call(body, heads, in_specs, out_specs, out_shape, operands, flops, scratch=()):
    return pl.pallas_call(
        body,
        scratch_shapes=scratch,
        grid=(heads,),
        in_specs=in_specs,
        out_specs=out_specs,
        out_shape=out_shape,
        cost_estimate=pl.CostEstimate(flops=flops, bytes_accessed=20_000_000, transcendentals=0),
    )(*operands)


def shaped(*shape, dtype=F32):
    return jax.ShapeDtypeStruct(shape, dtype)


def decays(segment, before, decay_pre, beta_pre, a_log):
    length = segment.shape[0]
    beta = jax.nn.sigmoid(beta_pre)
    decay_log = -jnp.exp(a_log) * jax.nn.softplus(decay_pre)
    order = jnp.arange(length)
    lower = order[:, None] >= order[None, :]
    running = exact(lower.astype(F32), decay_log).T
    live = (segment[:, None] == segment[None, :]) & lower
    gap = running[:, :, None] - running[:, None, :]
    decay = jnp.where(live, jnp.exp(jnp.where(live, gap, 0.0)), 0.0)
    start = jnp.exp(running) * (segment == before).astype(F32)
    live_last = segment == segment[-1]
    last_gap = running[:, -1:] - running
    tail = jnp.where(live_last, jnp.exp(jnp.where(live_last, last_gap, 0.0)), 0.0)
    return beta.T[:, :, None], decay, start[:, :, None], tail[:, :, None]


def local(
    hidden_in,
    segment_ids,
    grad_out,
    attn_gain,
    w_query,
    w_key,
    w_value,
    w_decay,
    w_beta,
    w_outgate,
    a_log,
    conv_query,
    conv_key,
    conv_value,
    out_gain,
    w_output,
    mlp_gain,
    w_gate,
    w_up,
    w_down,
):
    rows, count = lax.axis_size("dp"), lax.axis_size("zq")
    group = 2 * rows
    segment = segment_ids[0]
    length, width = hidden_in.shape[1:]
    heads = a_log.shape[0]
    key_width, value_width = w_query.shape[1], w_value.shape[1]
    key_size, value_size = key_width // heads, out_gain.shape[0]
    mixer_width = 2 * key_width + value_width
    hidden_width = w_gate.shape[1]
    owned = w_query.shape[0]
    margin = CONV - 1
    me = lax.axis_index("dp") * 2 + lax.axis_index("c")
    mixer_part = mixer_width // group
    back_width = value_width // group
    ffn_width = hidden_width // group

    def shuffled(values):
        return (
            values.reshape(-1, rows, count, 2 * owned).swapaxes(1, 2).reshape(-1, width)
        )

    def unshuffled(values):
        return (
            values.reshape(-1, count, rows, 2 * owned).swapaxes(1, 2).reshape(-1, width)
        )

    def cut(values):
        return values.astype(BF16).reshape(owned, group, -1).swapaxes(0, 1)

    def joined(values):
        return values.swapaxes(0, 1).reshape(values.shape[1], -1)

    def gathered(values):
        return lax.all_gather(values.reshape(group * owned, -1), "zq", axis=0, tiled=True)

    def scattered(values):
        return lax.psum_scatter(
            values, "zq", scatter_dimension=0, tiled=True
        ).reshape(group, owned, -1)

    def blocks(values):
        return values.astype(BF16).reshape(group, length, -1)

    (
        mixer_weights,
        first_own,
        gate_up_own,
        normed_all,
        grad_all,
        hidden_low,
        normed_low,
        grad_low,
    ) = begin(
        hidden_in[0],
        grad_out[0],
        attn_gain[None],
        w_decay,
        w_beta,
        (w_query, w_key, w_value, w_outgate, w_output, w_down, w_gate, w_up),
        0,
    )
    mixer_weights = mixer_weights.reshape(width, -1)
    normed_all = normed_all.reshape(-1, width)
    grad_all = grad_all.reshape(-1, width)
    project = mixer_weights[:, : mixer_part + back_width]
    small_weights = mixer_weights[:, mixer_part + back_width :]
    first_weights = gathered(first_own)
    output_weights, down = first_weights[:, :back_width], first_weights[:, back_width:]

    inputs = hidden_low.astype(F32)
    attn_row, mlp_row = shuffled(attn_gain[None]), shuffled(mlp_gain[None])
    normed, norm_pull = jax.vjp(rms_scale, inputs)
    pre_all = mm(normed_all, project[:, :mixer_part])
    gate_all = mm(normed_all, project[:, mixer_part:])
    pre, rim = swap_on(blocks(pre_all), 3)
    small_pre = mm(normed_low, small_weights)
    decay_pre, beta_pre = small_pre[:, :heads], small_pre[:, heads : 2 * heads]
    rim_ids = lax.ppermute(
        segment[-margin:],
        ("zq", "c"),
        [(i, i + 1) for i in range(2 * count - 1)],
    )
    seg_ext = jnp.concatenate([rim_ids, segment])
    same = jnp.stack(
        [
            (segment == seg_ext[margin - lag : margin - lag + length]).astype(F32)
            for lag in range(CONV)
        ],
        axis=1,
    )
    (beta, decay, start, tail), decay_pull = jax.vjp(
        partial(decays, segment, seg_ext[margin - 1]), decay_pre, beta_pre, a_log
    )
    slabs, slab = group, mixer_part
    if slab % key_size:
        slabs, slab = mixer_width // (3 * key_size), 3 * key_size
        pre, rim = [
            joined(part).reshape(-1, slabs, slab).swapaxes(0, 1) for part in (pre, rim)
        ]
    per = slab // key_size
    taps = jnp.concatenate([conv_query, conv_key, conv_value], axis=1)
    channel_blocks = [
        lambda h: h,
        lambda h: heads + h,
        lambda h: 2 * heads + 2 * h,
        lambda h: 2 * heads + 2 * h + 1,
    ]

    def slab_specs(lines):
        return [
            pl.BlockSpec((1, lines, key_size), lambda h, b=b: (b(h) // per, 0, b(h) % per))
            for b in channel_blocks
        ]

    token_specs = (
        slab_specs(length)
        + slab_specs(RIM)
        + [pl.BlockSpec((CONV, key_size), lambda h, b=b: (0, b(h))) for b in channel_blocks]
        + [pl.BlockSpec((length, CONV), lambda h: (0, 0))]
        + [by_head(length, 1), by_head(length, length), by_head(length, 1), by_head(length, 1)]
    )
    token_args = (pre,) * 4 + (rim,) * 4 + (taps,) * 4 + (same, beta, decay, start, tail)
    ext_shape = pltpu.VMEM((4, RIM + length, key_size), F32)
    values_spec = by_columns(length, value_size)
    state_spec = by_head(key_size, value_size)
    inverse, scores, own, effect, offset, high, low, back_high, back_low = head_call(
        chunk_forward_kernel,
        heads,
        token_specs,
        [
            by_head(length, length),
            by_head(length, length),
            values_spec,
            by_head(length, key_size),
            state_spec,
        ]
        + [by_head(key_size, key_size)] * 4,
        [
            shaped(heads, length, length),
            shaped(heads, length, length),
            shaped(length, value_width),
            shaped(heads, length, key_size),
            shaped(heads, key_size, value_size),
        ]
        + [shaped(heads, key_size, key_size, dtype=BF16)] * 4,
        token_args,
        6_000_000_000,
        [ext_shape],
    )
    state, gate_back = chain(high, low, offset, (gate_all.reshape(group, length, -1),), True, 5)
    gate_pre = joined(gate_back)
    gate_up_own, state, first_weights = lax.optimization_barrier(
        (gate_up_own, state, first_weights)
    )
    gate_up = gathered(gate_up_own)
    gain_spec = pl.BlockSpec((1, value_size), lambda h: (0, 0))
    gain_row = out_gain[None]
    mixed, gated = head_call(
        gate_forward_kernel,
        heads,
        [values_spec, by_head(length, key_size), state_spec, values_spec, gain_spec],
        [values_spec, values_spec],
        [shaped(length, value_width), shaped(length, value_width, dtype=BF16)],
        (own, effect, state, gate_pre, gain_row),
        1_000_000_000,
    )
    gated_cut = gated.reshape(length, group, back_width).swapaxes(0, 1)
    gated_all = swap(gated_cut, 6).reshape(-1, back_width)
    middle, normed_two_all = turn(
        blocks(mm(gated_all, output_weights, (1, 1))), mlp_row, inputs, None, 4
    )
    normed_two_all = normed_two_all.reshape(-1, width)

    both = mm(normed_two_all, gate_up)
    hidden, swiglu_pull = jax.vjp(swiglu, both[:, :ffn_width], both[:, ffn_width:])
    hidden_low = hidden.astype(BF16)
    grad_gate, grad_up = swiglu_pull(mm(grad_all, down))
    both_grad_low = jnp.concatenate([grad_gate, grad_up], axis=1).astype(BF16)
    grad_normed_two_parts = blocks(mm(both_grad_low, gate_up, (1, 1)))
    gate_up_rows = mm(normed_two_all, both_grad_low, (0, 0)).astype(BF16)
    grad_normed_two_parts, gate_up_rows = lax.optimization_barrier(
        (grad_normed_two_parts, gate_up_rows)
    )
    gate_up_rows = scattered(gate_up_rows)
    grad_middle, attended_grad_all, grad_mlp_gain = turn(
        grad_normed_two_parts, mlp_row, grad_low, middle, 2
    )
    attended_grad_all = attended_grad_all.reshape(-1, width)

    grad_gated = joined(swap(blocks(mm(attended_grad_all, output_weights)), 6))
    output_rows = mm(attended_grad_all, gated_all, (0, 0)).astype(BF16)
    down_rows = mm(grad_all, hidden_low, (0, 0)).astype(BF16)
    mlp_parts = blocks(mm(hidden_low, down, (1, 1)))
    mixed_grad, gate_pre_grad, gain_grad, state_add = head_call(
        gate_backward_kernel,
        heads,
        [values_spec, values_spec, gain_spec, values_spec, by_head(length, key_size)],
        [values_spec, values_spec, by_head(1, value_size), state_spec],
        [
            shaped(length, value_width),
            shaped(length, value_width, dtype=BF16),
            shaped(heads, 1, value_size),
            shaped(heads, key_size, value_size),
        ],
        (mixed, gate_pre, gain_row, grad_gated, effect),
        1_000_000_000,
    )
    grad_out_gain = jnp.sum(gain_grad, axis=(0, 1))
    side_rows = jnp.concatenate([down_rows, output_rows], axis=1)
    state_add, mlp_parts, gate_up_rows, side_rows = lax.optimization_barrier(
        (state_add, mlp_parts, gate_up_rows, side_rows)
    )
    ending, gate_grad_back, mlp_back = chain(
        back_high,
        back_low,
        state_add,
        (gate_pre_grad.reshape(length, group, back_width).swapaxes(0, 1), mlp_parts),
        False,
        8,
    )
    gate_grad_all = gate_grad_back.reshape(-1, back_width)
    side_rows, ending = lax.optimization_barrier((side_rows, ending))
    side_rows = scattered(side_rows)
    gate_up_back = lax.all_to_all(gate_up_rows, ("dp", "c"), 0, 0, tiled=True)
    whole = lambda *shape: pl.BlockSpec(shape, lambda h: (0, 0, 0))
    grad_pre, grad_tail, grad_rim, grad_taps, dbeta, ddecay, dstart, dtail = head_call(
        partial(chunk_backward_kernel, heads),
        heads,
        token_specs
        + [
            by_head(length, length),
            by_head(length, length),
            state_spec,
            values_spec,
            state_spec,
        ],
        [
            whole(slabs, length, slab),
            whole(slabs, RIM, slab),
            whole(slabs, RIM, slab),
            whole(slabs, 2 * CONV, slab),
        ]
        + [by_head(length, 1), by_head(length, length), by_head(length, 1), by_head(length, 1)],
        [
            shaped(slabs, length, slab, dtype=BF16),
            shaped(slabs, RIM, slab),
            shaped(slabs, RIM, slab, dtype=BF16),
            shaped(slabs, 2 * CONV, slab),
            shaped(heads, length, 1),
            shaped(heads, length, length),
            shaped(heads, length, 1),
            shaped(heads, length, 1),
        ],
        token_args + (inverse, scores, state, mixed_grad, ending),
        12_000_000_000,
        [ext_shape, pltpu.VMEM((RIM + length, key_size), F32)],
    )
    grad_decay, grad_beta, grad_alog = decay_pull((dbeta, ddecay, dstart, dtail))
    grad_taps = joined(grad_taps)[:CONV]
    grad_conv_one = grad_taps[:, :key_width]
    grad_conv_two = grad_taps[:, key_width : 2 * key_width]
    grad_conv_three = grad_taps[:, 2 * key_width :]
    small_grad = jnp.concatenate([grad_decay, grad_beta], axis=1).astype(BF16)
    small_grad = jnp.pad(small_grad, ((0, 0), (0, LANES - 2 * heads)))
    if slabs != group:
        grad_pre, grad_tail, grad_rim = [
            joined(part).reshape(-1, group, mixer_part).swapaxes(0, 1)
            for part in (grad_pre, grad_tail, grad_rim)
        ]
    grad_pre, gate_up_back = lax.optimization_barrier((grad_pre, gate_up_back))
    grads_all = swap_back(grad_pre, grad_tail, grad_rim, small_grad, 10).reshape(
        group * length, -1
    )
    mixer_parts = jnp.concatenate(
        [
            mm(normed_all, grads_all, (0, 0)).astype(BF16),
            mm(normed_all, gate_grad_all, (0, 0)).astype(BF16),
        ],
        axis=1,
    )
    mixer_parts, side_rows = lax.optimization_barrier((mixer_parts, side_rows))
    mixer_rows = scattered(mixer_parts)
    combined = fold(
        blocks(
            mm(
                jnp.concatenate([grads_all[:, :mixer_part], gate_grad_all], axis=1),
                project,
                (1, 1),
            )
        ),
        7,
    )
    mlp_part = jnp.sum(mlp_back.astype(F32), axis=0)
    result = (middle + mlp_part).astype(BF16)
    combined = combined + mm(small_grad, small_weights, (1, 1))
    grad_attn_gain = jnp.sum(combined * normed, axis=0)
    grad_inputs = grad_middle + norm_pull(combined * attn_row)[0]

    side_back = lax.all_to_all(side_rows, ("dp", "c"), 0, 0, tiled=True).astype(F32)
    gate_grad = joined(gate_up_back[:, :, :ffn_width].astype(F32))
    up_grad = joined(gate_up_back[:, :, ffn_width:].astype(F32))
    down_grad = joined(side_back[:, :, :ffn_width])
    output_grad = joined(side_back[:, :, ffn_width:])

    pieces = (
        grad_attn_gain,
        grad_alog,
        grad_conv_one,
        grad_conv_two,
        grad_conv_three,
        grad_out_gain,
        grad_mlp_gain,
    )
    flat = jnp.concatenate([piece.reshape(-1) for piece in pieces])
    lines = -(-flat.shape[0] // (8 * LANES)) * 8
    flat = jnp.pad(flat, (0, lines * LANES - flat.shape[0])).reshape(lines, LANES)
    flat = jnp.sum(spread(flat, 11), axis=0)
    flat = jnp.sum(column(flat, 12), axis=0).reshape(-1)
    mixer_rows, _ = lax.optimization_barrier((mixer_rows, (flat, grad_inputs, side_back)))
    mixer_swapped = swap(
        jnp.concatenate(
            [mixer_rows[:, :, :mixer_part], mixer_rows[:, :, mixer_part + LANES :]], axis=2
        ),
        15,
    ).astype(F32)
    mixer_back = joined(mixer_swapped[:, :, :mixer_part])
    outgate_grad = joined(mixer_swapped[:, :, mixer_part:])
    small_rows = lax.dynamic_index_in_dim(mixer_rows, me, 0, keepdims=False)
    small_rows = small_rows[:, mixer_part : mixer_part + LANES].astype(F32)
    summed, at = [], 0
    for piece in pieces:
        summed.append(flat[at : at + piece.size].reshape(piece.shape))
        at += piece.size

    return (
        unshuffled(result)[None],
        unshuffled(grad_inputs.astype(BF16))[None],
        unshuffled(summed[0][None])[0],
        mixer_back[:, :key_width],
        mixer_back[:, key_width : 2 * key_width],
        mixer_back[:, 2 * key_width :],
        small_rows[:, :heads],
        small_rows[:, heads : 2 * heads],
        outgate_grad,
        summed[1],
        summed[2],
        summed[3],
        summed[4],
        summed[5],
        output_grad,
        unshuffled(summed[6][None])[0],
        gate_grad,
        up_grad,
        down_grad,
    )


def solution(mesh):
    rows, places = mesh.shape["dp"], mesh.shape["seq"]
    fine = Mesh(mesh.devices.reshape(rows, places // 2, 2), ("dp", "zq", "c"))
    tokens = P("dp", ("zq", "c"), None)
    owned = P(("dp", "zq", "c"), None)
    return jax.shard_map(
        local,
        mesh=fine,
        in_specs=(tokens, P("dp", ("zq", "c")), tokens, P())
        + (owned,) * 6
        + (P(),) * 5
        + (owned, P(), owned, owned, owned),
        out_specs=(tokens, tokens, P())
        + (owned,) * 6
        + (P(),) * 5
        + (owned, P(), owned, owned, owned),
        check_vma=False,
    )
```

```python
from functools import partial

import jax
import jax.numpy as jnp
from jax import lax
from jax.experimental import pallas as pl
from jax.experimental.pallas import tpu as pltpu
from jax.sharding import Mesh
from jax.sharding import PartitionSpec as P

CONV = 4
EPSILON = 1e-06
EXACT = lax.Precision.HIGHEST
BF16 = jnp.bfloat16
F32 = jnp.float32
BY_MESH = pl.DeviceIdType.MESH
LANES = 128
PIECES = 2
CHUNKS = 2
RIM = 16


def rms_scale(values):
    return values * lax.rsqrt(jnp.mean(values * values, axis=-1, keepdims=True) + EPSILON)


def swiglu(gate_values, up_values):
    return jax.nn.silu(gate_values) * up_values


def mm(left, right, over=(1, 0)):
    return lax.dot_general(
        left, right, (((over[0],), (over[1],)), ((), ())), preferred_element_type=F32
    )


def exact(left, right, over=(1, 0)):
    return lax.dot_general(
        left,
        right,
        (((over[0],), (over[1],)), ((), ())),
        precision=EXACT,
        preferred_element_type=F32,
    )


def place():
    return lax.axis_index("dp"), lax.axis_index("zq"), lax.axis_index("c")


def greet(peers):
    barrier = pltpu.get_barrier_semaphore()
    for peer in peers:
        pl.semaphore_signal(barrier, inc=1, device_id=peer, device_id_type=BY_MESH)
    pl.semaphore_wait(barrier, len(peers))


def remote(source, target, send, recv, peer):
    return pltpu.make_async_remote_copy(
        src_ref=source,
        dst_ref=target,
        send_sem=send,
        recv_sem=recv,
        device_id=peer,
        device_id_type=BY_MESH,
    )


def plane_offsets(rows):
    return [(k, flip) for k in range(rows) for flip in (0, 1) if (k, flip) != (0, 0)]


def plane_peer(offset, rows):
    d, z, c = place()
    k, flip = offset
    return (lax.rem(d + k, rows), z, 1 - c if flip else c)


def swap_kernel(rows, x_ref, o_ref, own, send, recv):
    d, z, c = place()
    me = d * 2 + c
    offsets = plane_offsets(rows)
    greet([plane_peer(offset, rows) for offset in offsets])
    copies = []
    for i, offset in enumerate(offsets):
        peer = plane_peer(offset, rows)
        copy = remote(
            x_ref.at[peer[0] * 2 + peer[2]], o_ref.at[me], send.at[i], recv.at[i], peer
        )
        copy.start()
        copies.append(copy)
    keep = pltpu.make_async_copy(x_ref.at[me], o_ref.at[me], own)
    keep.start()
    keep.wait()
    for copy in copies:
        copy.wait()


def spread_kernel(rows, x_ref, o_ref, own, send, recv, pair_send, pair_recv):
    d, z, c = place()
    me = d * 2 + c
    pair = (d, z, 1 - c)
    others = [(lax.rem(d + k, rows), z, c) for k in range(1, rows)]
    greet(others + [pair])
    copies = []
    for i, peer in enumerate(others):
        copy = remote(x_ref, o_ref.at[me], send.at[i], recv.at[i], peer)
        copy.start()
        copies.append(copy)
    hand = remote(x_ref, o_ref.at[me], pair_send.at[0], pair_recv.at[0], pair)
    hand.start()
    keep = pltpu.make_async_copy(x_ref, o_ref.at[me], own)
    keep.start()
    hands = [hand]
    for i, copy in enumerate(copies):
        copy.wait_recv()
        origin = lax.rem(d + rows - (i + 1), rows) * 2 + c
        hand = remote(
            o_ref.at[origin], o_ref.at[origin], pair_send.at[i + 1], pair_recv.at[i + 1], pair
        )
        hand.start()
        hands.append(hand)
    keep.wait()
    for copy in copies:
        copy.wait_send()
    for hand in hands:
        hand.wait()


def fold_kernel(
    rows, x_ref, o_ref, mine, theirs, load, pair_send, pair_recv, send, recv, own
):
    d, z, c = place()
    pair = (d, z, 1 - c)
    others = [(lax.rem(d + k, rows), z, c) for k in range(1, rows)]
    greet(others + [pair])
    order = [lax.rem(d + k, rows) for k in range(1, rows)] + [d]
    hands, loads = [], []
    for i, to in enumerate(order):
        hand = remote(
            x_ref.at[to * 2 + (1 - c)], theirs.at[i], pair_send.at[i], pair_recv.at[i], pair
        )
        hand.start()
        hands.append(hand)
        copy = pltpu.make_async_copy(x_ref.at[to * 2 + c], mine.at[i], load.at[i])
        copy.start()
        loads.append(copy)
    copies = []
    for i in range(rows):
        loads[i].wait()
        hands[i].wait_recv()
        mine[i] = (mine[i].astype(F32) + theirs[i].astype(F32)).astype(BF16)
        if i < rows - 1:
            copy = remote(mine.at[i], o_ref.at[d], send.at[i], recv.at[i], others[i])
        else:
            copy = pltpu.make_async_copy(mine.at[i], o_ref.at[d], own)
        copy.start()
        copies.append(copy)
    for hand in hands:
        hand.wait_send()
    for copy in copies:
        copy.wait()


def slab_pieces(widths, slab, t):
    at, end, base = t * slab, (t + 1) * slab, 0
    for source, width in enumerate(widths):
        low, high = max(at, base), min(end, base + width)
        if low < high:
            yield source, low - base, low - at, high - low
        base += width


def start_kernel(rows, count, hidden_ref, grad_ref, gain_ref, decay_ref, beta_ref, *refs):
    weight_refs = refs[:8]
    all_ref, *side_outs = refs[8:11]
    one_out_ref, two_out_ref, hidden_out_ref, one_ref, two_ref = refs[11:16]
    raws, cut_ref, sides = refs[16:24], refs[24], refs[25:27]
    (
        load,
        own,
        deal_send,
        deal_recv,
        side_send,
        side_recv,
        round_send,
        round_recv,
        pair_send,
        pair_recv,
        up_send,
        up_recv,
        down_send,
        down_recv,
    ) = refs[27:]
    loads = [
        pltpu.make_async_copy(weight, raw, load.at[i])
        for i, (weight, raw) in enumerate(zip(weight_refs, raws))
    ]
    for copy in loads:
        copy.start()
    d, z, c = place()
    me = d * 2 + c
    group = 2 * rows
    pair = (d, z, 1 - c)
    others = [(lax.rem(d + k, rows), z, c) for k in range(1, rows)]
    above = (d, lax.rem(z + 1, count), c)
    below = (d, lax.rem(z + count - 1, count), c)
    has_above, has_below = z < count - 1, z > 0
    offsets = plane_offsets(rows)
    barrier = pltpu.get_barrier_semaphore()
    for offset in offsets:
        pl.semaphore_signal(
            barrier, inc=1, device_id=plane_peer(offset, rows), device_id_type=BY_MESH
        )

    @pl.when(has_above)
    def _():
        pl.semaphore_signal(barrier, inc=1, device_id=above, device_id_type=BY_MESH)

    @pl.when(has_below)
    def _():
        pl.semaphore_signal(barrier, inc=1, device_id=below, device_id_type=BY_MESH)

    owned = raws[0].shape[0]
    wide = cut_ref.shape[2]
    heads = decay_ref.shape[1]
    back = raws[3].shape[1] // group
    slab = wide - LANES - back
    for copy in loads[:4]:
        copy.wait()
    widths = [raw.shape[1] for raw in raws[:3]]
    for t in range(group):
        for source, at, to, size in slab_pieces(widths, slab, t):
            cut_ref[t, :, to : to + size] = raws[source][:, at : at + size].astype(BF16)
        cut_ref[t, :, slab : slab + back] = raws[3][:, t * back : (t + 1) * back].astype(BF16)
        cut_ref[t, :, slab + back :] = jnp.concatenate(
            [decay_ref[...], beta_ref[...], jnp.zeros((owned, LANES - 2 * heads), F32)], axis=1
        ).astype(BF16)
    pl.semaphore_wait(
        barrier, len(offsets) + has_above.astype(jnp.int32) + has_below.astype(jnp.int32)
    )

    def deal(source, target, send, recv):
        copies = []
        for i, offset in enumerate(offsets):
            peer = plane_peer(offset, rows)
            copy = remote(
                source.at[peer[0] * 2 + peer[2]], target.at[me], send.at[i], recv.at[i], peer
            )
            copy.start()
            copies.append(copy)
        return copies

    def origin(offset):
        k, flip = offset
        return lax.rem(d + rows - k, rows) * 2 + (1 - c if flip else c)

    def passed(k, i, block, upward):
        at = z - k if upward else z + k
        at = lax.rem(at + count, count)
        send, recv = (up_send, up_recv) if upward else (down_send, down_recv)
        return remote(
            all_ref.at[at, block],
            all_ref.at[at, block],
            send.at[k, i],
            recv.at[k, i],
            above if upward else below,
        )

    def give(k, i, block):
        @pl.when(has_above & (z - k >= 0))
        def _():
            passed(k, i, block, True).start()

        @pl.when(has_below & (z + k <= count - 1))
        def _():
            passed(k, i, block, False).start()

    def take(k, i, block):
        @pl.when(z - k - 1 >= 0)
        def _():
            passed(k, i, block, True).wait_recv()

        @pl.when(z + k + 1 <= count - 1)
        def _():
            passed(k, i, block, False).wait_recv()

    def given(k, i, block):
        @pl.when(has_above & (z - k >= 0))
        def _():
            passed(k, i, block, True).wait_send()

        @pl.when(has_below & (z + k <= count - 1))
        def _():
            passed(k, i, block, False).wait_send()

    dealt = deal(cut_ref, all_ref.at[z], deal_send, deal_recv)
    keep = pltpu.make_async_copy(cut_ref.at[me], all_ref.at[z, me], own.at[0])
    keep.start()
    keep.wait()
    blocks = [me] + [origin(offset) for offset in offsets]
    give(0, 0, me)
    run = 2 * owned
    width = hidden_ref.shape[1]

    def moved(values):
        return jnp.concatenate(
            [
                values[:, (b * count + a) * run : (b * count + a + 1) * run]
                for a in range(count)
                for b in range(rows)
            ],
            axis=1,
        )

    hidden = moved(hidden_ref[...])
    hidden_out_ref[...] = hidden
    one_ref[...] = (rms_scale(hidden.astype(F32)) * moved(gain_ref[...])).astype(BF16)
    two_ref[...] = moved(grad_ref[...])
    rounds = []
    for j, (source, target) in enumerate(((one_ref, one_out_ref), (two_ref, two_out_ref))):
        copies = []
        for i, peer in enumerate(others):
            copies.append(
                remote(source, target.at[me], round_send.at[j, i], round_recv.at[j, i], peer)
            )
        copies.append(
            remote(source, target.at[me], pair_send.at[j, 0], pair_recv.at[j, 0], pair)
        )
        rounds.append(copies)
    for i, copy in enumerate(dealt):
        copy.wait_recv()
        give(0, i + 1, blocks[i + 1])
    keeps = [
        pltpu.make_async_copy(one_ref, one_out_ref.at[me], own.at[1]),
        pltpu.make_async_copy(two_ref, two_out_ref.at[me], own.at[2]),
    ]
    for copy in rounds[0] + keeps:
        copy.start()
    for copy in loads[4:]:
        copy.wait()
    deals = []
    for j, (laid, side, side_out) in enumerate(zip((raws[4:6], raws[6:]), sides, side_outs)):
        for t in range(group):
            at = 0
            for raw in laid:
                size = raw.shape[1] // group
                side[t, :, at : at + size] = raw[:, t * size : (t + 1) * size].astype(BF16)
                at += size
        deals += deal(side, side_out, side_send.at[j], side_recv.at[j])
        keep = pltpu.make_async_copy(side.at[me], side_out.at[me], own.at[3 + j])
        keep.start()
        keeps.append(keep)
    for copy in rounds[1]:
        copy.start()
    hands = []
    for k in range(count - 1):
        for i, block in enumerate(blocks):
            take(k, i, block)
            if k < count - 2:
                give(k + 1, i, block)
        if k < 2:
            target = (one_out_ref, two_out_ref)[k]
            for i, copy in enumerate(rounds[k][:-1]):
                copy.wait_recv()
                at = lax.rem(d + rows - (i + 1), rows) * 2 + c
                hand = remote(
                    target.at[at], target.at[at], pair_send.at[k, i + 1], pair_recv.at[k, i + 1], pair
                )
                hand.start()
                hands.append(hand)
    for copy in keeps:
        copy.wait()
    for copy in dealt:
        copy.wait_send()
    for copies in rounds:
        for copy in copies[:-1]:
            copy.wait_send()
        copies[-1].wait()
    for copy in hands + deals:
        copy.wait()
    for k in range(count - 1):
        for i, block in enumerate(blocks):
            given(k, i, block)


def turn_kernel(rows, backward, x_ref, gain_ref, base_ref, *refs):
    if backward:
        middle_ref, extra_ref, out_ref, all_ref, sums_ref, paired_ref = refs[:6]
        *scratch, extra, extra_load, extra_send, extra_recv = refs[6:]
    else:
        out_ref, all_ref = refs[:2]
        scratch = refs[2:]
    (
        mine,
        theirs,
        stage,
        land,
        low,
        load,
        fold_pair_send,
        fold_pair_recv,
        fold_send,
        fold_recv,
        own,
        send,
        recv,
        pair_send,
        pair_recv,
    ) = scratch
    d, z, c = place()
    me = d * 2 + c
    pair = (d, z, 1 - c)
    others = [(lax.rem(d + k, rows), z, c) for k in range(1, rows)]
    greet(others + [pair])
    order = [lax.rem(d + k, rows) for k in range(1, rows)] + [d]
    step = x_ref.shape[1] // CHUNKS
    parts = [pl.ds(j * step, step) for j in range(CHUNKS)]
    hands, loads = {}, {}
    for j, part in enumerate(parts):
        for i, to in enumerate(order):
            hands[j, i] = remote(
                x_ref.at[to * 2 + (1 - c), part],
                theirs.at[i, part],
                fold_pair_send.at[j, i],
                fold_pair_recv.at[j, i],
                pair,
            )
            hands[j, i].start()
            loads[j, i] = pltpu.make_async_copy(
                x_ref.at[to * 2 + c, part], mine.at[i, part], load.at[j, i]
            )
            loads[j, i].start()
    folds, extras = {}, []
    if backward:
        for i, to in enumerate(order):
            extras.append(
                (
                    remote(
                        extra_ref.at[to * 2 + (1 - c)],
                        extra.at[i],
                        extra_send.at[i],
                        extra_recv.at[i],
                        pair,
                    ),
                    pltpu.make_async_copy(
                        extra_ref.at[to * 2 + c], paired_ref.at[i], extra_load.at[i]
                    ),
                )
            )
    for j, part in enumerate(parts):
        for i in range(rows):
            loads[j, i].wait()
            hands[j, i].wait_recv()
            if i < rows - 1:
                stage[i, part] = (mine[i, part] + theirs[i, part]).astype(BF16)
                folds[j, i] = remote(
                    stage.at[i, part],
                    land.at[i, part],
                    fold_send.at[j, i],
                    fold_recv.at[j, i],
                    others[i],
                )
                folds[j, i].start()
    for pieces in extras:
        for copy in pieces:
            copy.start()
    gain = gain_ref[...]
    sends, keeps = {}, []
    if backward:
        sums_ref[...] = jnp.zeros_like(sums_ref)
    for j, part in enumerate(parts):
        total = mine[rows - 1, part] + theirs[rows - 1, part]
        for i in range(rows - 1):
            folds[j, i].wait_recv()
            total = total + land[i, part].astype(F32)
        if backward:
            middle = middle_ref[part, :]
            scale = lax.rsqrt(jnp.mean(middle * middle, axis=-1, keepdims=True) + EPSILON)
            normed = middle * scale
            sums_ref[...] += jnp.sum(total * normed, axis=0, keepdims=True)
            inner = total * gain
            result = base_ref[part, :].astype(F32) + scale * (
                inner - normed * jnp.mean(inner * normed, axis=-1, keepdims=True)
            )
            out_ref[part, :] = result
            low[part, :] = result.astype(BF16)
        else:
            result = base_ref[part, :].astype(F32) + total
            out_ref[part, :] = result
            low[part, :] = (rms_scale(result) * gain).astype(BF16)
        for i, peer in enumerate(others + [pair]):
            at = (send.at[j, i], recv.at[j, i])
            if i == rows - 1:
                at = (pair_send.at[j, rows - 1], pair_recv.at[j, rows - 1])
            sends[j, i] = remote(low.at[part], all_ref.at[me, part], *at, peer)
            sends[j, i].start()
        keep = pltpu.make_async_copy(low.at[part], all_ref.at[me, part], own.at[j])
        keep.start()
        keeps.append(keep)
    for i, (hand, copy) in enumerate(extras):
        copy.wait()
        hand.wait_recv()
        paired_ref[i] = (paired_ref[i].astype(F32) + extra[i].astype(F32)).astype(BF16)
    for hand, _ in extras:
        hand.wait_send()
    for j, part in enumerate(parts):
        for i in range(rows - 1):
            sends[j, i].wait_recv()
            at = lax.rem(d + rows - (i + 1), rows) * 2 + c
            hand = remote(
                all_ref.at[at, part],
                all_ref.at[at, part],
                pair_send.at[j, i],
                pair_recv.at[j, i],
                pair,
            )
            hand.start()
            hands[j, rows + i] = hand
    for keep in keeps:
        keep.wait()
    for (j, i), hand in hands.items():
        hand.wait_send()
        if i >= rows:
            hand.wait_recv()
    for copy in folds.values():
        copy.wait_send()
    for (j, i), copy in sends.items():
        copy.wait_send()
        if i == rows - 1:
            copy.wait_recv()


def greet_plane_and_line(rows, count):
    d, z, c = place()
    spot, before, after = neighbours(count)
    offsets = plane_offsets(rows)
    lower, upper = (c == 0) & (z > 0), (c == 1) & (z < count - 1)
    barrier = pltpu.get_barrier_semaphore()
    for offset in offsets:
        pl.semaphore_signal(
            barrier, inc=1, device_id=plane_peer(offset, rows), device_id_type=BY_MESH
        )

    @pl.when(lower)
    def _():
        pl.semaphore_signal(barrier, inc=1, device_id=before, device_id_type=BY_MESH)

    @pl.when(upper)
    def _():
        pl.semaphore_signal(barrier, inc=1, device_id=after, device_id_type=BY_MESH)

    pl.semaphore_wait(
        barrier, len(offsets) + lower.astype(jnp.int32) + upper.astype(jnp.int32)
    )


def swap_on_kernel(rows, count, x_ref, o_ref, rim_ref, land, own, send, recv, rim_send, rim_recv):
    d, z, c = place()
    me = d * 2 + c
    spot, before, after = neighbours(count)
    greet_plane_and_line(rows, count)
    copies = []
    for i, offset in enumerate(plane_offsets(rows)):
        peer = plane_peer(offset, rows)
        copy = remote(
            x_ref.at[peer[0] * 2 + peer[2]], o_ref.at[me], send.at[i], recv.at[i], peer
        )
        copy.start()
        copies.append(copy)
    keep = pltpu.make_async_copy(x_ref.at[me], o_ref.at[me], own)
    keep.start()
    keep.wait()
    for copy in copies:
        copy.wait_recv()
    size = x_ref.shape[1]
    rim = remote(o_ref.at[:, pl.ds(size - RIM, RIM)], land, rim_send, rim_recv, after)
    gives, takes = spot < 2 * count - 1, spot > 0

    @pl.when(gives)
    def _():
        rim.start()

    @pl.when(takes)
    def _():
        rim.wait_recv()

    @pl.when(jnp.logical_not(takes))
    def _():
        land[...] = jnp.zeros_like(land)

    rim_ref[...] = land[...]
    for copy in copies:
        copy.wait_send()

    @pl.when(gives)
    def _():
        rim.wait_send()


def swap_back_kernel(
    rows,
    count,
    x_ref,
    tail_ref,
    rim_ref,
    small_ref,
    o_ref,
    land,
    fixed,
    own,
    send,
    recv,
    rim_send,
    rim_recv,
):
    d, z, c = place()
    me = d * 2 + c
    spot, before, after = neighbours(count)
    greet_plane_and_line(rows, count)
    size, part = x_ref.shape[1:]
    wide = o_ref.shape[2]
    rim = remote(rim_ref, land, rim_send, rim_recv, before)
    gives, takes = spot > 0, spot < 2 * count - 1

    @pl.when(gives)
    def _():
        rim.start()

    body, end = pl.ds(0, size - RIM), pl.ds(size - RIM, RIM)
    left, right = pl.ds(0, part), pl.ds(part, wide - part)
    copies = []
    for i, offset in enumerate(plane_offsets(rows)):
        peer = plane_peer(offset, rows)
        to = peer[0] * 2 + peer[2]
        copies.append(
            (
                remote(
                    x_ref.at[to, body], o_ref.at[me, body, left], send.at[0, i], recv.at[0, i], peer
                ),
                remote(small_ref, o_ref.at[me, :, right], send.at[1, i], recv.at[1, i], peer),
                remote(fixed.at[to], o_ref.at[me, end, left], send.at[2, i], recv.at[2, i], peer),
            )
        )
        copies[-1][0].start()
        copies[-1][1].start()
    keeps = [
        pltpu.make_async_copy(x_ref.at[me, body], o_ref.at[me, body, left], own.at[0]),
        pltpu.make_async_copy(small_ref, o_ref.at[me, :, right], own.at[1]),
        pltpu.make_async_copy(fixed.at[me], o_ref.at[me, end, left], own.at[2]),
    ]
    keeps[0].start()
    keeps[1].start()

    @pl.when(takes)
    def _():
        rim.wait_recv()

    @pl.when(jnp.logical_not(takes))
    def _():
        land[...] = jnp.zeros_like(land)

    fixed[...] = (tail_ref[...] + land[...].astype(F32)).astype(BF16)
    keeps[2].start()
    for group in copies:
        group[2].start()
    for keep in keeps:
        keep.wait()
    for group in copies:
        for copy in group:
            copy.wait()

    @pl.when(gives)
    def _():
        rim.wait_send()


def column_kernel(count, x_ref, o_ref, own, send, recv):
    d, z, c = place()
    others = [(d, lax.rem(z + k, count), c) for k in range(1, count)]
    greet(others)
    copies = []
    for i, peer in enumerate(others):
        copy = remote(x_ref, o_ref.at[z], send.at[i], recv.at[i], peer)
        copy.start()
        copies.append(copy)
    keep = pltpu.make_async_copy(x_ref, o_ref.at[z], own)
    keep.start()
    keep.wait()
    for copy in copies:
        copy.wait()


def neighbours(count):
    d, z, c = place()
    after = (d, lax.rem(z + c, count), 1 - c)
    before = (d, lax.rem(z + c - 1 + count, count), 1 - c)
    spot = z * 2 + c
    return spot, before, after


def greet_chain(count):
    spot, before, after = neighbours(count)
    barrier = pltpu.get_barrier_semaphore()

    @pl.when(spot > 0)
    def _():
        pl.semaphore_signal(barrier, inc=1, device_id=before, device_id_type=BY_MESH)

    @pl.when(spot < 2 * count - 1)
    def _():
        pl.semaphore_signal(barrier, inc=1, device_id=after, device_id_type=BY_MESH)

    pl.semaphore_wait(
        barrier,
        (spot > 0).astype(jnp.int32) + (spot < 2 * count - 1).astype(jnp.int32),
    )


def hop_kernel(count, forward, x_ref, o_ref, send, recv):
    spot, before, after = neighbours(count)
    greet_chain(count)
    if forward:
        gives, takes, to = spot < 2 * count - 1, spot > 0, after
    else:
        gives, takes, to = spot > 0, spot < 2 * count - 1, before
    copy = remote(x_ref, o_ref, send, recv, to)

    @pl.when(gives)
    def _():
        copy.start()

    @pl.when(takes)
    def _():
        copy.wait_recv()

    @pl.when(jnp.logical_not(takes))
    def _():
        o_ref[...] = jnp.zeros_like(o_ref)

    @pl.when(gives)
    def _():
        copy.wait_send()


def chain_kernel(
    count,
    rows,
    heads,
    sides,
    forward,
    high_ref,
    low_ref,
    add_ref,
    *refs,
):
    side_refs, (o_ref, *side_out_refs) = refs[:sides], refs[sides : 2 * sides + 1]
    land, stage, send, recv, own, side_send, side_recv = refs[2 * sides + 1 :]
    d, z, c = place()
    me = d * 2 + c
    spot, before, after = neighbours(count)
    offsets = plane_offsets(rows)
    barrier = pltpu.get_barrier_semaphore()
    for offset in offsets:
        pl.semaphore_signal(
            barrier, inc=1, device_id=plane_peer(offset, rows), device_id_type=BY_MESH
        )

    @pl.when((c == 0) & (z > 0))
    def _():
        pl.semaphore_signal(barrier, inc=1, device_id=before, device_id_type=BY_MESH)

    @pl.when((c == 1) & (z < count - 1))
    def _():
        pl.semaphore_signal(barrier, inc=1, device_id=after, device_id_type=BY_MESH)

    pl.semaphore_wait(
        barrier,
        len(offsets)
        + ((c == 0) & (z > 0)).astype(jnp.int32)
        + ((c == 1) & (z < count - 1)).astype(jnp.int32),
    )
    waits = []
    for j in range(sides):
        if side_refs[j].shape[0] == rows:
            for i in range(rows - 1):
                waits.append(
                    remote(
                        side_refs[j].at[i],
                        side_out_refs[j].at[i],
                        side_send.at[j, i],
                        side_recv.at[j, i],
                        (lax.rem(d + i + 1, rows), z, c),
                    )
                )
            waits.append(
                pltpu.make_async_copy(
                    side_refs[j].at[rows - 1], side_out_refs[j].at[rows - 1], own.at[j]
                )
            )
            continue
        for i, offset in enumerate(offsets):
            peer = plane_peer(offset, rows)
            waits.append(
                remote(
                    side_refs[j].at[peer[0] * 2 + peer[2]],
                    side_out_refs[j].at[me],
                    side_send.at[j, i],
                    side_recv.at[j, i],
                    peer,
                )
            )
        waits.append(
            pltpu.make_async_copy(side_refs[j].at[me], side_out_refs[j].at[me], own.at[j])
        )
    for copy in waits:
        copy.start()
    if forward:
        gives, takes, to = spot < 2 * count - 1, spot > 0, after
    else:
        gives, takes, to = spot > 0, spot < 2 * count - 1, before
    part = o_ref.shape[2] // PIECES
    copies = [
        remote(stage.at[i], land.at[i], send.at[i], recv.at[i], to)
        for i in range(heads * PIECES)
    ]
    for h in range(heads):
        for j in range(PIECES):
            i = h * PIECES + j
            columns = slice(j * part, (j + 1) * part)

            @pl.when(jnp.logical_not(takes))
            def _():
                land[i] = jnp.zeros_like(land[i])

            @pl.when(takes)
            def _():
                copies[i].wait_recv()

            @pl.when(gives)
            def _():
                state = land[i]
                leaving = add_ref[h, :, columns] + mm(high_ref[h], state) + mm(low_ref[h], state)
                stage[i] = leaving.astype(BF16)
                copies[i].start()

    for copy in copies:

        @pl.when(gives)
        def _():
            copy.wait_send()

    for h in range(heads):
        for j in range(PIECES):
            o_ref[h, :, j * part : (j + 1) * part] = land[h * PIECES + j]
    for copy in waits:
        copy.wait()


ANY = pl.BlockSpec(memory_space=pl.ANY)
IN_VMEM = pl.BlockSpec(memory_space=pltpu.VMEM)
IN_HBM = pl.BlockSpec(memory_space=pltpu.HBM)


def dma(*shape):
    return pltpu.SemaphoreType.DMA(shape)


def comm_call(body, out, scratch, ident, operands, spec=ANY, cost=30):
    return pl.pallas_call(
        body,
        out_shape=out,
        in_specs=[spec] * len(operands),
        out_specs=spec,
        scratch_shapes=scratch,
        compiler_params=pltpu.CompilerParams(collective_id=ident, has_side_effects=True),
        cost_estimate=pl.CostEstimate(
            flops=0, bytes_accessed=int(cost * 3.0e6), transcendentals=0
        ),
    )(*operands)


def swap(x, ident):
    rows = lax.axis_size("dp")
    links = 2 * rows - 1
    return comm_call(
        partial(swap_kernel, rows),
        jax.ShapeDtypeStruct(x.shape, x.dtype),
        [pltpu.SemaphoreType.DMA, dma(links), dma(links)],
        ident,
        (x,),
    )


def spread(x, ident):
    rows = lax.axis_size("dp")
    return comm_call(
        partial(spread_kernel, rows),
        jax.ShapeDtypeStruct((2 * rows,) + x.shape, x.dtype),
        [pltpu.SemaphoreType.DMA, dma(rows - 1), dma(rows - 1), dma(rows), dma(rows)],
        ident,
        (x,),
    )


def fold(x, ident):
    rows = lax.axis_size("dp")
    part = (rows,) + x.shape[1:]
    received = comm_call(
        partial(fold_kernel, rows),
        jax.ShapeDtypeStruct(part, x.dtype),
        [
            pltpu.VMEM(part, x.dtype),
            pltpu.VMEM(part, x.dtype),
            dma(rows),
            dma(rows),
            dma(rows),
            dma(rows - 1),
            dma(rows - 1),
            pltpu.SemaphoreType.DMA,
        ],
        ident,
        (x,),
    )
    return jnp.sum(received.astype(F32), axis=0)


def turn(x, gain, base, more, ident):
    rows = lax.axis_size("dp")
    group, length, width = x.shape
    backward = bool(more)
    part, sent = (rows, length, width), (rows - 1, length, width)
    return pl.pallas_call(
        partial(turn_kernel, rows, backward),
        out_shape=[
            jax.ShapeDtypeStruct((length, width), F32),
            jax.ShapeDtypeStruct((group, length, width), BF16),
        ]
        + (
            [jax.ShapeDtypeStruct((1, width), F32), jax.ShapeDtypeStruct(part, BF16)]
            if backward
            else []
        ),
        in_specs=[ANY, IN_VMEM, IN_VMEM] + ([IN_VMEM, ANY] if backward else []),
        out_specs=[IN_VMEM, ANY] + ([IN_VMEM, IN_VMEM] if backward else []),
        scratch_shapes=[
            pltpu.VMEM(part, F32),
            pltpu.VMEM(part, F32),
            pltpu.VMEM(sent, BF16),
            pltpu.VMEM(sent, BF16),
            pltpu.VMEM((length, width), BF16),
        ]
        + [dma(CHUNKS, rows)] * 3
        + [dma(CHUNKS, rows - 1)] * 2
        + [dma(CHUNKS)]
        + [dma(CHUNKS, rows - 1)] * 2
        + [dma(CHUNKS, rows)] * 2
        + ([pltpu.VMEM(part, BF16)] + [dma(rows)] * 3 if backward else []),
        compiler_params=pltpu.CompilerParams(collective_id=ident, has_side_effects=True),
        cost_estimate=pl.CostEstimate(
            flops=0, bytes_accessed=150_000_000, transcendentals=0
        ),
    )(x, gain, base, *more)


def swap_on(x, ident):
    rows, count = lax.axis_size("dp"), lax.axis_size("zq")
    group, length, part = x.shape
    links = 2 * rows - 1
    return pl.pallas_call(
        partial(swap_on_kernel, rows, count),
        out_shape=[
            jax.ShapeDtypeStruct(x.shape, x.dtype),
            jax.ShapeDtypeStruct((group, RIM, part), x.dtype),
        ],
        in_specs=[ANY],
        out_specs=[ANY, IN_VMEM],
        scratch_shapes=[
            pltpu.VMEM((group, RIM, part), x.dtype),
            pltpu.SemaphoreType.DMA,
            dma(links),
            dma(links),
            pltpu.SemaphoreType.DMA,
            pltpu.SemaphoreType.DMA,
        ],
        compiler_params=pltpu.CompilerParams(collective_id=ident, has_side_effects=True),
        cost_estimate=pl.CostEstimate(flops=0, bytes_accessed=90_000_000, transcendentals=0),
    )(x)


def swap_back(x, tail, rim, small, ident):
    rows, count = lax.axis_size("dp"), lax.axis_size("zq")
    group, length, part = x.shape
    links = 2 * rows - 1
    return pl.pallas_call(
        partial(swap_back_kernel, rows, count),
        out_shape=jax.ShapeDtypeStruct((group, length, part + small.shape[1]), x.dtype),
        in_specs=[ANY, IN_VMEM, ANY, ANY],
        out_specs=ANY,
        scratch_shapes=[
            pltpu.VMEM((group, RIM, part), x.dtype),
            pltpu.VMEM((group, RIM, part), x.dtype),
            dma(3),
            dma(3, links),
            dma(3, links),
            pltpu.SemaphoreType.DMA,
            pltpu.SemaphoreType.DMA,
        ],
        compiler_params=pltpu.CompilerParams(collective_id=ident, has_side_effects=True),
        cost_estimate=pl.CostEstimate(flops=0, bytes_accessed=90_000_000, transcendentals=0),
    )(x, tail, rim, small)


def begin(hidden, grad, gain, decay, beta, weights, ident):
    rows, count = lax.axis_size("dp"), lax.axis_size("zq")
    group, links = 2 * rows, 2 * rows - 1
    owned = decay.shape[0]
    parts = [weight.shape[1] // group for weight in weights]
    wide = sum(parts[:4]) + LANES
    cut = (group, owned, wide)
    side_shapes = [(group, owned, sum(parts[4:6])), (group, owned, sum(parts[6:]))]
    assert count > 2
    tokens = jax.ShapeDtypeStruct(hidden.shape, BF16)
    everyone = jax.ShapeDtypeStruct((group,) + hidden.shape, BF16)
    return pl.pallas_call(
        partial(start_kernel, rows, count),
        out_shape=[jax.ShapeDtypeStruct((count,) + cut, BF16)]
        + [jax.ShapeDtypeStruct(shape, BF16) for shape in side_shapes]
        + [everyone] * 2
        + [tokens] * 3,
        in_specs=[IN_VMEM] * 5 + [IN_HBM] * 8,
        out_specs=[ANY] * 5 + [IN_VMEM] * 3,
        scratch_shapes=[pltpu.VMEM(weight.shape, F32) for weight in weights]
        + [pltpu.VMEM(cut, BF16)]
        + [pltpu.VMEM(shape, BF16) for shape in side_shapes]
        + [
            dma(8),
            dma(5),
            dma(links),
            dma(links),
            dma(2, links),
            dma(2, links),
            dma(2, rows - 1),
            dma(2, rows - 1),
            dma(2, rows),
            dma(2, rows),
        ]
        + [dma(count - 1, group)] * 4,
        compiler_params=pltpu.CompilerParams(
            collective_id=ident, has_side_effects=True, vmem_limit_bytes=40 << 20
        ),
        cost_estimate=pl.CostEstimate(
            flops=0, bytes_accessed=300_000_000, transcendentals=0
        ),
    )(hidden, grad, gain, decay, beta, *weights)


def column(x, ident):
    count = lax.axis_size("zq")
    return comm_call(
        partial(column_kernel, count),
        jax.ShapeDtypeStruct((count,) + x.shape, x.dtype),
        [pltpu.SemaphoreType.DMA, dma(count - 1), dma(count - 1)],
        ident,
        (x,),
    )


def hop(x, forward, ident):
    count = lax.axis_size("zq")
    return comm_call(
        partial(hop_kernel, count, forward),
        jax.ShapeDtypeStruct(x.shape, x.dtype),
        [pltpu.SemaphoreType.DMA, pltpu.SemaphoreType.DMA],
        ident,
        (x,),
        IN_VMEM,
    )


def chain(high, low, add, sides, forward, ident):
    rows, count = lax.axis_size("dp"), lax.axis_size("zq")
    heads, key_size, value_size = add.shape
    links = 2 * rows - 1
    pieces = (heads * PIECES, key_size, value_size // PIECES)
    return pl.pallas_call(
        partial(chain_kernel, count, rows, heads, len(sides), forward),
        out_shape=[jax.ShapeDtypeStruct(add.shape, BF16)]
        + [jax.ShapeDtypeStruct(side.shape, side.dtype) for side in sides],
        in_specs=[IN_VMEM] * 3 + [ANY] * len(sides),
        out_specs=[IN_VMEM] + [ANY] * len(sides),
        scratch_shapes=[
            pltpu.VMEM(pieces, BF16),
            pltpu.VMEM(pieces, BF16),
            dma(heads * PIECES),
            dma(heads * PIECES),
            dma(len(sides)),
            dma(len(sides), links),
            dma(len(sides), links),
        ],
        compiler_params=pltpu.CompilerParams(collective_id=ident, has_side_effects=True),
        cost_estimate=pl.CostEstimate(
            flops=0, bytes_accessed=200_000_000, transcendentals=0
        ),
    )(high, low, add, *sides)


def unit_lower_inverse(low):
    size = low.shape[0]
    row = lax.broadcasted_iota(jnp.int32, low.shape, 0)
    col = lax.broadcasted_iota(jnp.int32, low.shape, 1)

    def same(width):
        shift = width.bit_length() - 1
        return (row >> shift) == (col >> shift)

    eye = (row == col).astype(F32)
    width = 8
    near = jnp.where(same(width), low, 0.0)
    square = exact(near, near)
    inverse = eye - near
    inverse = inverse + exact(inverse, square)
    square = exact(square, square)
    inverse = inverse + exact(inverse, square)
    while width < size:
        cross = jnp.where(same(2 * width) & jnp.logical_not(same(width)), low, 0.0)
        inverse = inverse - exact(inverse, exact(cross, inverse))
        width *= 2
    return inverse


def unit_parts(values):
    scale = lax.rsqrt(jnp.sum(values * values, axis=-1, keepdims=True) + EPSILON)
    return values * scale, scale


def unit_back(unit, scale, grad):
    return scale * (grad - unit * jnp.sum(unit * grad, axis=-1, keepdims=True))


def strict_lower(size):
    row = lax.broadcasted_iota(jnp.int32, (size, size), 0)
    col = lax.broadcasted_iota(jnp.int32, (size, size), 1)
    return (row > col).astype(F32)


def convolve(x_ref, rim_ref, taps_ref, same_ref, ext):
    size = x_ref.shape[1]
    ext[:RIM] = rim_ref[0].astype(F32)
    ext[RIM:] = x_ref[0].astype(F32)
    mixed = taps_ref[0:1] * ext[RIM:]
    for lag in range(1, CONV):
        mixed = mixed + taps_ref[lag : lag + 1] * ext[RIM - lag : RIM - lag + size] * (
            same_ref[:, lag : lag + 1]
        )
    return mixed


def convolve_back(grad, taps_ref, same_ref, ext, back):
    size = grad.shape[0]
    back[:RIM] = jnp.zeros((RIM, grad.shape[1]), F32)
    back[RIM:] = taps_ref[0:1] * grad
    sums = [jnp.sum(grad * ext[RIM:], axis=0, keepdims=True)]
    for lag in range(1, CONV):
        kept = grad * same_ref[:, lag : lag + 1]
        sums.append(
            jnp.sum(kept * ext[RIM - lag : RIM - lag + size], axis=0, keepdims=True)
        )
        back[RIM - lag : RIM - lag + size] += taps_ref[lag : lag + 1] * kept
    return jnp.concatenate(sums, axis=0)


def silu_parts(values):
    sig = jax.nn.sigmoid(values)
    return values * sig, sig * (1.0 + values * (1.0 - sig))


def chunk_forward_kernel(
    *refs,
):
    pre_refs, rim_refs, tap_refs = refs[:4], refs[4:8], refs[8:12]
    same_ref, beta_ref, decay_ref, start_ref, tail_ref = refs[12:17]
    (
        inverse_ref,
        scores_ref,
        own_ref,
        effect_ref,
        offset_ref,
        high_ref,
        low_ref,
        back_high_ref,
        back_low_ref,
    ) = refs[17:26]
    ext = refs[26]
    active = []
    for i in range(4):
        mixed = convolve(pre_refs[i], rim_refs[i], tap_refs[i], same_ref, ext.at[i])
        active.append(silu_parts(mixed)[0])
    size, key_size = active[0].shape
    beta, start, tail = beta_ref[0], start_ref[0], tail_ref[0]
    decay = decay_ref[0]
    query = unit_parts(active[0])[0] * key_size ** (-0.5)
    key = unit_parts(active[1])[0]
    values = jnp.concatenate(active[2:], axis=1)
    inner = exact(key, key, (1, 1))
    inverse = unit_lower_inverse(beta * inner * (decay * strict_lower(size)))
    scores = exact(query, key, (1, 1)) * decay
    update = exact(inverse, beta * values)
    reach = exact(inverse, (beta * start) * key)
    inverse_ref[0] = inverse
    scores_ref[0] = scores
    own_ref[...] = exact(scores, update)
    effect_ref[0] = start * query - exact(scores, reach)
    last = tail * key
    offset_ref[0] = exact(last, update, (0, 0))
    row = lax.broadcasted_iota(jnp.int32, (key_size, key_size), 0)
    col = lax.broadcasted_iota(jnp.int32, (key_size, key_size), 1)
    transfer = jnp.where(row == col, start[size - 1 :, :], 0.0) - exact(last, reach, (0, 0))
    for matrix, top_ref, rest_ref in (
        (transfer, high_ref, low_ref),
        (transfer.T, back_high_ref, back_low_ref),
    ):
        top = matrix.astype(BF16)
        top_ref[0] = top
        rest_ref[0] = (matrix - top.astype(F32)).astype(BF16)


def gate_forward_kernel(own_ref, effect_ref, state_ref, gate_ref, gain_ref, mixed_ref, gated_ref):
    mixed = own_ref[...] + exact(effect_ref[0], state_ref[0].astype(F32))
    mixed_ref[...] = mixed
    gate = gate_ref[...].astype(F32)
    gated_ref[...] = (
        rms_scale(mixed) * gain_ref[...] * (gate * jax.nn.sigmoid(gate))
    ).astype(BF16)


def gate_backward_kernel(
    mixed_ref, gate_ref, gain_ref, grad_ref, effect_ref, out_ref, gate_grad_ref, gain_grad_ref, add_ref
):
    mixed = mixed_ref[...]
    gate = gate_ref[...].astype(F32)
    grad = grad_ref[...].astype(F32)
    gain = gain_ref[...]
    scale = lax.rsqrt(jnp.mean(mixed * mixed, axis=-1, keepdims=True) + EPSILON)
    normed = mixed * scale
    sig = jax.nn.sigmoid(gate)
    act = gate * sig
    gain_grad_ref[0] = jnp.sum(grad * normed * act, axis=0, keepdims=True)
    gate_grad_ref[...] = (
        grad * normed * gain * (sig * (1.0 + gate * (1.0 - sig)))
    ).astype(BF16)
    inner = grad * gain * act
    mixed_grad = scale * (inner - normed * jnp.mean(inner * normed, axis=-1, keepdims=True))
    out_ref[...] = mixed_grad
    add_ref[0] = exact(effect_ref[0], mixed_grad, (0, 0))


def chunk_backward_kernel(heads, *refs):
    pre_refs, rim_refs, tap_refs = refs[:4], refs[4:8], refs[8:12]
    same_ref, beta_ref, decay_ref, start_ref, tail_ref = refs[12:17]
    inverse_ref, scores_ref, state_ref, mixed_ref, ending_ref = refs[17:22]
    (
        grad_ref,
        grad_tail_ref,
        grad_rim_ref,
        taps_grad_ref,
        dbeta_ref,
        ddecay_ref,
        dstart_ref,
        dtail_ref,
    ) = refs[22:30]
    ext, back = refs[30:]
    active, slopes = [], []
    for i in range(4):
        mixed = convolve(pre_refs[i], rim_refs[i], tap_refs[i], same_ref, ext.at[i])
        value, slope = silu_parts(mixed)
        active.append(value)
        slopes.append(slope)
    size, key_size = active[0].shape
    values = jnp.concatenate(active[2:], axis=1)
    beta, start, tail = beta_ref[0], start_ref[0], tail_ref[0]
    decay, inverse, scores = decay_ref[0], inverse_ref[0], scores_ref[0]
    state = state_ref[0].astype(F32)
    ending = ending_ref[0].astype(F32)
    mixed_grad = mixed_ref[...]
    unit_q, scale_q = unit_parts(active[0])
    query = unit_q * key_size ** (-0.5)
    key, scale_k = unit_parts(active[1])
    below = strict_lower(size)
    inner = exact(key, key, (1, 1))
    raw = exact(query, key, (1, 1))
    recalled = exact(key, state)
    miss = values - start * recalled
    update = exact(inverse, beta * miss)
    mixed_state = exact(mixed_grad, state, (1, 1))
    last = tail * key
    dupdate = exact(scores, mixed_grad, (0, 0)) + exact(last, ending)
    dscores = exact(mixed_grad, update, (1, 1))
    dlast = exact(update, ending, (1, 1))
    dright = exact(inverse, dupdate, (0, 0))
    dlower = -exact(dright, update, (1, 1)) * below
    dscaled = dscores * decay
    dquery = start * mixed_state + exact(dscaled, key)
    dinner = beta * dlower * decay
    dkey = (
        tail * dlast
        + exact(dscaled, query, (0, 0))
        - exact((beta * start) * dright, state, (1, 1))
        + exact(dinner, key)
        + exact(dinner, key, (0, 0))
    )
    right_recalled = jnp.sum(dright * recalled, axis=-1, keepdims=True)
    dbeta_ref[0] = jnp.sum(dright * miss, axis=-1, keepdims=True) + jnp.sum(
        dlower * inner * decay, axis=-1, keepdims=True
    )
    final = jnp.sum(jnp.sum(ending * state, axis=-1, keepdims=True), axis=0, keepdims=True)
    row = lax.broadcasted_iota(jnp.int32, (size, 1), 0)
    dstart_ref[0] = (
        jnp.sum(query * mixed_state, axis=-1, keepdims=True)
        - beta * right_recalled
        + jnp.where(row == size - 1, final, 0.0)
    )
    dtail_ref[0] = jnp.sum(key * dlast, axis=-1, keepdims=True)
    ddecay_ref[0] = dscores * raw + beta * dlower * inner
    dvalues = beta * dright
    grads = [
        unit_back(unit_q, scale_q, dquery * key_size ** (-0.5)),
        unit_back(key, scale_k, dkey),
        dvalues[:, :key_size],
        dvalues[:, key_size:],
    ]
    head = pl.program_id(0)
    per = grad_ref.shape[2] // key_size
    for i, block in enumerate((head, heads + head, 2 * heads + 2 * head, 2 * heads + 2 * head + 1)):
        sums = convolve_back(grads[i] * slopes[i], tap_refs[i], same_ref, ext.at[i], back)
        slab = block // per
        columns = pl.ds(pl.multiple_of((block % per) * key_size, key_size), key_size)
        grad_ref[slab, :, columns] = back[RIM:].astype(BF16)
        grad_tail_ref[slab, :, columns] = back[size:]
        grad_rim_ref[slab, :, columns] = back[:RIM].astype(BF16)
        taps_grad_ref[slab, 0:CONV, columns] = sums


def by_head(*shape):
    return pl.BlockSpec((1,) + shape, lambda h: (h, 0, 0))


def by_columns(rows, width, offset=0):
    return pl.BlockSpec((rows, width), lambda h: (0, h + offset))


def head_call(body, heads, in_specs, out_specs, out_shape, operands, flops, scratch=()):
    return pl.pallas_call(
        body,
        scratch_shapes=scratch,
        grid=(heads,),
        in_specs=in_specs,
        out_specs=out_specs,
        out_shape=out_shape,
        cost_estimate=pl.CostEstimate(flops=flops, bytes_accessed=20_000_000, transcendentals=0),
    )(*operands)


def shaped(*shape, dtype=F32):
    return jax.ShapeDtypeStruct(shape, dtype)


def decays(segment, before, decay_pre, beta_pre, a_log):
    length = segment.shape[0]
    beta = jax.nn.sigmoid(beta_pre)
    decay_log = -jnp.exp(a_log) * jax.nn.softplus(decay_pre)
    order = jnp.arange(length)
    lower = order[:, None] >= order[None, :]
    running = exact(lower.astype(F32), decay_log).T
    live = (segment[:, None] == segment[None, :]) & lower
    gap = running[:, :, None] - running[:, None, :]
    decay = jnp.where(live, jnp.exp(jnp.where(live, gap, 0.0)), 0.0)
    start = jnp.exp(running) * (segment == before).astype(F32)
    live_last = segment == segment[-1]
    last_gap = running[:, -1:] - running
    tail = jnp.where(live_last, jnp.exp(jnp.where(live_last, last_gap, 0.0)), 0.0)
    return beta.T[:, :, None], decay, start[:, :, None], tail[:, :, None]


def local(
    hidden_in,
    segment_ids,
    grad_out,
    attn_gain,
    w_query,
    w_key,
    w_value,
    w_decay,
    w_beta,
    w_outgate,
    a_log,
    conv_query,
    conv_key,
    conv_value,
    out_gain,
    w_output,
    mlp_gain,
    w_gate,
    w_up,
    w_down,
):
    rows, count = lax.axis_size("dp"), lax.axis_size("zq")
    group = 2 * rows
    segment = segment_ids[0]
    length, width = hidden_in.shape[1:]
    heads = a_log.shape[0]
    key_width, value_width = w_query.shape[1], w_value.shape[1]
    key_size, value_size = key_width // heads, out_gain.shape[0]
    mixer_width = 2 * key_width + value_width
    hidden_width = w_gate.shape[1]
    owned = w_query.shape[0]
    margin = CONV - 1
    me = lax.axis_index("dp") * 2 + lax.axis_index("c")
    mixer_part = mixer_width // group
    back_width = value_width // group
    ffn_width = hidden_width // group

    def shuffled(values):
        return (
            values.reshape(-1, rows, count, 2 * owned).swapaxes(1, 2).reshape(-1, width)
        )

    def unshuffled(values):
        return (
            values.reshape(-1, count, rows, 2 * owned).swapaxes(1, 2).reshape(-1, width)
        )

    def cut(values):
        return values.astype(BF16).reshape(owned, group, -1).swapaxes(0, 1)

    def joined(values):
        return values.swapaxes(0, 1).reshape(values.shape[1], -1)

    def gathered(values):
        return lax.all_gather(values.reshape(group * owned, -1), "zq", axis=0, tiled=True)

    def scattered(values):
        return lax.psum_scatter(
            values, "zq", scatter_dimension=0, tiled=True
        ).reshape(group, owned, -1)

    def blocks(values):
        return values.astype(BF16).reshape(group, length, -1)

    (
        mixer_weights,
        first_own,
        gate_up_own,
        normed_all,
        grad_all,
        hidden_low,
        normed_low,
        grad_low,
    ) = begin(
        hidden_in[0],
        grad_out[0],
        attn_gain[None],
        w_decay,
        w_beta,
        (w_query, w_key, w_value, w_outgate, w_output, w_down, w_gate, w_up),
        0,
    )
    mixer_weights = mixer_weights.reshape(width, -1)
    normed_all = normed_all.reshape(-1, width)
    grad_all = grad_all.reshape(-1, width)
    project = mixer_weights[:, : mixer_part + back_width]
    small_weights = mixer_weights[:, mixer_part + back_width :]
    first_weights = gathered(first_own)
    output_weights, down = first_weights[:, :back_width], first_weights[:, back_width:]

    inputs = hidden_low.astype(F32)
    attn_row, mlp_row = shuffled(attn_gain[None]), shuffled(mlp_gain[None])
    normed, norm_pull = jax.vjp(rms_scale, inputs)
    pre_all = mm(normed_all, project[:, :mixer_part])
    gate_all = mm(normed_all, project[:, mixer_part:])
    pre, rim = swap_on(blocks(pre_all), 3)
    small_pre = mm(normed_low, small_weights)
    decay_pre, beta_pre = small_pre[:, :heads], small_pre[:, heads : 2 * heads]
    rim_ids = lax.ppermute(
        segment[-margin:],
        ("zq", "c"),
        [(i, i + 1) for i in range(2 * count - 1)],
    )
    seg_ext = jnp.concatenate([rim_ids, segment])
    same = jnp.stack(
        [
            (segment == seg_ext[margin - lag : margin - lag + length]).astype(F32)
            for lag in range(CONV)
        ],
        axis=1,
    )
    (beta, decay, start, tail), decay_pull = jax.vjp(
        partial(decays, segment, seg_ext[margin - 1]), decay_pre, beta_pre, a_log
    )
    slabs, slab = group, mixer_part
    if slab % key_size:
        slabs, slab = mixer_width // (3 * key_size), 3 * key_size
        pre, rim = [
            joined(part).reshape(-1, slabs, slab).swapaxes(0, 1) for part in (pre, rim)
        ]
    per = slab // key_size
    taps = jnp.concatenate([conv_query, conv_key, conv_value], axis=1)
    channel_blocks = [
        lambda h: h,
        lambda h: heads + h,
        lambda h: 2 * heads + 2 * h,
        lambda h: 2 * heads + 2 * h + 1,
    ]

    def slab_specs(lines):
        return [
            pl.BlockSpec((1, lines, key_size), lambda h, b=b: (b(h) // per, 0, b(h) % per))
            for b in channel_blocks
        ]

    token_specs = (
        slab_specs(length)
        + slab_specs(RIM)
        + [pl.BlockSpec((CONV, key_size), lambda h, b=b: (0, b(h))) for b in channel_blocks]
        + [pl.BlockSpec((length, CONV), lambda h: (0, 0))]
        + [by_head(length, 1), by_head(length, length), by_head(length, 1), by_head(length, 1)]
    )
    token_args = (pre,) * 4 + (rim,) * 4 + (taps,) * 4 + (same, beta, decay, start, tail)
    ext_shape = pltpu.VMEM((4, RIM + length, key_size), F32)
    values_spec = by_columns(length, value_size)
    state_spec = by_head(key_size, value_size)
    inverse, scores, own, effect, offset, high, low, back_high, back_low = head_call(
        chunk_forward_kernel,
        heads,
        token_specs,
        [
            by_head(length, length),
            by_head(length, length),
            values_spec,
            by_head(length, key_size),
            state_spec,
        ]
        + [by_head(key_size, key_size)] * 4,
        [
            shaped(heads, length, length),
            shaped(heads, length, length),
            shaped(length, value_width),
            shaped(heads, length, key_size),
            shaped(heads, key_size, value_size),
        ]
        + [shaped(heads, key_size, key_size, dtype=BF16)] * 4,
        token_args,
        6_000_000_000,
        [ext_shape],
    )
    state, gate_back = chain(high, low, offset, (gate_all.reshape(group, length, -1),), True, 5)
    gate_pre = joined(gate_back)
    gate_up_own, state, first_weights = lax.optimization_barrier(
        (gate_up_own, state, first_weights)
    )
    gate_up = gathered(gate_up_own)
    gain_spec = pl.BlockSpec((1, value_size), lambda h: (0, 0))
    gain_row = out_gain[None]
    mixed, gated = head_call(
        gate_forward_kernel,
        heads,
        [values_spec, by_head(length, key_size), state_spec, values_spec, gain_spec],
        [values_spec, values_spec],
        [shaped(length, value_width), shaped(length, value_width, dtype=BF16)],
        (own, effect, state, gate_pre, gain_row),
        1_000_000_000,
    )
    gated_cut = gated.reshape(length, group, back_width).swapaxes(0, 1)
    gated_all = swap(gated_cut, 6).reshape(-1, back_width)
    middle, normed_two_all = turn(
        mm(gated_all, output_weights, (1, 1)).reshape(group, length, width),
        mlp_row,
        inputs,
        (),
        4,
    )
    normed_two_all = normed_two_all.reshape(-1, width)

    both = mm(normed_two_all, gate_up)
    hidden, swiglu_pull = jax.vjp(swiglu, both[:, :ffn_width], both[:, ffn_width:])
    hidden_low = hidden.astype(BF16)
    grad_gate, grad_up = swiglu_pull(mm(grad_all, down))
    both_grad_low = jnp.concatenate([grad_gate, grad_up], axis=1).astype(BF16)
    grad_normed_two_parts = mm(both_grad_low, gate_up, (1, 1)).reshape(group, length, width)
    mlp_parts = blocks(mm(hidden_low, down, (1, 1)))
    gate_up_rows = mm(normed_two_all, both_grad_low, (0, 0)).astype(BF16)
    grad_normed_two_parts, gate_up_rows = lax.optimization_barrier(
        (grad_normed_two_parts, gate_up_rows)
    )
    gate_up_rows = scattered(gate_up_rows)
    grad_middle, attended_grad_all, grad_mlp_gain, mlp_pairs = turn(
        grad_normed_two_parts, mlp_row, grad_low, (middle, mlp_parts), 2
    )
    attended_grad_all = attended_grad_all.reshape(-1, width)

    grad_gated = joined(swap(blocks(mm(attended_grad_all, output_weights)), 6))
    output_rows = mm(attended_grad_all, gated_all, (0, 0)).astype(BF16)
    down_rows = mm(grad_all, hidden_low, (0, 0)).astype(BF16)
    mixed_grad, gate_pre_grad, gain_grad, state_add = head_call(
        gate_backward_kernel,
        heads,
        [values_spec, values_spec, gain_spec, values_spec, by_head(length, key_size)],
        [values_spec, values_spec, by_head(1, value_size), state_spec],
        [
            shaped(length, value_width),
            shaped(length, value_width, dtype=BF16),
            shaped(heads, 1, value_size),
            shaped(heads, key_size, value_size),
        ],
        (mixed, gate_pre, gain_row, grad_gated, effect),
        1_000_000_000,
    )
    grad_out_gain = jnp.sum(gain_grad, axis=(0, 1))
    side_rows = jnp.concatenate([down_rows, output_rows], axis=1)
    state_add, gate_up_rows, side_rows = lax.optimization_barrier(
        (state_add, gate_up_rows, side_rows)
    )
    ending, gate_grad_back, mlp_back = chain(
        back_high,
        back_low,
        state_add,
        (gate_pre_grad.reshape(length, group, back_width).swapaxes(0, 1), mlp_pairs),
        False,
        8,
    )
    gate_grad_all = gate_grad_back.reshape(-1, back_width)
    side_rows, ending = lax.optimization_barrier((side_rows, ending))
    side_rows = scattered(side_rows)
    gate_up_back = lax.all_to_all(gate_up_rows, ("dp", "c"), 0, 0, tiled=True)
    whole = lambda *shape: pl.BlockSpec(shape, lambda h: (0, 0, 0))
    grad_pre, grad_tail, grad_rim, grad_taps, dbeta, ddecay, dstart, dtail = head_call(
        partial(chunk_backward_kernel, heads),
        heads,
        token_specs
        + [
            by_head(length, length),
            by_head(length, length),
            state_spec,
            values_spec,
            state_spec,
        ],
        [
            whole(slabs, length, slab),
            whole(slabs, RIM, slab),
            whole(slabs, RIM, slab),
            whole(slabs, 2 * CONV, slab),
        ]
        + [by_head(length, 1), by_head(length, length), by_head(length, 1), by_head(length, 1)],
        [
            shaped(slabs, length, slab, dtype=BF16),
            shaped(slabs, RIM, slab),
            shaped(slabs, RIM, slab, dtype=BF16),
            shaped(slabs, 2 * CONV, slab),
            shaped(heads, length, 1),
            shaped(heads, length, length),
            shaped(heads, length, 1),
            shaped(heads, length, 1),
        ],
        token_args + (inverse, scores, state, mixed_grad, ending),
        12_000_000_000,
        [ext_shape, pltpu.VMEM((RIM + length, key_size), F32)],
    )
    grad_decay, grad_beta, grad_alog = decay_pull((dbeta, ddecay, dstart, dtail))
    grad_taps = joined(grad_taps)[:CONV]
    grad_conv_one = grad_taps[:, :key_width]
    grad_conv_two = grad_taps[:, key_width : 2 * key_width]
    grad_conv_three = grad_taps[:, 2 * key_width :]
    small_grad = jnp.concatenate([grad_decay, grad_beta], axis=1).astype(BF16)
    small_grad = jnp.pad(small_grad, ((0, 0), (0, LANES - 2 * heads)))
    if slabs != group:
        grad_pre, grad_tail, grad_rim = [
            joined(part).reshape(-1, group, mixer_part).swapaxes(0, 1)
            for part in (grad_pre, grad_tail, grad_rim)
        ]
    grad_pre, gate_up_back = lax.optimization_barrier((grad_pre, gate_up_back))
    grads_all = swap_back(grad_pre, grad_tail, grad_rim, small_grad, 10).reshape(
        group * length, -1
    )
    mixer_parts = jnp.concatenate(
        [
            mm(normed_all, grads_all, (0, 0)).astype(BF16),
            mm(normed_all, gate_grad_all, (0, 0)).astype(BF16),
        ],
        axis=1,
    )
    mixer_parts, side_rows = lax.optimization_barrier((mixer_parts, side_rows))
    mixer_rows = scattered(mixer_parts)
    combined = fold(
        blocks(
            mm(
                jnp.concatenate([grads_all[:, :mixer_part], gate_grad_all], axis=1),
                project,
                (1, 1),
            )
        ),
        7,
    )
    mlp_part = jnp.sum(mlp_back.astype(F32), axis=0)
    result = (middle + mlp_part).astype(BF16)
    combined = combined + mm(small_grad, small_weights, (1, 1))
    grad_attn_gain = jnp.sum(combined * normed, axis=0)
    grad_inputs = grad_middle + norm_pull(combined * attn_row)[0]

    side_back = lax.all_to_all(side_rows, ("dp", "c"), 0, 0, tiled=True).astype(F32)
    gate_grad = joined(gate_up_back[:, :, :ffn_width].astype(F32))
    up_grad = joined(gate_up_back[:, :, ffn_width:].astype(F32))
    down_grad = joined(side_back[:, :, :ffn_width])
    output_grad = joined(side_back[:, :, ffn_width:])

    pieces = (
        grad_attn_gain,
        grad_alog,
        grad_conv_one,
        grad_conv_two,
        grad_conv_three,
        grad_out_gain,
        grad_mlp_gain,
    )
    flat = jnp.concatenate([piece.reshape(-1) for piece in pieces])
    lines = -(-flat.shape[0] // (group * 8 * LANES)) * 8
    flat = jnp.pad(flat, (0, group * lines * LANES - flat.shape[0])).reshape(group, lines, LANES)
    flat = jnp.sum(swap(flat, 11), axis=0)
    flat = jnp.sum(column(flat, 12), axis=0)
    flat = spread(flat, 16).reshape(-1)
    mixer_rows, _ = lax.optimization_barrier((mixer_rows, (flat, grad_inputs)))
    mixer_swapped = swap(
        jnp.concatenate(
            [mixer_rows[:, :, :mixer_part], mixer_rows[:, :, mixer_part + LANES :]], axis=2
        ),
        15,
    ).astype(F32)
    mixer_back = joined(mixer_swapped[:, :, :mixer_part])
    outgate_grad = joined(mixer_swapped[:, :, mixer_part:])
    small_rows = lax.dynamic_index_in_dim(mixer_rows, me, 0, keepdims=False)
    small_rows = small_rows[:, mixer_part : mixer_part + LANES].astype(F32)
    summed, at = [], 0
    for piece in pieces:
        summed.append(flat[at : at + piece.size].reshape(piece.shape))
        at += piece.size

    return (
        unshuffled(result)[None],
        unshuffled(grad_inputs.astype(BF16))[None],
        unshuffled(summed[0][None])[0],
        mixer_back[:, :key_width],
        mixer_back[:, key_width : 2 * key_width],
        mixer_back[:, 2 * key_width :],
        small_rows[:, :heads],
        small_rows[:, heads : 2 * heads],
        outgate_grad,
        summed[1],
        summed[2],
        summed[3],
        summed[4],
        summed[5],
        output_grad,
        unshuffled(summed[6][None])[0],
        gate_grad,
        up_grad,
        down_grad,
    )


def solution(mesh):
    rows, places = mesh.shape["dp"], mesh.shape["seq"]
    fine = Mesh(mesh.devices.reshape(rows, places // 2, 2), ("dp", "zq", "c"))
    tokens = P("dp", ("zq", "c"), None)
    owned = P(("dp", "zq", "c"), None)
    return jax.shard_map(
        local,
        mesh=fine,
        in_specs=(tokens, P("dp", ("zq", "c")), tokens, P())
        + (owned,) * 6
        + (P(),) * 5
        + (owned, P(), owned, owned, owned),
        out_specs=(tokens, tokens, P())
        + (owned,) * 6
        + (P(),) * 5
        + (owned, P(), owned, owned, owned),
        check_vma=False,
    )
```

```python
from functools import partial

import jax
import jax.numpy as jnp
from jax import lax
from jax.experimental import pallas as pl
from jax.experimental.pallas import tpu as pltpu
from jax.sharding import Mesh
from jax.sharding import PartitionSpec as P

CONV = 4
EPSILON = 1e-06
EXACT = lax.Precision.HIGHEST
BF16 = jnp.bfloat16
F32 = jnp.float32
BY_MESH = pl.DeviceIdType.MESH
LANES = 128
PIECES = 2
CHUNKS = 2
RIM = 16


def rms_scale(values):
    return values * lax.rsqrt(jnp.mean(values * values, axis=-1, keepdims=True) + EPSILON)


def swiglu(gate_values, up_values):
    return jax.nn.silu(gate_values) * up_values


def mm(left, right, over=(1, 0)):
    return lax.dot_general(
        left, right, (((over[0],), (over[1],)), ((), ())), preferred_element_type=F32
    )


def exact(left, right, over=(1, 0)):
    return lax.dot_general(
        left,
        right,
        (((over[0],), (over[1],)), ((), ())),
        precision=EXACT,
        preferred_element_type=F32,
    )


def place():
    return lax.axis_index("dp"), lax.axis_index("zq"), lax.axis_index("c")


def greet(peers):
    barrier = pltpu.get_barrier_semaphore()
    for peer in peers:
        pl.semaphore_signal(barrier, inc=1, device_id=peer, device_id_type=BY_MESH)
    pl.semaphore_wait(barrier, len(peers))


def remote(source, target, send, recv, peer):
    return pltpu.make_async_remote_copy(
        src_ref=source,
        dst_ref=target,
        send_sem=send,
        recv_sem=recv,
        device_id=peer,
        device_id_type=BY_MESH,
    )


def plane_offsets(rows):
    return [(k, flip) for k in range(rows) for flip in (0, 1) if (k, flip) != (0, 0)]


def plane_peer(offset, rows):
    d, z, c = place()
    k, flip = offset
    return (lax.rem(d + k, rows), z, 1 - c if flip else c)


def swap_kernel(rows, x_ref, o_ref, own, send, recv):
    d, z, c = place()
    me = d * 2 + c
    offsets = plane_offsets(rows)
    greet([plane_peer(offset, rows) for offset in offsets])
    copies = []
    for i, offset in enumerate(offsets):
        peer = plane_peer(offset, rows)
        copy = remote(
            x_ref.at[peer[0] * 2 + peer[2]], o_ref.at[me], send.at[i], recv.at[i], peer
        )
        copy.start()
        copies.append(copy)
    keep = pltpu.make_async_copy(x_ref.at[me], o_ref.at[me], own)
    keep.start()
    keep.wait()
    for copy in copies:
        copy.wait()


def spread_kernel(rows, x_ref, o_ref, own, send, recv, pair_send, pair_recv):
    d, z, c = place()
    me = d * 2 + c
    pair = (d, z, 1 - c)
    others = [(lax.rem(d + k, rows), z, c) for k in range(1, rows)]
    greet(others + [pair])
    copies = []
    for i, peer in enumerate(others):
        copy = remote(x_ref, o_ref.at[me], send.at[i], recv.at[i], peer)
        copy.start()
        copies.append(copy)
    hand = remote(x_ref, o_ref.at[me], pair_send.at[0], pair_recv.at[0], pair)
    hand.start()
    keep = pltpu.make_async_copy(x_ref, o_ref.at[me], own)
    keep.start()
    hands = [hand]
    for i, copy in enumerate(copies):
        copy.wait_recv()
        origin = lax.rem(d + rows - (i + 1), rows) * 2 + c
        hand = remote(
            o_ref.at[origin], o_ref.at[origin], pair_send.at[i + 1], pair_recv.at[i + 1], pair
        )
        hand.start()
        hands.append(hand)
    keep.wait()
    for copy in copies:
        copy.wait_send()
    for hand in hands:
        hand.wait()


def fold_kernel(
    rows, x_ref, o_ref, mine, theirs, load, pair_send, pair_recv, send, recv, own
):
    d, z, c = place()
    pair = (d, z, 1 - c)
    others = [(lax.rem(d + k, rows), z, c) for k in range(1, rows)]
    greet(others + [pair])
    order = [lax.rem(d + k, rows) for k in range(1, rows)] + [d]
    hands, loads = [], []
    for i, to in enumerate(order):
        hand = remote(
            x_ref.at[to * 2 + (1 - c)], theirs.at[i], pair_send.at[i], pair_recv.at[i], pair
        )
        hand.start()
        hands.append(hand)
        copy = pltpu.make_async_copy(x_ref.at[to * 2 + c], mine.at[i], load.at[i])
        copy.start()
        loads.append(copy)
    copies = []
    for i in range(rows):
        loads[i].wait()
        hands[i].wait_recv()
        mine[i] = (mine[i].astype(F32) + theirs[i].astype(F32)).astype(BF16)
        if i < rows - 1:
            copy = remote(mine.at[i], o_ref.at[d], send.at[i], recv.at[i], others[i])
        else:
            copy = pltpu.make_async_copy(mine.at[i], o_ref.at[d], own)
        copy.start()
        copies.append(copy)
    for hand in hands:
        hand.wait_send()
    for copy in copies:
        copy.wait()


def slab_pieces(widths, slab, t):
    at, end, base = t * slab, (t + 1) * slab, 0
    for source, width in enumerate(widths):
        low, high = max(at, base), min(end, base + width)
        if low < high:
            yield source, low - base, low - at, high - low
        base += width


def start_kernel(rows, count, hidden_ref, grad_ref, gain_ref, decay_ref, beta_ref, *refs):
    weight_refs = refs[:8]
    all_ref, *side_outs = refs[8:11]
    one_out_ref, two_out_ref, hidden_out_ref, one_ref, two_ref = refs[11:16]
    raws, cut_ref, sides = refs[16:24], refs[24], refs[25:27]
    (
        load,
        own,
        deal_send,
        deal_recv,
        side_send,
        side_recv,
        round_send,
        round_recv,
        pair_send,
        pair_recv,
        up_send,
        up_recv,
        down_send,
        down_recv,
    ) = refs[27:]
    loads = [
        pltpu.make_async_copy(weight, raw, load.at[i])
        for i, (weight, raw) in enumerate(zip(weight_refs, raws))
    ]
    for copy in loads:
        copy.start()
    d, z, c = place()
    me = d * 2 + c
    group = 2 * rows
    pair = (d, z, 1 - c)
    others = [(lax.rem(d + k, rows), z, c) for k in range(1, rows)]
    above = (d, lax.rem(z + 1, count), c)
    below = (d, lax.rem(z + count - 1, count), c)
    has_above, has_below = z < count - 1, z > 0
    offsets = plane_offsets(rows)
    barrier = pltpu.get_barrier_semaphore()
    for offset in offsets:
        pl.semaphore_signal(
            barrier, inc=1, device_id=plane_peer(offset, rows), device_id_type=BY_MESH
        )

    @pl.when(has_above)
    def _():
        pl.semaphore_signal(barrier, inc=1, device_id=above, device_id_type=BY_MESH)

    @pl.when(has_below)
    def _():
        pl.semaphore_signal(barrier, inc=1, device_id=below, device_id_type=BY_MESH)

    owned = raws[0].shape[0]
    wide = cut_ref.shape[2]
    heads = decay_ref.shape[1]
    back = raws[3].shape[1] // group
    slab = wide - LANES - back
    for copy in loads[:4]:
        copy.wait()
    widths = [raw.shape[1] for raw in raws[:3]]
    for t in range(group):
        for source, at, to, size in slab_pieces(widths, slab, t):
            cut_ref[t, :, to : to + size] = raws[source][:, at : at + size].astype(BF16)
        cut_ref[t, :, slab : slab + back] = raws[3][:, t * back : (t + 1) * back].astype(BF16)
        cut_ref[t, :, slab + back :] = jnp.concatenate(
            [decay_ref[...], beta_ref[...], jnp.zeros((owned, LANES - 2 * heads), F32)], axis=1
        ).astype(BF16)
    pl.semaphore_wait(
        barrier, len(offsets) + has_above.astype(jnp.int32) + has_below.astype(jnp.int32)
    )

    def deal(source, target, send, recv):
        copies = []
        for i, offset in enumerate(offsets):
            peer = plane_peer(offset, rows)
            copy = remote(
                source.at[peer[0] * 2 + peer[2]], target.at[me], send.at[i], recv.at[i], peer
            )
            copy.start()
            copies.append(copy)
        return copies

    def origin(offset):
        k, flip = offset
        return lax.rem(d + rows - k, rows) * 2 + (1 - c if flip else c)

    def passed(k, i, block, upward):
        at = z - k if upward else z + k
        at = lax.rem(at + count, count)
        send, recv = (up_send, up_recv) if upward else (down_send, down_recv)
        return remote(
            all_ref.at[at, block],
            all_ref.at[at, block],
            send.at[k, i],
            recv.at[k, i],
            above if upward else below,
        )

    def give(k, i, block):
        @pl.when(has_above & (z - k >= 0))
        def _():
            passed(k, i, block, True).start()

        @pl.when(has_below & (z + k <= count - 1))
        def _():
            passed(k, i, block, False).start()

    def take(k, i, block):
        @pl.when(z - k - 1 >= 0)
        def _():
            passed(k, i, block, True).wait_recv()

        @pl.when(z + k + 1 <= count - 1)
        def _():
            passed(k, i, block, False).wait_recv()

    def given(k, i, block):
        @pl.when(has_above & (z - k >= 0))
        def _():
            passed(k, i, block, True).wait_send()

        @pl.when(has_below & (z + k <= count - 1))
        def _():
            passed(k, i, block, False).wait_send()

    dealt = deal(cut_ref, all_ref.at[z], deal_send, deal_recv)
    keep = pltpu.make_async_copy(cut_ref.at[me], all_ref.at[z, me], own.at[0])
    keep.start()
    keep.wait()
    blocks = [me] + [origin(offset) for offset in offsets]
    give(0, 0, me)
    run = 2 * owned
    width = hidden_ref.shape[1]

    def moved(values):
        return jnp.concatenate(
            [
                values[:, (b * count + a) * run : (b * count + a + 1) * run]
                for a in range(count)
                for b in range(rows)
            ],
            axis=1,
        )

    hidden = moved(hidden_ref[...])
    hidden_out_ref[...] = hidden
    one_ref[...] = (rms_scale(hidden.astype(F32)) * moved(gain_ref[...])).astype(BF16)
    two_ref[...] = moved(grad_ref[...])
    rounds = []
    for j, (source, target) in enumerate(((one_ref, one_out_ref), (two_ref, two_out_ref))):
        copies = []
        for i, peer in enumerate(others):
            copies.append(
                remote(source, target.at[me], round_send.at[j, i], round_recv.at[j, i], peer)
            )
        copies.append(
            remote(source, target.at[me], pair_send.at[j, 0], pair_recv.at[j, 0], pair)
        )
        rounds.append(copies)
    for i, copy in enumerate(dealt):
        copy.wait_recv()
        give(0, i + 1, blocks[i + 1])
    keeps = [
        pltpu.make_async_copy(one_ref, one_out_ref.at[me], own.at[1]),
        pltpu.make_async_copy(two_ref, two_out_ref.at[me], own.at[2]),
    ]
    for copy in rounds[0] + keeps:
        copy.start()
    for copy in loads[4:]:
        copy.wait()
    deals = []
    for j, (laid, side, side_out) in enumerate(zip((raws[4:6], raws[6:]), sides, side_outs)):
        for t in range(group):
            at = 0
            for raw in laid:
                size = raw.shape[1] // group
                side[t, :, at : at + size] = raw[:, t * size : (t + 1) * size].astype(BF16)
                at += size
        deals += deal(side, side_out, side_send.at[j], side_recv.at[j])
        keep = pltpu.make_async_copy(side.at[me], side_out.at[me], own.at[3 + j])
        keep.start()
        keeps.append(keep)
    for copy in rounds[1]:
        copy.start()
    hands = []
    for k in range(count - 1):
        for i, block in enumerate(blocks):
            take(k, i, block)
            if k < count - 2:
                give(k + 1, i, block)
        if k < 2:
            target = (one_out_ref, two_out_ref)[k]
            for i, copy in enumerate(rounds[k][:-1]):
                copy.wait_recv()
                at = lax.rem(d + rows - (i + 1), rows) * 2 + c
                hand = remote(
                    target.at[at], target.at[at], pair_send.at[k, i + 1], pair_recv.at[k, i + 1], pair
                )
                hand.start()
                hands.append(hand)
    for copy in keeps:
        copy.wait()
    for copy in dealt:
        copy.wait_send()
    for copies in rounds:
        for copy in copies[:-1]:
            copy.wait_send()
        copies[-1].wait()
    for copy in hands + deals:
        copy.wait()
    for k in range(count - 1):
        for i, block in enumerate(blocks):
            given(k, i, block)


def turn_kernel(rows, backward, x_ref, gain_ref, base_ref, *refs):
    if backward:
        middle_ref, extra_ref, out_ref, all_ref, sums_ref, paired_ref = refs[:6]
        *scratch, extra, extra_load, extra_send, extra_recv = refs[6:]
    else:
        out_ref, all_ref = refs[:2]
        scratch = refs[2:]
    (
        mine,
        theirs,
        stage,
        land,
        low,
        load,
        fold_pair_send,
        fold_pair_recv,
        fold_send,
        fold_recv,
        own,
        send,
        recv,
        pair_send,
        pair_recv,
    ) = scratch
    d, z, c = place()
    me = d * 2 + c
    pair = (d, z, 1 - c)
    others = [(lax.rem(d + k, rows), z, c) for k in range(1, rows)]
    greet(others + [pair])
    order = [lax.rem(d + k, rows) for k in range(1, rows)] + [d]
    step = x_ref.shape[1] // CHUNKS
    parts = [pl.ds(j * step, step) for j in range(CHUNKS)]
    hands, loads = {}, {}
    for j, part in enumerate(parts):
        for i, to in enumerate(order):
            hands[j, i] = remote(
                x_ref.at[to * 2 + (1 - c), part],
                theirs.at[i, part],
                fold_pair_send.at[j, i],
                fold_pair_recv.at[j, i],
                pair,
            )
            hands[j, i].start()
            loads[j, i] = pltpu.make_async_copy(
                x_ref.at[to * 2 + c, part], mine.at[i, part], load.at[j, i]
            )
            loads[j, i].start()
    folds, extras = {}, []
    if backward:
        for i, to in enumerate(order):
            extras.append(
                (
                    remote(
                        extra_ref.at[to * 2 + (1 - c)],
                        extra.at[i],
                        extra_send.at[i],
                        extra_recv.at[i],
                        pair,
                    ),
                    pltpu.make_async_copy(
                        extra_ref.at[to * 2 + c], paired_ref.at[i], extra_load.at[i]
                    ),
                )
            )
    for j, part in enumerate(parts):
        for i in range(rows):
            loads[j, i].wait()
            hands[j, i].wait_recv()
            if i < rows - 1:
                stage[i, part] = (mine[i, part] + theirs[i, part]).astype(BF16)
                folds[j, i] = remote(
                    stage.at[i, part],
                    land.at[i, part],
                    fold_send.at[j, i],
                    fold_recv.at[j, i],
                    others[i],
                )
                folds[j, i].start()
    for pieces in extras:
        for copy in pieces:
            copy.start()
    gain = gain_ref[...]
    sends, keeps = {}, []
    if backward:
        sums_ref[...] = jnp.zeros_like(sums_ref)
    for j, part in enumerate(parts):
        total = mine[rows - 1, part] + theirs[rows - 1, part]
        for i in range(rows - 1):
            folds[j, i].wait_recv()
            total = total + land[i, part].astype(F32)
        if backward:
            middle = middle_ref[part, :]
            scale = lax.rsqrt(jnp.mean(middle * middle, axis=-1, keepdims=True) + EPSILON)
            normed = middle * scale
            sums_ref[...] += jnp.sum(total * normed, axis=0, keepdims=True)
            inner = total * gain
            result = base_ref[part, :].astype(F32) + scale * (
                inner - normed * jnp.mean(inner * normed, axis=-1, keepdims=True)
            )
            out_ref[part, :] = result
            low[part, :] = result.astype(BF16)
        else:
            result = base_ref[part, :].astype(F32) + total
            out_ref[part, :] = result
            low[part, :] = (rms_scale(result) * gain).astype(BF16)
        for i, peer in enumerate(others + [pair]):
            at = (send.at[j, i], recv.at[j, i])
            if i == rows - 1:
                at = (pair_send.at[j, rows - 1], pair_recv.at[j, rows - 1])
            sends[j, i] = remote(low.at[part], all_ref.at[me, part], *at, peer)
            sends[j, i].start()
        keep = pltpu.make_async_copy(low.at[part], all_ref.at[me, part], own.at[j])
        keep.start()
        keeps.append(keep)
    for i, (hand, copy) in enumerate(extras):
        copy.wait()
        hand.wait_recv()
        paired_ref[i] = (paired_ref[i].astype(F32) + extra[i].astype(F32)).astype(BF16)
    for hand, _ in extras:
        hand.wait_send()
    for j, part in enumerate(parts):
        for i in range(rows - 1):
            sends[j, i].wait_recv()
            at = lax.rem(d + rows - (i + 1), rows) * 2 + c
            hand = remote(
                all_ref.at[at, part],
                all_ref.at[at, part],
                pair_send.at[j, i],
                pair_recv.at[j, i],
                pair,
            )
            hand.start()
            hands[j, rows + i] = hand
    for keep in keeps:
        keep.wait()
    for (j, i), hand in hands.items():
        hand.wait_send()
        if i >= rows:
            hand.wait_recv()
    for copy in folds.values():
        copy.wait_send()
    for (j, i), copy in sends.items():
        copy.wait_send()
        if i == rows - 1:
            copy.wait_recv()


def greet_plane_and_line(rows, count):
    d, z, c = place()
    spot, before, after = neighbours(count)
    offsets = plane_offsets(rows)
    lower, upper = (c == 0) & (z > 0), (c == 1) & (z < count - 1)
    barrier = pltpu.get_barrier_semaphore()
    for offset in offsets:
        pl.semaphore_signal(
            barrier, inc=1, device_id=plane_peer(offset, rows), device_id_type=BY_MESH
        )

    @pl.when(lower)
    def _():
        pl.semaphore_signal(barrier, inc=1, device_id=before, device_id_type=BY_MESH)

    @pl.when(upper)
    def _():
        pl.semaphore_signal(barrier, inc=1, device_id=after, device_id_type=BY_MESH)

    pl.semaphore_wait(
        barrier, len(offsets) + lower.astype(jnp.int32) + upper.astype(jnp.int32)
    )


def swap_on_kernel(rows, count, x_ref, o_ref, rim_ref, land, own, send, recv, rim_send, rim_recv):
    d, z, c = place()
    me = d * 2 + c
    spot, before, after = neighbours(count)
    greet_plane_and_line(rows, count)
    copies = []
    for i, offset in enumerate(plane_offsets(rows)):
        peer = plane_peer(offset, rows)
        copy = remote(
            x_ref.at[peer[0] * 2 + peer[2]], o_ref.at[me], send.at[i], recv.at[i], peer
        )
        copy.start()
        copies.append(copy)
    keep = pltpu.make_async_copy(x_ref.at[me], o_ref.at[me], own)
    keep.start()
    keep.wait()
    for copy in copies:
        copy.wait_recv()
    size = x_ref.shape[1]
    rim = remote(o_ref.at[:, pl.ds(size - RIM, RIM)], land, rim_send, rim_recv, after)
    gives, takes = spot < 2 * count - 1, spot > 0

    @pl.when(gives)
    def _():
        rim.start()

    @pl.when(takes)
    def _():
        rim.wait_recv()

    @pl.when(jnp.logical_not(takes))
    def _():
        land[...] = jnp.zeros_like(land)

    rim_ref[...] = land[...]
    for copy in copies:
        copy.wait_send()

    @pl.when(gives)
    def _():
        rim.wait_send()


def swap_back_kernel(
    rows,
    count,
    x_ref,
    tail_ref,
    rim_ref,
    small_ref,
    o_ref,
    land,
    fixed,
    own,
    send,
    recv,
    rim_send,
    rim_recv,
):
    d, z, c = place()
    me = d * 2 + c
    spot, before, after = neighbours(count)
    greet_plane_and_line(rows, count)
    size, part = x_ref.shape[1:]
    wide = o_ref.shape[2]
    rim = remote(rim_ref, land, rim_send, rim_recv, before)
    gives, takes = spot > 0, spot < 2 * count - 1

    @pl.when(gives)
    def _():
        rim.start()

    body, end = pl.ds(0, size - RIM), pl.ds(size - RIM, RIM)
    left, right = pl.ds(0, part), pl.ds(part, wide - part)
    copies = []
    for i, offset in enumerate(plane_offsets(rows)):
        peer = plane_peer(offset, rows)
        to = peer[0] * 2 + peer[2]
        copies.append(
            (
                remote(
                    x_ref.at[to, body], o_ref.at[me, body, left], send.at[0, i], recv.at[0, i], peer
                ),
                remote(small_ref, o_ref.at[me, :, right], send.at[1, i], recv.at[1, i], peer),
                remote(fixed.at[to], o_ref.at[me, end, left], send.at[2, i], recv.at[2, i], peer),
            )
        )
        copies[-1][0].start()
        copies[-1][1].start()
    keeps = [
        pltpu.make_async_copy(x_ref.at[me, body], o_ref.at[me, body, left], own.at[0]),
        pltpu.make_async_copy(small_ref, o_ref.at[me, :, right], own.at[1]),
        pltpu.make_async_copy(fixed.at[me], o_ref.at[me, end, left], own.at[2]),
    ]
    keeps[0].start()
    keeps[1].start()

    @pl.when(takes)
    def _():
        rim.wait_recv()

    @pl.when(jnp.logical_not(takes))
    def _():
        land[...] = jnp.zeros_like(land)

    fixed[...] = (tail_ref[...] + land[...].astype(F32)).astype(BF16)
    keeps[2].start()
    for group in copies:
        group[2].start()
    for keep in keeps:
        keep.wait()
    for group in copies:
        for copy in group:
            copy.wait()

    @pl.when(gives)
    def _():
        rim.wait_send()


def column_kernel(count, x_ref, o_ref, own, send, recv):
    d, z, c = place()
    others = [(d, lax.rem(z + k, count), c) for k in range(1, count)]
    greet(others)
    copies = []
    for i, peer in enumerate(others):
        copy = remote(x_ref, o_ref.at[z], send.at[i], recv.at[i], peer)
        copy.start()
        copies.append(copy)
    keep = pltpu.make_async_copy(x_ref, o_ref.at[z], own)
    keep.start()
    keep.wait()
    for copy in copies:
        copy.wait()


def neighbours(count):
    d, z, c = place()
    after = (d, lax.rem(z + c, count), 1 - c)
    before = (d, lax.rem(z + c - 1 + count, count), 1 - c)
    spot = z * 2 + c
    return spot, before, after


def greet_chain(count):
    spot, before, after = neighbours(count)
    barrier = pltpu.get_barrier_semaphore()

    @pl.when(spot > 0)
    def _():
        pl.semaphore_signal(barrier, inc=1, device_id=before, device_id_type=BY_MESH)

    @pl.when(spot < 2 * count - 1)
    def _():
        pl.semaphore_signal(barrier, inc=1, device_id=after, device_id_type=BY_MESH)

    pl.semaphore_wait(
        barrier,
        (spot > 0).astype(jnp.int32) + (spot < 2 * count - 1).astype(jnp.int32),
    )


def hop_kernel(count, forward, x_ref, o_ref, send, recv):
    spot, before, after = neighbours(count)
    greet_chain(count)
    if forward:
        gives, takes, to = spot < 2 * count - 1, spot > 0, after
    else:
        gives, takes, to = spot > 0, spot < 2 * count - 1, before
    copy = remote(x_ref, o_ref, send, recv, to)

    @pl.when(gives)
    def _():
        copy.start()

    @pl.when(takes)
    def _():
        copy.wait_recv()

    @pl.when(jnp.logical_not(takes))
    def _():
        o_ref[...] = jnp.zeros_like(o_ref)

    @pl.when(gives)
    def _():
        copy.wait_send()


def chain_kernel(
    count,
    rows,
    heads,
    sides,
    forward,
    high_ref,
    low_ref,
    add_ref,
    *refs,
):
    side_refs, (o_ref, *side_out_refs) = refs[:sides], refs[sides : 2 * sides + 1]
    land, stage, send, recv, own, side_send, side_recv = refs[2 * sides + 1 :]
    d, z, c = place()
    me = d * 2 + c
    spot, before, after = neighbours(count)
    offsets = plane_offsets(rows)
    barrier = pltpu.get_barrier_semaphore()
    for offset in offsets:
        pl.semaphore_signal(
            barrier, inc=1, device_id=plane_peer(offset, rows), device_id_type=BY_MESH
        )

    @pl.when((c == 0) & (z > 0))
    def _():
        pl.semaphore_signal(barrier, inc=1, device_id=before, device_id_type=BY_MESH)

    @pl.when((c == 1) & (z < count - 1))
    def _():
        pl.semaphore_signal(barrier, inc=1, device_id=after, device_id_type=BY_MESH)

    pl.semaphore_wait(
        barrier,
        len(offsets)
        + ((c == 0) & (z > 0)).astype(jnp.int32)
        + ((c == 1) & (z < count - 1)).astype(jnp.int32),
    )
    waits = []
    for j in range(sides):
        if side_refs[j].shape[0] == rows:
            for i in range(rows - 1):
                waits.append(
                    remote(
                        side_refs[j].at[i],
                        side_out_refs[j].at[i],
                        side_send.at[j, i],
                        side_recv.at[j, i],
                        (lax.rem(d + i + 1, rows), z, c),
                    )
                )
            waits.append(
                pltpu.make_async_copy(
                    side_refs[j].at[rows - 1], side_out_refs[j].at[rows - 1], own.at[j]
                )
            )
            continue
        for i, offset in enumerate(offsets):
            peer = plane_peer(offset, rows)
            waits.append(
                remote(
                    side_refs[j].at[peer[0] * 2 + peer[2]],
                    side_out_refs[j].at[me],
                    side_send.at[j, i],
                    side_recv.at[j, i],
                    peer,
                )
            )
        waits.append(
            pltpu.make_async_copy(side_refs[j].at[me], side_out_refs[j].at[me], own.at[j])
        )
    for copy in waits:
        copy.start()
    if forward:
        gives, takes, to = spot < 2 * count - 1, spot > 0, after
    else:
        gives, takes, to = spot > 0, spot < 2 * count - 1, before
    part = o_ref.shape[2] // PIECES
    copies = [
        remote(stage.at[i], land.at[i], send.at[i], recv.at[i], to)
        for i in range(heads * PIECES)
    ]
    for h in range(heads):
        for j in range(PIECES):
            i = h * PIECES + j
            columns = slice(j * part, (j + 1) * part)

            @pl.when(jnp.logical_not(takes))
            def _():
                land[i] = jnp.zeros_like(land[i])

            @pl.when(takes)
            def _():
                copies[i].wait_recv()

            @pl.when(gives)
            def _():
                state = land[i]
                leaving = add_ref[h, :, columns] + mm(high_ref[h], state) + mm(low_ref[h], state)
                stage[i] = leaving.astype(BF16)
                copies[i].start()

    for copy in copies:

        @pl.when(gives)
        def _():
            copy.wait_send()

    for h in range(heads):
        for j in range(PIECES):
            o_ref[h, :, j * part : (j + 1) * part] = land[h * PIECES + j]
    for copy in waits:
        copy.wait()


ANY = pl.BlockSpec(memory_space=pl.ANY)
IN_VMEM = pl.BlockSpec(memory_space=pltpu.VMEM)
IN_HBM = pl.BlockSpec(memory_space=pltpu.HBM)


def dma(*shape):
    return pltpu.SemaphoreType.DMA(shape)


def comm_call(body, out, scratch, ident, operands, spec=ANY, cost=30):
    return pl.pallas_call(
        body,
        out_shape=out,
        in_specs=[spec] * len(operands),
        out_specs=spec,
        scratch_shapes=scratch,
        compiler_params=pltpu.CompilerParams(collective_id=ident, has_side_effects=True),
        cost_estimate=pl.CostEstimate(
            flops=0, bytes_accessed=int(cost * 3.0e6), transcendentals=0
        ),
    )(*operands)


def swap(x, ident):
    rows = lax.axis_size("dp")
    links = 2 * rows - 1
    return comm_call(
        partial(swap_kernel, rows),
        jax.ShapeDtypeStruct(x.shape, x.dtype),
        [pltpu.SemaphoreType.DMA, dma(links), dma(links)],
        ident,
        (x,),
    )


def spread(x, ident):
    rows = lax.axis_size("dp")
    return comm_call(
        partial(spread_kernel, rows),
        jax.ShapeDtypeStruct((2 * rows,) + x.shape, x.dtype),
        [pltpu.SemaphoreType.DMA, dma(rows - 1), dma(rows - 1), dma(rows), dma(rows)],
        ident,
        (x,),
    )


def fold(x, ident):
    rows = lax.axis_size("dp")
    part = (rows,) + x.shape[1:]
    received = comm_call(
        partial(fold_kernel, rows),
        jax.ShapeDtypeStruct(part, x.dtype),
        [
            pltpu.VMEM(part, x.dtype),
            pltpu.VMEM(part, x.dtype),
            dma(rows),
            dma(rows),
            dma(rows),
            dma(rows - 1),
            dma(rows - 1),
            pltpu.SemaphoreType.DMA,
        ],
        ident,
        (x,),
    )
    return jnp.sum(received.astype(F32), axis=0)


def turn(x, gain, base, more, ident):
    rows = lax.axis_size("dp")
    group, length, width = x.shape
    backward = bool(more)
    part, sent = (rows, length, width), (rows - 1, length, width)
    return pl.pallas_call(
        partial(turn_kernel, rows, backward),
        out_shape=[
            jax.ShapeDtypeStruct((length, width), F32),
            jax.ShapeDtypeStruct((group, length, width), BF16),
        ]
        + (
            [jax.ShapeDtypeStruct((1, width), F32), jax.ShapeDtypeStruct(part, BF16)]
            if backward
            else []
        ),
        in_specs=[ANY, IN_VMEM, IN_VMEM] + ([IN_VMEM, ANY] if backward else []),
        out_specs=[IN_VMEM, ANY] + ([IN_VMEM, IN_VMEM] if backward else []),
        scratch_shapes=[
            pltpu.VMEM(part, F32),
            pltpu.VMEM(part, F32),
            pltpu.VMEM(sent, BF16),
            pltpu.VMEM(sent, BF16),
            pltpu.VMEM((length, width), BF16),
        ]
        + [dma(CHUNKS, rows)] * 3
        + [dma(CHUNKS, rows - 1)] * 2
        + [dma(CHUNKS)]
        + [dma(CHUNKS, rows - 1)] * 2
        + [dma(CHUNKS, rows)] * 2
        + ([pltpu.VMEM(part, BF16)] + [dma(rows)] * 3 if backward else []),
        compiler_params=pltpu.CompilerParams(collective_id=ident, has_side_effects=True),
        cost_estimate=pl.CostEstimate(
            flops=0, bytes_accessed=150_000_000, transcendentals=0
        ),
    )(x, gain, base, *more)


def swap_on(x, ident):
    rows, count = lax.axis_size("dp"), lax.axis_size("zq")
    group, length, part = x.shape
    links = 2 * rows - 1
    return pl.pallas_call(
        partial(swap_on_kernel, rows, count),
        out_shape=[
            jax.ShapeDtypeStruct(x.shape, x.dtype),
            jax.ShapeDtypeStruct((group, RIM, part), x.dtype),
        ],
        in_specs=[ANY],
        out_specs=[ANY, IN_VMEM],
        scratch_shapes=[
            pltpu.VMEM((group, RIM, part), x.dtype),
            pltpu.SemaphoreType.DMA,
            dma(links),
            dma(links),
            pltpu.SemaphoreType.DMA,
            pltpu.SemaphoreType.DMA,
        ],
        compiler_params=pltpu.CompilerParams(collective_id=ident, has_side_effects=True),
        cost_estimate=pl.CostEstimate(flops=0, bytes_accessed=90_000_000, transcendentals=0),
    )(x)


def swap_back(x, tail, rim, small, ident):
    rows, count = lax.axis_size("dp"), lax.axis_size("zq")
    group, length, part = x.shape
    links = 2 * rows - 1
    return pl.pallas_call(
        partial(swap_back_kernel, rows, count),
        out_shape=jax.ShapeDtypeStruct((group, length, part + small.shape[1]), x.dtype),
        in_specs=[ANY, IN_VMEM, ANY, ANY],
        out_specs=ANY,
        scratch_shapes=[
            pltpu.VMEM((group, RIM, part), x.dtype),
            pltpu.VMEM((group, RIM, part), x.dtype),
            dma(3),
            dma(3, links),
            dma(3, links),
            pltpu.SemaphoreType.DMA,
            pltpu.SemaphoreType.DMA,
        ],
        compiler_params=pltpu.CompilerParams(collective_id=ident, has_side_effects=True),
        cost_estimate=pl.CostEstimate(flops=0, bytes_accessed=90_000_000, transcendentals=0),
    )(x, tail, rim, small)


def begin(hidden, grad, gain, decay, beta, weights, ident):
    rows, count = lax.axis_size("dp"), lax.axis_size("zq")
    group, links = 2 * rows, 2 * rows - 1
    owned = decay.shape[0]
    parts = [weight.shape[1] // group for weight in weights]
    wide = sum(parts[:4]) + LANES
    cut = (group, owned, wide)
    side_shapes = [(group, owned, sum(parts[4:6])), (group, owned, sum(parts[6:]))]
    assert count > 2
    tokens = jax.ShapeDtypeStruct(hidden.shape, BF16)
    everyone = jax.ShapeDtypeStruct((group,) + hidden.shape, BF16)
    return pl.pallas_call(
        partial(start_kernel, rows, count),
        out_shape=[jax.ShapeDtypeStruct((count,) + cut, BF16)]
        + [jax.ShapeDtypeStruct(shape, BF16) for shape in side_shapes]
        + [everyone] * 2
        + [tokens] * 3,
        in_specs=[IN_VMEM] * 5 + [IN_HBM] * 8,
        out_specs=[ANY] * 5 + [IN_VMEM] * 3,
        scratch_shapes=[pltpu.VMEM(weight.shape, F32) for weight in weights]
        + [pltpu.VMEM(cut, BF16)]
        + [pltpu.VMEM(shape, BF16) for shape in side_shapes]
        + [
            dma(8),
            dma(5),
            dma(links),
            dma(links),
            dma(2, links),
            dma(2, links),
            dma(2, rows - 1),
            dma(2, rows - 1),
            dma(2, rows),
            dma(2, rows),
        ]
        + [dma(count - 1, group)] * 4,
        compiler_params=pltpu.CompilerParams(
            collective_id=ident, has_side_effects=True
        ),
        cost_estimate=pl.CostEstimate(
            flops=0, bytes_accessed=300_000_000, transcendentals=0
        ),
    )(hidden, grad, gain, decay, beta, *weights)


def column(x, ident):
    count = lax.axis_size("zq")
    return comm_call(
        partial(column_kernel, count),
        jax.ShapeDtypeStruct((count,) + x.shape, x.dtype),
        [pltpu.SemaphoreType.DMA, dma(count - 1), dma(count - 1)],
        ident,
        (x,),
    )


def hop(x, forward, ident):
    count = lax.axis_size("zq")
    return comm_call(
        partial(hop_kernel, count, forward),
        jax.ShapeDtypeStruct(x.shape, x.dtype),
        [pltpu.SemaphoreType.DMA, pltpu.SemaphoreType.DMA],
        ident,
        (x,),
        IN_VMEM,
    )


def chain(high, low, add, sides, forward, ident):
    rows, count = lax.axis_size("dp"), lax.axis_size("zq")
    heads, key_size, value_size = add.shape
    links = 2 * rows - 1
    pieces = (heads * PIECES, key_size, value_size // PIECES)
    return pl.pallas_call(
        partial(chain_kernel, count, rows, heads, len(sides), forward),
        out_shape=[jax.ShapeDtypeStruct(add.shape, BF16)]
        + [jax.ShapeDtypeStruct(side.shape, side.dtype) for side in sides],
        in_specs=[IN_VMEM] * 3 + [ANY] * len(sides),
        out_specs=[IN_VMEM] + [ANY] * len(sides),
        scratch_shapes=[
            pltpu.VMEM(pieces, BF16),
            pltpu.VMEM(pieces, BF16),
            dma(heads * PIECES),
            dma(heads * PIECES),
            dma(len(sides)),
            dma(len(sides), links),
            dma(len(sides), links),
        ],
        compiler_params=pltpu.CompilerParams(collective_id=ident, has_side_effects=True),
        cost_estimate=pl.CostEstimate(
            flops=0, bytes_accessed=200_000_000, transcendentals=0
        ),
    )(high, low, add, *sides)


def unit_lower_inverses(lows):
    shape = lows[0].shape
    row = lax.broadcasted_iota(jnp.int32, shape, 0)
    col = lax.broadcasted_iota(jnp.int32, shape, 1)

    def same(width):
        shift = width.bit_length() - 1
        return (row >> shift) == (col >> shift)

    def products(lefts, rights):
        return [exact(left, right) for left, right in zip(lefts, rights)]

    eye = (row == col).astype(F32)
    width = 8
    near = [jnp.where(same(width), low, 0.0) for low in lows]
    square = products(near, near)
    inverse = [eye - block for block in near]
    inverse = [x + y for x, y in zip(inverse, products(inverse, square))]
    square = products(square, square)
    inverse = [x + y for x, y in zip(inverse, products(inverse, square))]
    while width < shape[0]:
        picked = same(2 * width) & jnp.logical_not(same(width))
        cross = [jnp.where(picked, low, 0.0) for low in lows]
        inverse = [
            x - y for x, y in zip(inverse, products(inverse, products(cross, inverse)))
        ]
        width *= 2
    return inverse


def unit_parts(values):
    scale = lax.rsqrt(jnp.sum(values * values, axis=-1, keepdims=True) + EPSILON)
    return values * scale, scale


def unit_back(unit, scale, grad):
    return scale * (grad - unit * jnp.sum(unit * grad, axis=-1, keepdims=True))


def strict_lower(size):
    row = lax.broadcasted_iota(jnp.int32, (size, size), 0)
    col = lax.broadcasted_iota(jnp.int32, (size, size), 1)
    return (row > col).astype(F32)


def convolve(x_ref, rim_ref, taps_ref, same_ref, ext):
    size = x_ref.shape[1]
    ext[:RIM] = rim_ref[0].astype(F32)
    ext[RIM:] = x_ref[0].astype(F32)
    mixed = taps_ref[0:1] * ext[RIM:]
    for lag in range(1, CONV):
        mixed = mixed + taps_ref[lag : lag + 1] * ext[RIM - lag : RIM - lag + size] * (
            same_ref[:, lag : lag + 1]
        )
    return mixed


def convolve_back(grad, taps_ref, same_ref, ext, back):
    size = grad.shape[0]
    back[:RIM] = jnp.zeros((RIM, grad.shape[1]), F32)
    back[RIM:] = taps_ref[0:1] * grad
    sums = [jnp.sum(grad * ext[RIM:], axis=0, keepdims=True)]
    for lag in range(1, CONV):
        kept = grad * same_ref[:, lag : lag + 1]
        sums.append(
            jnp.sum(kept * ext[RIM - lag : RIM - lag + size], axis=0, keepdims=True)
        )
        back[RIM - lag : RIM - lag + size] += taps_ref[lag : lag + 1] * kept
    return jnp.concatenate(sums, axis=0)


def silu_parts(values):
    sig = jax.nn.sigmoid(values)
    return values * sig, sig * (1.0 + values * (1.0 - sig))


def chunk_forward_kernel(step, *refs):
    count = 4 * step
    pre_refs, rim_refs, tap_refs = refs[:count], refs[count : 2 * count], refs[2 * count : 3 * count]
    same_ref, lines_ref, decay_ref = refs[3 * count : 3 * count + 3]
    (
        inverse_ref,
        scores_ref,
        own_ref,
        effect_ref,
        offset_ref,
        high_ref,
        low_ref,
        back_high_ref,
        back_low_ref,
    ) = refs[3 * count + 3 : 3 * count + 12]
    ext = refs[3 * count + 12]
    heads, lows = [], []
    for u in range(step):
        active = []
        for i in range(4 * u, 4 * u + 4):
            mixed = convolve(pre_refs[i], rim_refs[i], tap_refs[i], same_ref, ext.at[i])
            active.append(silu_parts(mixed)[0])
        size, key_size = active[0].shape
        columns = lines_ref[u].T
        beta, start, tail = columns[:, 0:1], columns[:, 1:2], columns[:, 2:3]
        decay = decay_ref[u]
        query = unit_parts(active[0])[0] * key_size ** (-0.5)
        key = unit_parts(active[1])[0]
        values = jnp.concatenate(active[2:], axis=1)
        inner = exact(key, key, (1, 1))
        lows.append(beta * inner * (decay * strict_lower(size)))
        heads.append((query, key, values, beta, start, tail, decay))
    inverses = unit_lower_inverses(lows)
    row = lax.broadcasted_iota(jnp.int32, (key_size, key_size), 0)
    col = lax.broadcasted_iota(jnp.int32, (key_size, key_size), 1)
    for u in range(step):
        query, key, values, beta, start, tail, decay = heads[u]
        inverse = inverses[u]
        width = values.shape[1]
        scores = exact(query, key, (1, 1)) * decay
        update = exact(inverse, beta * values)
        reach = exact(inverse, (beta * start) * key)
        inverse_ref[u] = inverse
        scores_ref[u] = scores
        own_ref[:, u * width : (u + 1) * width] = exact(scores, update)
        effect_ref[u] = start * query - exact(scores, reach)
        last = tail * key
        offset_ref[u] = exact(last, update, (0, 0))
        transfer = jnp.where(row == col, start[size - 1 :, :], 0.0) - exact(
            last, reach, (0, 0)
        )
        for matrix, top_ref, rest_ref in (
            (transfer, high_ref, low_ref),
            (transfer.T, back_high_ref, back_low_ref),
        ):
            top = matrix.astype(BF16)
            top_ref[u] = top
            rest_ref[u] = (matrix - top.astype(F32)).astype(BF16)


def gate_forward_kernel(own_ref, effect_ref, state_ref, gate_ref, gain_ref, mixed_ref, gated_ref):
    mixed = own_ref[...] + exact(effect_ref[0], state_ref[0].astype(F32))
    mixed_ref[...] = mixed
    gate = gate_ref[...].astype(F32)
    gated_ref[...] = (
        rms_scale(mixed) * gain_ref[...] * (gate * jax.nn.sigmoid(gate))
    ).astype(BF16)


def gate_backward_kernel(
    mixed_ref, gate_ref, gain_ref, grad_ref, effect_ref, out_ref, gate_grad_ref, gain_grad_ref, add_ref
):
    mixed = mixed_ref[...]
    gate = gate_ref[...].astype(F32)
    grad = grad_ref[...].astype(F32)
    gain = gain_ref[...]
    scale = lax.rsqrt(jnp.mean(mixed * mixed, axis=-1, keepdims=True) + EPSILON)
    normed = mixed * scale
    sig = jax.nn.sigmoid(gate)
    act = gate * sig
    gain_grad_ref[0] = jnp.sum(grad * normed * act, axis=0, keepdims=True)
    gate_grad_ref[...] = (
        grad * normed * gain * (sig * (1.0 + gate * (1.0 - sig)))
    ).astype(BF16)
    inner = grad * gain * act
    mixed_grad = scale * (inner - normed * jnp.mean(inner * normed, axis=-1, keepdims=True))
    out_ref[...] = mixed_grad
    add_ref[0] = exact(effect_ref[0], mixed_grad, (0, 0))


def chunk_backward_kernel(heads, *refs):
    pre_refs, rim_refs, tap_refs = refs[:4], refs[4:8], refs[8:12]
    same_ref, lines_ref, decay_ref = refs[12:15]
    inverse_ref, scores_ref, state_ref, mixed_ref, ending_ref = refs[15:20]
    (
        grad_ref,
        grad_tail_ref,
        grad_rim_ref,
        taps_grad_ref,
        dlines_ref,
        ddecay_ref,
    ) = refs[20:26]
    ext, back = refs[26:]
    active, slopes = [], []
    for i in range(4):
        mixed = convolve(pre_refs[i], rim_refs[i], tap_refs[i], same_ref, ext.at[i])
        value, slope = silu_parts(mixed)
        active.append(value)
        slopes.append(slope)
    size, key_size = active[0].shape
    values = jnp.concatenate(active[2:], axis=1)
    columns = lines_ref[0].T
    beta, start, tail = columns[:, 0:1], columns[:, 1:2], columns[:, 2:3]
    decay, inverse, scores = decay_ref[0], inverse_ref[0], scores_ref[0]
    state = state_ref[0].astype(F32)
    ending = ending_ref[0].astype(F32)
    mixed_grad = mixed_ref[...]
    unit_q, scale_q = unit_parts(active[0])
    query = unit_q * key_size ** (-0.5)
    key, scale_k = unit_parts(active[1])
    below = strict_lower(size)
    inner = exact(key, key, (1, 1))
    raw = exact(query, key, (1, 1))
    recalled = exact(key, state)
    miss = values - start * recalled
    update = exact(inverse, beta * miss)
    mixed_state = exact(mixed_grad, state, (1, 1))
    last = tail * key
    dupdate = exact(scores, mixed_grad, (0, 0)) + exact(last, ending)
    dscores = exact(mixed_grad, update, (1, 1))
    dlast = exact(update, ending, (1, 1))
    dright = exact(inverse, dupdate, (0, 0))
    dlower = -exact(dright, update, (1, 1)) * below
    dscaled = dscores * decay
    dquery = start * mixed_state + exact(dscaled, key)
    dinner = beta * dlower * decay
    dkey = (
        tail * dlast
        + exact(dscaled, query, (0, 0))
        - exact((beta * start) * dright, state, (1, 1))
        + exact(dinner, key)
        + exact(dinner, key, (0, 0))
    )
    right_recalled = jnp.sum(dright * recalled, axis=-1, keepdims=True)
    dbeta = jnp.sum(dright * miss, axis=-1, keepdims=True) + jnp.sum(
        dlower * inner * decay, axis=-1, keepdims=True
    )
    final = jnp.sum(jnp.sum(ending * state, axis=-1, keepdims=True), axis=0, keepdims=True)
    row = lax.broadcasted_iota(jnp.int32, (size, 1), 0)
    dstart = (
        jnp.sum(query * mixed_state, axis=-1, keepdims=True)
        - beta * right_recalled
        + jnp.where(row == size - 1, final, 0.0)
    )
    dtail = jnp.sum(key * dlast, axis=-1, keepdims=True)
    dlines_ref[0] = jnp.concatenate(
        [dbeta, dstart, dtail, jnp.zeros((size, 5), F32)], axis=1
    ).T
    ddecay_ref[0] = dscores * raw + beta * dlower * inner
    dvalues = beta * dright
    grads = [
        unit_back(unit_q, scale_q, dquery * key_size ** (-0.5)),
        unit_back(key, scale_k, dkey),
        dvalues[:, :key_size],
        dvalues[:, key_size:],
    ]
    head = pl.program_id(0)
    per = grad_ref.shape[2] // key_size
    for i, block in enumerate((head, heads + head, 2 * heads + 2 * head, 2 * heads + 2 * head + 1)):
        sums = convolve_back(grads[i] * slopes[i], tap_refs[i], same_ref, ext.at[i], back)
        slab = block // per
        columns = pl.ds(pl.multiple_of((block % per) * key_size, key_size), key_size)
        grad_ref[slab, :, columns] = back[RIM:].astype(BF16)
        grad_tail_ref[slab, :, columns] = back[size:]
        grad_rim_ref[slab, :, columns] = back[:RIM].astype(BF16)
        taps_grad_ref[slab, 0:CONV, columns] = sums


def by_head(*shape):
    return pl.BlockSpec((1,) + shape, lambda h: (h, 0, 0))


def by_heads(step, *shape):
    return pl.BlockSpec((step,) + shape, lambda h: (h, 0, 0))


def by_columns(rows, width, offset=0):
    return pl.BlockSpec((rows, width), lambda h: (0, h + offset))


def head_call(body, heads, in_specs, out_specs, out_shape, operands, flops, scratch=()):
    return pl.pallas_call(
        body,
        scratch_shapes=scratch,
        grid=(heads,),
        in_specs=in_specs,
        out_specs=out_specs,
        out_shape=out_shape,
        cost_estimate=pl.CostEstimate(flops=flops, bytes_accessed=20_000_000, transcendentals=0),
    )(*operands)


def shaped(*shape, dtype=F32):
    return jax.ShapeDtypeStruct(shape, dtype)


def decays(segment, before, decay_pre, beta_pre, a_log):
    length = segment.shape[0]
    beta = jax.nn.sigmoid(beta_pre)
    decay_log = -jnp.exp(a_log) * jax.nn.softplus(decay_pre)
    order = jnp.arange(length)
    lower = order[:, None] >= order[None, :]
    running = exact(lower.astype(F32), decay_log).T
    live = (segment[:, None] == segment[None, :]) & lower
    gap = running[:, :, None] - running[:, None, :]
    decay = jnp.where(live, jnp.exp(jnp.where(live, gap, 0.0)), 0.0)
    start = jnp.exp(running) * (segment == before).astype(F32)
    live_last = segment == segment[-1]
    last_gap = running[:, -1:] - running
    tail = jnp.where(live_last, jnp.exp(jnp.where(live_last, last_gap, 0.0)), 0.0)
    filler = jnp.zeros((5,) + start.shape, F32)
    return jnp.moveaxis(jnp.concatenate([jnp.stack([beta.T, start, tail]), filler]), 0, 1), decay


def local(
    hidden_in,
    segment_ids,
    grad_out,
    attn_gain,
    w_query,
    w_key,
    w_value,
    w_decay,
    w_beta,
    w_outgate,
    a_log,
    conv_query,
    conv_key,
    conv_value,
    out_gain,
    w_output,
    mlp_gain,
    w_gate,
    w_up,
    w_down,
):
    rows, count = lax.axis_size("dp"), lax.axis_size("zq")
    group = 2 * rows
    segment = segment_ids[0]
    length, width = hidden_in.shape[1:]
    heads = a_log.shape[0]
    key_width, value_width = w_query.shape[1], w_value.shape[1]
    key_size, value_size = key_width // heads, out_gain.shape[0]
    mixer_width = 2 * key_width + value_width
    hidden_width = w_gate.shape[1]
    owned = w_query.shape[0]
    margin = CONV - 1
    me = lax.axis_index("dp") * 2 + lax.axis_index("c")
    mixer_part = mixer_width // group
    back_width = value_width // group
    ffn_width = hidden_width // group

    def shuffled(values):
        return (
            values.reshape(-1, rows, count, 2 * owned).swapaxes(1, 2).reshape(-1, width)
        )

    def unshuffled(values):
        return (
            values.reshape(-1, count, rows, 2 * owned).swapaxes(1, 2).reshape(-1, width)
        )

    def cut(values):
        return values.astype(BF16).reshape(owned, group, -1).swapaxes(0, 1)

    def joined(values):
        return values.swapaxes(0, 1).reshape(values.shape[1], -1)

    def gathered(values):
        return lax.all_gather(values.reshape(group * owned, -1), "zq", axis=0, tiled=True)

    def scattered(values):
        return lax.psum_scatter(
            values, "zq", scatter_dimension=0, tiled=True
        ).reshape(group, owned, -1)

    def blocks(values):
        return values.astype(BF16).reshape(group, length, -1)

    (
        mixer_weights,
        first_own,
        gate_up_own,
        normed_all,
        grad_all,
        hidden_low,
        normed_low,
        grad_low,
    ) = begin(
        hidden_in[0],
        grad_out[0],
        attn_gain[None],
        w_decay,
        w_beta,
        (w_query, w_key, w_value, w_outgate, w_output, w_down, w_gate, w_up),
        0,
    )
    mixer_weights = mixer_weights.reshape(width, -1)
    normed_all = normed_all.reshape(-1, width)
    grad_all = grad_all.reshape(-1, width)
    project = mixer_weights[:, : mixer_part + back_width]
    small_weights = mixer_weights[:, mixer_part + back_width :]
    first_weights = gathered(first_own)
    output_weights, down = first_weights[:, :back_width], first_weights[:, back_width:]

    inputs = hidden_low.astype(F32)
    attn_row, mlp_row = shuffled(attn_gain[None]), shuffled(mlp_gain[None])
    normed, norm_pull = jax.vjp(rms_scale, inputs)
    pre_all = mm(normed_all, project[:, :mixer_part])
    gate_all = mm(normed_all, project[:, mixer_part:])
    pre, rim = swap_on(blocks(pre_all), 3)
    small_pre = mm(normed_low, small_weights)
    decay_pre, beta_pre = small_pre[:, :heads], small_pre[:, heads : 2 * heads]
    rim_ids = lax.ppermute(
        segment[-margin:],
        ("zq", "c"),
        [(i, i + 1) for i in range(2 * count - 1)],
    )
    seg_ext = jnp.concatenate([rim_ids, segment])
    same = jnp.stack(
        [
            (segment == seg_ext[margin - lag : margin - lag + length]).astype(F32)
            for lag in range(CONV)
        ],
        axis=1,
    )
    (lines, decay), decay_pull = jax.vjp(
        partial(decays, segment, seg_ext[margin - 1]), decay_pre, beta_pre, a_log
    )
    slabs, slab = group, mixer_part
    if slab % key_size:
        slabs, slab = mixer_width // (3 * key_size), 3 * key_size
        pre, rim = [
            joined(part).reshape(-1, slabs, slab).swapaxes(0, 1) for part in (pre, rim)
        ]
    per = slab // key_size
    taps = jnp.concatenate([conv_query, conv_key, conv_value], axis=1)
    channel_blocks = [
        lambda h: h,
        lambda h: heads + h,
        lambda h: 2 * heads + 2 * h,
        lambda h: 2 * heads + 2 * h + 1,
    ]

    step = 2 if heads % 2 == 0 else 1

    def at_blocks(make, step):
        return [
            make(lambda h, b=b, u=u: b(step * h + u)) for u in range(step) for b in channel_blocks
        ]

    def token_specs(step):
        def in_slab(lines):
            return lambda at: pl.BlockSpec(
                (1, lines, key_size), lambda h: (at(h) // per, 0, at(h) % per)
            )

        return (
            at_blocks(in_slab(length), step)
            + at_blocks(in_slab(RIM), step)
            + at_blocks(lambda at: pl.BlockSpec((CONV, key_size), lambda h: (0, at(h))), step)
            + [pl.BlockSpec((length, CONV), lambda h: (0, 0))]
            + [by_heads(step, 8, length), by_heads(step, length, length)]
        )

    def token_args(step):
        blocks = 4 * step
        return (pre,) * blocks + (rim,) * blocks + (taps,) * blocks + (same, lines, decay)

    values_spec = by_columns(length, value_size)
    state_spec = by_head(key_size, value_size)
    inverse, scores, own, effect, offset, high, low, back_high, back_low = head_call(
        partial(chunk_forward_kernel, step),
        heads // step,
        token_specs(step),
        [
            by_heads(step, length, length),
            by_heads(step, length, length),
            by_columns(length, step * value_size),
            by_heads(step, length, key_size),
            by_heads(step, key_size, value_size),
        ]
        + [by_heads(step, key_size, key_size)] * 4,
        [
            shaped(heads, length, length),
            shaped(heads, length, length),
            shaped(length, value_width),
            shaped(heads, length, key_size),
            shaped(heads, key_size, value_size),
        ]
        + [shaped(heads, key_size, key_size, dtype=BF16)] * 4,
        token_args(step),
        6_000_000_000,
        [pltpu.VMEM((4 * step, RIM + length, key_size), F32)],
    )
    state, gate_back = chain(high, low, offset, (gate_all.reshape(group, length, -1),), True, 5)
    gate_pre = joined(gate_back)
    gate_up_own, state, first_weights = lax.optimization_barrier(
        (gate_up_own, state, first_weights)
    )
    gate_up = gathered(gate_up_own)
    gain_spec = pl.BlockSpec((1, value_size), lambda h: (0, 0))
    gain_row = out_gain[None]
    mixed, gated = head_call(
        gate_forward_kernel,
        heads,
        [values_spec, by_head(length, key_size), state_spec, values_spec, gain_spec],
        [values_spec, values_spec],
        [shaped(length, value_width), shaped(length, value_width, dtype=BF16)],
        (own, effect, state, gate_pre, gain_row),
        1_000_000_000,
    )
    gated_cut = gated.reshape(length, group, back_width).swapaxes(0, 1)
    gated_all = swap(gated_cut, 6).reshape(-1, back_width)
    middle, normed_two_all = turn(
        mm(gated_all, output_weights, (1, 1)).reshape(group, length, width),
        mlp_row,
        inputs,
        (),
        4,
    )
    normed_two_all = normed_two_all.reshape(-1, width)

    both = mm(normed_two_all, gate_up)
    hidden, swiglu_pull = jax.vjp(swiglu, both[:, :ffn_width], both[:, ffn_width:])
    hidden_low = hidden.astype(BF16)
    grad_gate, grad_up = swiglu_pull(mm(grad_all, down))
    both_grad_low = jnp.concatenate([grad_gate, grad_up], axis=1).astype(BF16)
    grad_normed_two_parts = mm(both_grad_low, gate_up, (1, 1)).reshape(group, length, width)
    mlp_parts = blocks(mm(hidden_low, down, (1, 1)))
    gate_up_rows = mm(normed_two_all, both_grad_low, (0, 0)).astype(BF16)
    grad_normed_two_parts, gate_up_rows = lax.optimization_barrier(
        (grad_normed_two_parts, gate_up_rows)
    )
    gate_up_rows = scattered(gate_up_rows)
    grad_middle, attended_grad_all, grad_mlp_gain, mlp_pairs = turn(
        grad_normed_two_parts, mlp_row, grad_low, (middle, mlp_parts), 2
    )
    attended_grad_all = attended_grad_all.reshape(-1, width)

    grad_gated = joined(swap(blocks(mm(attended_grad_all, output_weights)), 6))
    output_rows = mm(attended_grad_all, gated_all, (0, 0)).astype(BF16)
    down_rows = mm(grad_all, hidden_low, (0, 0)).astype(BF16)
    mixed_grad, gate_pre_grad, gain_grad, state_add = head_call(
        gate_backward_kernel,
        heads,
        [values_spec, values_spec, gain_spec, values_spec, by_head(length, key_size)],
        [values_spec, values_spec, by_head(1, value_size), state_spec],
        [
            shaped(length, value_width),
            shaped(length, value_width, dtype=BF16),
            shaped(heads, 1, value_size),
            shaped(heads, key_size, value_size),
        ],
        (mixed, gate_pre, gain_row, grad_gated, effect),
        1_000_000_000,
    )
    grad_out_gain = jnp.sum(gain_grad, axis=(0, 1))
    side_rows = jnp.concatenate([down_rows, output_rows], axis=1)
    state_add, gate_up_rows, side_rows = lax.optimization_barrier(
        (state_add, gate_up_rows, side_rows)
    )
    ending, gate_grad_back, mlp_back = chain(
        back_high,
        back_low,
        state_add,
        (gate_pre_grad.reshape(length, group, back_width).swapaxes(0, 1), mlp_pairs),
        False,
        8,
    )
    gate_grad_all = gate_grad_back.reshape(-1, back_width)
    side_rows, ending = lax.optimization_barrier((side_rows, ending))
    side_rows = scattered(side_rows)
    gate_up_back = lax.all_to_all(gate_up_rows, ("dp", "c"), 0, 0, tiled=True)
    whole = lambda *shape: pl.BlockSpec(shape, lambda h: (0, 0, 0))
    grad_pre, grad_tail, grad_rim, grad_taps, dlines, ddecay = head_call(
        partial(chunk_backward_kernel, heads),
        heads,
        token_specs(1)
        + [
            by_head(length, length),
            by_head(length, length),
            state_spec,
            values_spec,
            state_spec,
        ],
        [
            whole(slabs, length, slab),
            whole(slabs, RIM, slab),
            whole(slabs, RIM, slab),
            whole(slabs, 2 * CONV, slab),
        ]
        + [by_head(8, length), by_head(length, length)],
        [
            shaped(slabs, length, slab, dtype=BF16),
            shaped(slabs, RIM, slab),
            shaped(slabs, RIM, slab, dtype=BF16),
            shaped(slabs, 2 * CONV, slab),
            shaped(heads, 8, length),
            shaped(heads, length, length),
        ],
        token_args(1) + (inverse, scores, state, mixed_grad, ending),
        12_000_000_000,
        [pltpu.VMEM((4, RIM + length, key_size), F32), pltpu.VMEM((RIM + length, key_size), F32)],
    )
    grad_decay, grad_beta, grad_alog = decay_pull((dlines, ddecay))
    grad_taps = joined(grad_taps)[:CONV]
    grad_conv_one = grad_taps[:, :key_width]
    grad_conv_two = grad_taps[:, key_width : 2 * key_width]
    grad_conv_three = grad_taps[:, 2 * key_width :]
    small_grad = jnp.concatenate([grad_decay, grad_beta], axis=1).astype(BF16)
    small_grad = jnp.pad(small_grad, ((0, 0), (0, LANES - 2 * heads)))
    if slabs != group:
        grad_pre, grad_tail, grad_rim = [
            joined(part).reshape(-1, group, mixer_part).swapaxes(0, 1)
            for part in (grad_pre, grad_tail, grad_rim)
        ]
    grad_pre, gate_up_back = lax.optimization_barrier((grad_pre, gate_up_back))
    grads_all = swap_back(grad_pre, grad_tail, grad_rim, small_grad, 10).reshape(
        group * length, -1
    )
    mixer_parts = jnp.concatenate(
        [
            mm(normed_all, grads_all, (0, 0)).astype(BF16),
            mm(normed_all, gate_grad_all, (0, 0)).astype(BF16),
        ],
        axis=1,
    )
    mixer_parts, side_rows = lax.optimization_barrier((mixer_parts, side_rows))
    mixer_rows = scattered(mixer_parts)
    combined = fold(
        blocks(
            mm(
                jnp.concatenate([grads_all[:, :mixer_part], gate_grad_all], axis=1),
                project,
                (1, 1),
            )
        ),
        7,
    )
    mlp_part = jnp.sum(mlp_back.astype(F32), axis=0)
    result = (middle + mlp_part).astype(BF16)
    combined = combined + mm(small_grad, small_weights, (1, 1))
    grad_attn_gain = jnp.sum(combined * normed, axis=0)
    grad_inputs = grad_middle + norm_pull(combined * attn_row)[0]

    side_back = lax.all_to_all(side_rows, ("dp", "c"), 0, 0, tiled=True).astype(F32)
    gate_grad = joined(gate_up_back[:, :, :ffn_width].astype(F32))
    up_grad = joined(gate_up_back[:, :, ffn_width:].astype(F32))
    down_grad = joined(side_back[:, :, :ffn_width])
    output_grad = joined(side_back[:, :, ffn_width:])

    pieces = (
        grad_attn_gain,
        grad_alog,
        grad_conv_one,
        grad_conv_two,
        grad_conv_three,
        grad_out_gain,
        grad_mlp_gain,
    )
    flat = jnp.concatenate([piece.reshape(-1) for piece in pieces])
    lines = -(-flat.shape[0] // (group * 8 * LANES)) * 8
    flat = jnp.pad(flat, (0, group * lines * LANES - flat.shape[0])).reshape(group, lines, LANES)
    flat = jnp.sum(swap(flat, 11), axis=0)
    flat = jnp.sum(column(flat, 12), axis=0)
    flat = spread(flat, 16).reshape(-1)
    mixer_rows, _ = lax.optimization_barrier((mixer_rows, (flat, grad_inputs)))
    mixer_swapped = swap(
        jnp.concatenate(
            [mixer_rows[:, :, :mixer_part], mixer_rows[:, :, mixer_part + LANES :]], axis=2
        ),
        15,
    ).astype(F32)
    mixer_back = joined(mixer_swapped[:, :, :mixer_part])
    outgate_grad = joined(mixer_swapped[:, :, mixer_part:])
    small_rows = lax.dynamic_index_in_dim(mixer_rows, me, 0, keepdims=False)
    small_rows = small_rows[:, mixer_part : mixer_part + LANES].astype(F32)
    summed, at = [], 0
    for piece in pieces:
        summed.append(flat[at : at + piece.size].reshape(piece.shape))
        at += piece.size

    return (
        unshuffled(result)[None],
        unshuffled(grad_inputs.astype(BF16))[None],
        unshuffled(summed[0][None])[0],
        mixer_back[:, :key_width],
        mixer_back[:, key_width : 2 * key_width],
        mixer_back[:, 2 * key_width :],
        small_rows[:, :heads],
        small_rows[:, heads : 2 * heads],
        outgate_grad,
        summed[1],
        summed[2],
        summed[3],
        summed[4],
        summed[5],
        output_grad,
        unshuffled(summed[6][None])[0],
        gate_grad,
        up_grad,
        down_grad,
    )


def solution(mesh):
    rows, places = mesh.shape["dp"], mesh.shape["seq"]
    fine = Mesh(mesh.devices.reshape(rows, places // 2, 2), ("dp", "zq", "c"))
    tokens = P("dp", ("zq", "c"), None)
    owned = P(("dp", "zq", "c"), None)
    return jax.shard_map(
        local,
        mesh=fine,
        in_specs=(tokens, P("dp", ("zq", "c")), tokens, P())
        + (owned,) * 6
        + (P(),) * 5
        + (owned, P(), owned, owned, owned),
        out_specs=(tokens, tokens, P())
        + (owned,) * 6
        + (P(),) * 5
        + (owned, P(), owned, owned, owned),
        check_vma=False,
    )
```

```python
from functools import partial

import jax
import jax.numpy as jnp
from jax import lax
from jax.experimental import pallas as pl
from jax.experimental.pallas import tpu as pltpu
from jax.sharding import Mesh
from jax.sharding import PartitionSpec as P

CONV = 4
EPSILON = 1e-06
EXACT = lax.Precision.HIGHEST
BF16 = jnp.bfloat16
F32 = jnp.float32
BY_MESH = pl.DeviceIdType.MESH
LANES = 128
PIECES = 4
CHUNKS = 4
RIM = 16


def rms_scale(values):
    return values * lax.rsqrt(jnp.mean(values * values, axis=-1, keepdims=True) + EPSILON)


def swiglu(gate_values, up_values):
    return jax.nn.silu(gate_values) * up_values


def mm(left, right, over=(1, 0)):
    return lax.dot_general(
        left, right, (((over[0],), (over[1],)), ((), ())), preferred_element_type=F32
    )


def exact(left, right, over=(1, 0)):
    return lax.dot_general(
        left,
        right,
        (((over[0],), (over[1],)), ((), ())),
        precision=EXACT,
        preferred_element_type=F32,
    )


def place():
    return lax.axis_index("dp"), lax.axis_index("zq"), lax.axis_index("c")


def greet(peers):
    barrier = pltpu.get_barrier_semaphore()
    for peer in peers:
        pl.semaphore_signal(barrier, inc=1, device_id=peer, device_id_type=BY_MESH)
    pl.semaphore_wait(barrier, len(peers))


def remote(source, target, send, recv, peer):
    return pltpu.make_async_remote_copy(
        src_ref=source,
        dst_ref=target,
        send_sem=send,
        recv_sem=recv,
        device_id=peer,
        device_id_type=BY_MESH,
    )


def plane_offsets(rows):
    return [(k, flip) for k in range(rows) for flip in (0, 1) if (k, flip) != (0, 0)]


def plane_peer(offset, rows):
    d, z, c = place()
    k, flip = offset
    return (lax.rem(d + k, rows), z, 1 - c if flip else c)


def swap_kernel(rows, x_ref, o_ref, own, send, recv):
    d, z, c = place()
    me = d * 2 + c
    offsets = plane_offsets(rows)
    greet([plane_peer(offset, rows) for offset in offsets])
    copies = []
    for i, offset in enumerate(offsets):
        peer = plane_peer(offset, rows)
        copy = remote(
            x_ref.at[peer[0] * 2 + peer[2]], o_ref.at[me], send.at[i], recv.at[i], peer
        )
        copy.start()
        copies.append(copy)
    keep = pltpu.make_async_copy(x_ref.at[me], o_ref.at[me], own)
    keep.start()
    keep.wait()
    for copy in copies:
        copy.wait()


def spread_kernel(rows, x_ref, o_ref, own, send, recv, pair_send, pair_recv):
    d, z, c = place()
    me = d * 2 + c
    pair = (d, z, 1 - c)
    others = [(lax.rem(d + k, rows), z, c) for k in range(1, rows)]
    greet(others + [pair])
    copies = []
    for i, peer in enumerate(others):
        copy = remote(x_ref, o_ref.at[me], send.at[i], recv.at[i], peer)
        copy.start()
        copies.append(copy)
    hand = remote(x_ref, o_ref.at[me], pair_send.at[0], pair_recv.at[0], pair)
    hand.start()
    keep = pltpu.make_async_copy(x_ref, o_ref.at[me], own)
    keep.start()
    hands = [hand]
    for i, copy in enumerate(copies):
        copy.wait_recv()
        origin = lax.rem(d + rows - (i + 1), rows) * 2 + c
        hand = remote(
            o_ref.at[origin], o_ref.at[origin], pair_send.at[i + 1], pair_recv.at[i + 1], pair
        )
        hand.start()
        hands.append(hand)
    keep.wait()
    for copy in copies:
        copy.wait_send()
    for hand in hands:
        hand.wait()


def fold_kernel(
    rows, x_ref, o_ref, mine, theirs, load, pair_send, pair_recv, send, recv, own
):
    d, z, c = place()
    pair = (d, z, 1 - c)
    others = [(lax.rem(d + k, rows), z, c) for k in range(1, rows)]
    greet(others + [pair])
    order = [lax.rem(d + k, rows) for k in range(1, rows)] + [d]
    hands, loads = [], []
    for i, to in enumerate(order):
        hand = remote(
            x_ref.at[to * 2 + (1 - c)], theirs.at[i], pair_send.at[i], pair_recv.at[i], pair
        )
        hand.start()
        hands.append(hand)
        copy = pltpu.make_async_copy(x_ref.at[to * 2 + c], mine.at[i], load.at[i])
        copy.start()
        loads.append(copy)
    copies = []
    for i in range(rows):
        loads[i].wait()
        hands[i].wait_recv()
        mine[i] = (mine[i].astype(F32) + theirs[i].astype(F32)).astype(BF16)
        if i < rows - 1:
            copy = remote(mine.at[i], o_ref.at[d], send.at[i], recv.at[i], others[i])
        else:
            copy = pltpu.make_async_copy(mine.at[i], o_ref.at[d], own)
        copy.start()
        copies.append(copy)
    for hand in hands:
        hand.wait_send()
    for copy in copies:
        copy.wait()


def slab_pieces(widths, slab, t):
    at, end, base = t * slab, (t + 1) * slab, 0
    for source, width in enumerate(widths):
        low, high = max(at, base), min(end, base + width)
        if low < high:
            yield source, low - base, low - at, high - low
        base += width


def start_kernel(rows, count, hidden_ref, grad_ref, gain_ref, decay_ref, beta_ref, *refs):
    weight_refs = refs[:8]
    all_ref, *side_outs = refs[8:11]
    one_out_ref, two_out_ref, hidden_out_ref, one_ref, two_ref = refs[11:16]
    raws, cut_ref, sides = refs[16:24], refs[24], refs[25:27]
    (
        load,
        own,
        deal_send,
        deal_recv,
        side_send,
        side_recv,
        round_send,
        round_recv,
        pair_send,
        pair_recv,
        up_send,
        up_recv,
        down_send,
        down_recv,
    ) = refs[27:]
    loads = [
        pltpu.make_async_copy(weight, raw, load.at[i])
        for i, (weight, raw) in enumerate(zip(weight_refs, raws))
    ]
    for copy in loads:
        copy.start()
    d, z, c = place()
    me = d * 2 + c
    group = 2 * rows
    pair = (d, z, 1 - c)
    others = [(lax.rem(d + k, rows), z, c) for k in range(1, rows)]
    above = (d, lax.rem(z + 1, count), c)
    below = (d, lax.rem(z + count - 1, count), c)
    has_above, has_below = z < count - 1, z > 0
    offsets = plane_offsets(rows)
    barrier = pltpu.get_barrier_semaphore()
    for offset in offsets:
        pl.semaphore_signal(
            barrier, inc=1, device_id=plane_peer(offset, rows), device_id_type=BY_MESH
        )

    @pl.when(has_above)
    def _():
        pl.semaphore_signal(barrier, inc=1, device_id=above, device_id_type=BY_MESH)

    @pl.when(has_below)
    def _():
        pl.semaphore_signal(barrier, inc=1, device_id=below, device_id_type=BY_MESH)

    owned = raws[0].shape[0]
    wide = cut_ref.shape[2]
    heads = decay_ref.shape[1]
    back = raws[3].shape[1] // group
    slab = wide - LANES - back
    for copy in loads[:4]:
        copy.wait()
    widths = [raw.shape[1] for raw in raws[:3]]
    for t in range(group):
        for source, at, to, size in slab_pieces(widths, slab, t):
            cut_ref[t, :, to : to + size] = raws[source][:, at : at + size].astype(BF16)
        cut_ref[t, :, slab : slab + back] = raws[3][:, t * back : (t + 1) * back].astype(BF16)
        cut_ref[t, :, slab + back :] = jnp.concatenate(
            [decay_ref[...], beta_ref[...], jnp.zeros((owned, LANES - 2 * heads), F32)], axis=1
        ).astype(BF16)
    pl.semaphore_wait(
        barrier, len(offsets) + has_above.astype(jnp.int32) + has_below.astype(jnp.int32)
    )

    def deal(source, target, send, recv):
        copies = []
        for i, offset in enumerate(offsets):
            peer = plane_peer(offset, rows)
            copy = remote(
                source.at[peer[0] * 2 + peer[2]], target.at[me], send.at[i], recv.at[i], peer
            )
            copy.start()
            copies.append(copy)
        return copies

    def origin(offset):
        k, flip = offset
        return lax.rem(d + rows - k, rows) * 2 + (1 - c if flip else c)

    def passed(k, i, block, upward):
        at = z - k if upward else z + k
        at = lax.rem(at + count, count)
        send, recv = (up_send, up_recv) if upward else (down_send, down_recv)
        return remote(
            all_ref.at[at, block],
            all_ref.at[at, block],
            send.at[k, i],
            recv.at[k, i],
            above if upward else below,
        )

    def give(k, i, block):
        @pl.when(has_above & (z - k >= 0))
        def _():
            passed(k, i, block, True).start()

        @pl.when(has_below & (z + k <= count - 1))
        def _():
            passed(k, i, block, False).start()

    def take(k, i, block):
        @pl.when(z - k - 1 >= 0)
        def _():
            passed(k, i, block, True).wait_recv()

        @pl.when(z + k + 1 <= count - 1)
        def _():
            passed(k, i, block, False).wait_recv()

    def given(k, i, block):
        @pl.when(has_above & (z - k >= 0))
        def _():
            passed(k, i, block, True).wait_send()

        @pl.when(has_below & (z + k <= count - 1))
        def _():
            passed(k, i, block, False).wait_send()

    dealt = deal(cut_ref, all_ref.at[z], deal_send, deal_recv)
    keep = pltpu.make_async_copy(cut_ref.at[me], all_ref.at[z, me], own.at[0])
    keep.start()
    keep.wait()
    blocks = [me] + [origin(offset) for offset in offsets]
    give(0, 0, me)
    run = 2 * owned
    width = hidden_ref.shape[1]

    def moved(values):
        return jnp.concatenate(
            [
                values[:, (b * count + a) * run : (b * count + a + 1) * run]
                for a in range(count)
                for b in range(rows)
            ],
            axis=1,
        )

    hidden = moved(hidden_ref[...])
    hidden_out_ref[...] = hidden
    one_ref[...] = (rms_scale(hidden.astype(F32)) * moved(gain_ref[...])).astype(BF16)
    two_ref[...] = moved(grad_ref[...])
    rounds = []
    for j, (source, target) in enumerate(((one_ref, one_out_ref), (two_ref, two_out_ref))):
        copies = []
        for i, peer in enumerate(others):
            copies.append(
                remote(source, target.at[me], round_send.at[j, i], round_recv.at[j, i], peer)
            )
        copies.append(
            remote(source, target.at[me], pair_send.at[j, 0], pair_recv.at[j, 0], pair)
        )
        rounds.append(copies)
    for i, copy in enumerate(dealt):
        copy.wait_recv()
        give(0, i + 1, blocks[i + 1])
    keeps = [
        pltpu.make_async_copy(one_ref, one_out_ref.at[me], own.at[1]),
        pltpu.make_async_copy(two_ref, two_out_ref.at[me], own.at[2]),
    ]
    for copy in rounds[0] + keeps:
        copy.start()
    for copy in loads[4:]:
        copy.wait()
    deals = []
    for j, (laid, side, side_out) in enumerate(zip((raws[4:6], raws[6:]), sides, side_outs)):
        for t in range(group):
            at = 0
            for raw in laid:
                size = raw.shape[1] // group
                side[t, :, at : at + size] = raw[:, t * size : (t + 1) * size].astype(BF16)
                at += size
        deals += deal(side, side_out, side_send.at[j], side_recv.at[j])
        keep = pltpu.make_async_copy(side.at[me], side_out.at[me], own.at[3 + j])
        keep.start()
        keeps.append(keep)
    for copy in rounds[1]:
        copy.start()
    hands = []
    for k in range(count - 1):
        for i, block in enumerate(blocks):
            take(k, i, block)
            if k < count - 2:
                give(k + 1, i, block)
        if k < 2:
            target = (one_out_ref, two_out_ref)[k]
            for i, copy in enumerate(rounds[k][:-1]):
                copy.wait_recv()
                at = lax.rem(d + rows - (i + 1), rows) * 2 + c
                hand = remote(
                    target.at[at], target.at[at], pair_send.at[k, i + 1], pair_recv.at[k, i + 1], pair
                )
                hand.start()
                hands.append(hand)
    for copy in keeps:
        copy.wait()
    for copy in dealt:
        copy.wait_send()
    for copies in rounds:
        for copy in copies[:-1]:
            copy.wait_send()
        copies[-1].wait()
    for copy in hands + deals:
        copy.wait()
    for k in range(count - 1):
        for i, block in enumerate(blocks):
            given(k, i, block)


def turn_kernel(rows, backward, x_ref, gain_ref, base_ref, *refs):
    if backward:
        middle_ref, extra_ref, out_ref, all_ref, sums_ref, paired_ref = refs[:6]
        *scratch, extra, extra_load, extra_send, extra_recv = refs[6:]
    else:
        out_ref, all_ref = refs[:2]
        scratch = refs[2:]
    (
        mine,
        theirs,
        stage,
        land,
        low,
        load,
        fold_pair_send,
        fold_pair_recv,
        fold_send,
        fold_recv,
        own,
        send,
        recv,
        pair_send,
        pair_recv,
    ) = scratch
    d, z, c = place()
    me = d * 2 + c
    pair = (d, z, 1 - c)
    others = [(lax.rem(d + k, rows), z, c) for k in range(1, rows)]
    greet(others + [pair])
    order = [lax.rem(d + k, rows) for k in range(1, rows)] + [d]
    step = x_ref.shape[1] // CHUNKS
    parts = [pl.ds(j * step, step) for j in range(CHUNKS)]
    hands, loads = {}, {}
    for j, part in enumerate(parts):
        for i, to in enumerate(order):
            hands[j, i] = remote(
                x_ref.at[to * 2 + (1 - c), part],
                theirs.at[i, part],
                fold_pair_send.at[j, i],
                fold_pair_recv.at[j, i],
                pair,
            )
            hands[j, i].start()
            loads[j, i] = pltpu.make_async_copy(
                x_ref.at[to * 2 + c, part], mine.at[i, part], load.at[j, i]
            )
            loads[j, i].start()
    folds, extras = {}, []
    if backward:
        for i, to in enumerate(order):
            extras.append(
                (
                    remote(
                        extra_ref.at[to * 2 + (1 - c)],
                        extra.at[i],
                        extra_send.at[i],
                        extra_recv.at[i],
                        pair,
                    ),
                    pltpu.make_async_copy(
                        extra_ref.at[to * 2 + c], paired_ref.at[i], extra_load.at[i]
                    ),
                )
            )
    for j, part in enumerate(parts):
        for i in range(rows):
            loads[j, i].wait()
            hands[j, i].wait_recv()
            if i < rows - 1:
                stage[i, part] = (mine[i, part] + theirs[i, part]).astype(BF16)
                folds[j, i] = remote(
                    stage.at[i, part],
                    land.at[i, part],
                    fold_send.at[j, i],
                    fold_recv.at[j, i],
                    others[i],
                )
                folds[j, i].start()
    for pieces in extras:
        for copy in pieces:
            copy.start()
    gain = gain_ref[...]
    sends, keeps = {}, []
    if backward:
        sums_ref[...] = jnp.zeros_like(sums_ref)
    for j, part in enumerate(parts):
        total = mine[rows - 1, part] + theirs[rows - 1, part]
        for i in range(rows - 1):
            folds[j, i].wait_recv()
            total = total + land[i, part].astype(F32)
        if backward:
            middle = middle_ref[part, :]
            scale = lax.rsqrt(jnp.mean(middle * middle, axis=-1, keepdims=True) + EPSILON)
            normed = middle * scale
            sums_ref[...] += jnp.sum(total * normed, axis=0, keepdims=True)
            inner = total * gain
            result = base_ref[part, :].astype(F32) + scale * (
                inner - normed * jnp.mean(inner * normed, axis=-1, keepdims=True)
            )
            out_ref[part, :] = result
            low[part, :] = result.astype(BF16)
        else:
            result = base_ref[part, :].astype(F32) + total
            out_ref[part, :] = result
            low[part, :] = (rms_scale(result) * gain).astype(BF16)
        for i, peer in enumerate(others + [pair]):
            at = (send.at[j, i], recv.at[j, i])
            if i == rows - 1:
                at = (pair_send.at[j, rows - 1], pair_recv.at[j, rows - 1])
            sends[j, i] = remote(low.at[part], all_ref.at[me, part], *at, peer)
            sends[j, i].start()
        keep = pltpu.make_async_copy(low.at[part], all_ref.at[me, part], own.at[j])
        keep.start()
        keeps.append(keep)
    for i, (hand, copy) in enumerate(extras):
        copy.wait()
        hand.wait_recv()
        paired_ref[i] = (paired_ref[i].astype(F32) + extra[i].astype(F32)).astype(BF16)
    for hand, _ in extras:
        hand.wait_send()
    for j, part in enumerate(parts):
        for i in range(rows - 1):
            sends[j, i].wait_recv()
            at = lax.rem(d + rows - (i + 1), rows) * 2 + c
            hand = remote(
                all_ref.at[at, part],
                all_ref.at[at, part],
                pair_send.at[j, i],
                pair_recv.at[j, i],
                pair,
            )
            hand.start()
            hands[j, rows + i] = hand
    for keep in keeps:
        keep.wait()
    for (j, i), hand in hands.items():
        hand.wait_send()
        if i >= rows:
            hand.wait_recv()
    for copy in folds.values():
        copy.wait_send()
    for (j, i), copy in sends.items():
        copy.wait_send()
        if i == rows - 1:
            copy.wait_recv()


def greet_plane_and_line(rows, count):
    d, z, c = place()
    spot, before, after = neighbours(count)
    offsets = plane_offsets(rows)
    lower, upper = (c == 0) & (z > 0), (c == 1) & (z < count - 1)
    barrier = pltpu.get_barrier_semaphore()
    for offset in offsets:
        pl.semaphore_signal(
            barrier, inc=1, device_id=plane_peer(offset, rows), device_id_type=BY_MESH
        )

    @pl.when(lower)
    def _():
        pl.semaphore_signal(barrier, inc=1, device_id=before, device_id_type=BY_MESH)

    @pl.when(upper)
    def _():
        pl.semaphore_signal(barrier, inc=1, device_id=after, device_id_type=BY_MESH)

    pl.semaphore_wait(
        barrier, len(offsets) + lower.astype(jnp.int32) + upper.astype(jnp.int32)
    )


def swap_on_kernel(rows, count, x_ref, o_ref, rim_ref, land, own, send, recv, rim_send, rim_recv):
    d, z, c = place()
    me = d * 2 + c
    spot, before, after = neighbours(count)
    greet_plane_and_line(rows, count)
    copies = []
    for i, offset in enumerate(plane_offsets(rows)):
        peer = plane_peer(offset, rows)
        copy = remote(
            x_ref.at[peer[0] * 2 + peer[2]], o_ref.at[me], send.at[i], recv.at[i], peer
        )
        copy.start()
        copies.append(copy)
    keep = pltpu.make_async_copy(x_ref.at[me], o_ref.at[me], own)
    keep.start()
    keep.wait()
    for copy in copies:
        copy.wait_recv()
    size = x_ref.shape[1]
    rim = remote(o_ref.at[:, pl.ds(size - RIM, RIM)], land, rim_send, rim_recv, after)
    gives, takes = spot < 2 * count - 1, spot > 0

    @pl.when(gives)
    def _():
        rim.start()

    @pl.when(takes)
    def _():
        rim.wait_recv()

    @pl.when(jnp.logical_not(takes))
    def _():
        land[...] = jnp.zeros_like(land)

    rim_ref[...] = land[...]
    for copy in copies:
        copy.wait_send()

    @pl.when(gives)
    def _():
        rim.wait_send()


def swap_back_kernel(
    rows,
    count,
    x_ref,
    tail_ref,
    rim_ref,
    small_ref,
    o_ref,
    land,
    fixed,
    own,
    send,
    recv,
    rim_send,
    rim_recv,
):
    d, z, c = place()
    me = d * 2 + c
    spot, before, after = neighbours(count)
    greet_plane_and_line(rows, count)
    size, part = x_ref.shape[1:]
    wide = o_ref.shape[2]
    rim = remote(rim_ref, land, rim_send, rim_recv, before)
    gives, takes = spot > 0, spot < 2 * count - 1

    @pl.when(gives)
    def _():
        rim.start()

    body, end = pl.ds(0, size - RIM), pl.ds(size - RIM, RIM)
    left, right = pl.ds(0, part), pl.ds(part, wide - part)
    copies = []
    for i, offset in enumerate(plane_offsets(rows)):
        peer = plane_peer(offset, rows)
        to = peer[0] * 2 + peer[2]
        copies.append(
            (
                remote(
                    x_ref.at[to, body], o_ref.at[me, body, left], send.at[0, i], recv.at[0, i], peer
                ),
                remote(small_ref, o_ref.at[me, :, right], send.at[1, i], recv.at[1, i], peer),
                remote(fixed.at[to], o_ref.at[me, end, left], send.at[2, i], recv.at[2, i], peer),
            )
        )
        copies[-1][0].start()
        copies[-1][1].start()
    keeps = [
        pltpu.make_async_copy(x_ref.at[me, body], o_ref.at[me, body, left], own.at[0]),
        pltpu.make_async_copy(small_ref, o_ref.at[me, :, right], own.at[1]),
        pltpu.make_async_copy(fixed.at[me], o_ref.at[me, end, left], own.at[2]),
    ]
    keeps[0].start()
    keeps[1].start()

    @pl.when(takes)
    def _():
        rim.wait_recv()

    @pl.when(jnp.logical_not(takes))
    def _():
        land[...] = jnp.zeros_like(land)

    fixed[...] = (tail_ref[...] + land[...].astype(F32)).astype(BF16)
    keeps[2].start()
    for group in copies:
        group[2].start()
    for keep in keeps:
        keep.wait()
    for group in copies:
        for copy in group:
            copy.wait()

    @pl.when(gives)
    def _():
        rim.wait_send()


def column_kernel(count, x_ref, o_ref, own, send, recv):
    d, z, c = place()
    others = [(d, lax.rem(z + k, count), c) for k in range(1, count)]
    greet(others)
    copies = []
    for i, peer in enumerate(others):
        copy = remote(x_ref, o_ref.at[z], send.at[i], recv.at[i], peer)
        copy.start()
        copies.append(copy)
    keep = pltpu.make_async_copy(x_ref, o_ref.at[z], own)
    keep.start()
    keep.wait()
    for copy in copies:
        copy.wait()


def neighbours(count):
    d, z, c = place()
    after = (d, lax.rem(z + c, count), 1 - c)
    before = (d, lax.rem(z + c - 1 + count, count), 1 - c)
    spot = z * 2 + c
    return spot, before, after


def greet_chain(count):
    spot, before, after = neighbours(count)
    barrier = pltpu.get_barrier_semaphore()

    @pl.when(spot > 0)
    def _():
        pl.semaphore_signal(barrier, inc=1, device_id=before, device_id_type=BY_MESH)

    @pl.when(spot < 2 * count - 1)
    def _():
        pl.semaphore_signal(barrier, inc=1, device_id=after, device_id_type=BY_MESH)

    pl.semaphore_wait(
        barrier,
        (spot > 0).astype(jnp.int32) + (spot < 2 * count - 1).astype(jnp.int32),
    )


def hop_kernel(count, forward, x_ref, o_ref, send, recv):
    spot, before, after = neighbours(count)
    greet_chain(count)
    if forward:
        gives, takes, to = spot < 2 * count - 1, spot > 0, after
    else:
        gives, takes, to = spot > 0, spot < 2 * count - 1, before
    copy = remote(x_ref, o_ref, send, recv, to)

    @pl.when(gives)
    def _():
        copy.start()

    @pl.when(takes)
    def _():
        copy.wait_recv()

    @pl.when(jnp.logical_not(takes))
    def _():
        o_ref[...] = jnp.zeros_like(o_ref)

    @pl.when(gives)
    def _():
        copy.wait_send()


def chain_kernel(
    count,
    rows,
    heads,
    sides,
    forward,
    high_ref,
    low_ref,
    add_ref,
    *refs,
):
    side_refs, (o_ref, *side_out_refs) = refs[:sides], refs[sides : 2 * sides + 1]
    land, stage, send, recv, own, side_send, side_recv = refs[2 * sides + 1 :]
    d, z, c = place()
    me = d * 2 + c
    spot, before, after = neighbours(count)
    offsets = plane_offsets(rows)
    barrier = pltpu.get_barrier_semaphore()
    for offset in offsets:
        pl.semaphore_signal(
            barrier, inc=1, device_id=plane_peer(offset, rows), device_id_type=BY_MESH
        )

    @pl.when((c == 0) & (z > 0))
    def _():
        pl.semaphore_signal(barrier, inc=1, device_id=before, device_id_type=BY_MESH)

    @pl.when((c == 1) & (z < count - 1))
    def _():
        pl.semaphore_signal(barrier, inc=1, device_id=after, device_id_type=BY_MESH)

    pl.semaphore_wait(
        barrier,
        len(offsets)
        + ((c == 0) & (z > 0)).astype(jnp.int32)
        + ((c == 1) & (z < count - 1)).astype(jnp.int32),
    )
    waits = []
    for j in range(sides):
        if side_refs[j].shape[0] == rows:
            for i in range(rows - 1):
                waits.append(
                    remote(
                        side_refs[j].at[i],
                        side_out_refs[j].at[i],
                        side_send.at[j, i],
                        side_recv.at[j, i],
                        (lax.rem(d + i + 1, rows), z, c),
                    )
                )
            waits.append(
                pltpu.make_async_copy(
                    side_refs[j].at[rows - 1], side_out_refs[j].at[rows - 1], own.at[j]
                )
            )
            continue
        for i, offset in enumerate(offsets):
            peer = plane_peer(offset, rows)
            waits.append(
                remote(
                    side_refs[j].at[peer[0] * 2 + peer[2]],
                    side_out_refs[j].at[me],
                    side_send.at[j, i],
                    side_recv.at[j, i],
                    peer,
                )
            )
        waits.append(
            pltpu.make_async_copy(side_refs[j].at[me], side_out_refs[j].at[me], own.at[j])
        )
    for copy in waits:
        copy.start()
    if forward:
        gives, takes, to = spot < 2 * count - 1, spot > 0, after
    else:
        gives, takes, to = spot > 0, spot < 2 * count - 1, before
    part = o_ref.shape[2] // PIECES
    copies = [
        remote(stage.at[i], land.at[i], send.at[i], recv.at[i], to)
        for i in range(heads * PIECES)
    ]
    for h in range(heads):
        for j in range(PIECES):
            i = h * PIECES + j
            columns = slice(j * part, (j + 1) * part)

            @pl.when(jnp.logical_not(takes))
            def _():
                land[i] = jnp.zeros_like(land[i])

            @pl.when(takes)
            def _():
                copies[i].wait_recv()

            @pl.when(gives)
            def _():
                state = land[i]
                leaving = add_ref[h, :, columns] + mm(high_ref[h], state) + mm(low_ref[h], state)
                stage[i] = leaving.astype(BF16)
                copies[i].start()

    for copy in copies:

        @pl.when(gives)
        def _():
            copy.wait_send()

    for h in range(heads):
        for j in range(PIECES):
            o_ref[h, :, j * part : (j + 1) * part] = land[h * PIECES + j]
    for copy in waits:
        copy.wait()


ANY = pl.BlockSpec(memory_space=pl.ANY)
IN_VMEM = pl.BlockSpec(memory_space=pltpu.VMEM)
IN_HBM = pl.BlockSpec(memory_space=pltpu.HBM)


def dma(*shape):
    return pltpu.SemaphoreType.DMA(shape)


def comm_call(body, out, scratch, ident, operands, spec=ANY, cost=30):
    return pl.pallas_call(
        body,
        out_shape=out,
        in_specs=[spec] * len(operands),
        out_specs=spec,
        scratch_shapes=scratch,
        compiler_params=pltpu.CompilerParams(collective_id=ident, has_side_effects=True),
        cost_estimate=pl.CostEstimate(
            flops=0, bytes_accessed=int(cost * 3.0e6), transcendentals=0
        ),
    )(*operands)


def swap(x, ident):
    rows = lax.axis_size("dp")
    links = 2 * rows - 1
    return comm_call(
        partial(swap_kernel, rows),
        jax.ShapeDtypeStruct(x.shape, x.dtype),
        [pltpu.SemaphoreType.DMA, dma(links), dma(links)],
        ident,
        (x,),
    )


def spread(x, ident):
    rows = lax.axis_size("dp")
    return comm_call(
        partial(spread_kernel, rows),
        jax.ShapeDtypeStruct((2 * rows,) + x.shape, x.dtype),
        [pltpu.SemaphoreType.DMA, dma(rows - 1), dma(rows - 1), dma(rows), dma(rows)],
        ident,
        (x,),
    )


def fold(x, ident):
    rows = lax.axis_size("dp")
    part = (rows,) + x.shape[1:]
    received = comm_call(
        partial(fold_kernel, rows),
        jax.ShapeDtypeStruct(part, x.dtype),
        [
            pltpu.VMEM(part, x.dtype),
            pltpu.VMEM(part, x.dtype),
            dma(rows),
            dma(rows),
            dma(rows),
            dma(rows - 1),
            dma(rows - 1),
            pltpu.SemaphoreType.DMA,
        ],
        ident,
        (x,),
    )
    return jnp.sum(received.astype(F32), axis=0)


def turn(x, gain, base, more, ident):
    rows = lax.axis_size("dp")
    group, length, width = x.shape
    backward = bool(more)
    part, sent = (rows, length, width), (rows - 1, length, width)
    return pl.pallas_call(
        partial(turn_kernel, rows, backward),
        out_shape=[
            jax.ShapeDtypeStruct((length, width), F32),
            jax.ShapeDtypeStruct((group, length, width), BF16),
        ]
        + (
            [jax.ShapeDtypeStruct((1, width), F32), jax.ShapeDtypeStruct(part, BF16)]
            if backward
            else []
        ),
        in_specs=[ANY, IN_VMEM, IN_VMEM] + ([IN_VMEM, ANY] if backward else []),
        out_specs=[IN_VMEM, ANY] + ([IN_VMEM, IN_VMEM] if backward else []),
        scratch_shapes=[
            pltpu.VMEM(part, F32),
            pltpu.VMEM(part, F32),
            pltpu.VMEM(sent, BF16),
            pltpu.VMEM(sent, BF16),
            pltpu.VMEM((length, width), BF16),
        ]
        + [dma(CHUNKS, rows)] * 3
        + [dma(CHUNKS, rows - 1)] * 2
        + [dma(CHUNKS)]
        + [dma(CHUNKS, rows - 1)] * 2
        + [dma(CHUNKS, rows)] * 2
        + ([pltpu.VMEM(part, BF16)] + [dma(rows)] * 3 if backward else []),
        compiler_params=pltpu.CompilerParams(collective_id=ident, has_side_effects=True),
        cost_estimate=pl.CostEstimate(
            flops=0, bytes_accessed=150_000_000, transcendentals=0
        ),
    )(x, gain, base, *more)


def swap_on(x, ident):
    rows, count = lax.axis_size("dp"), lax.axis_size("zq")
    group, length, part = x.shape
    links = 2 * rows - 1
    return pl.pallas_call(
        partial(swap_on_kernel, rows, count),
        out_shape=[
            jax.ShapeDtypeStruct(x.shape, x.dtype),
            jax.ShapeDtypeStruct((group, RIM, part), x.dtype),
        ],
        in_specs=[ANY],
        out_specs=[ANY, IN_VMEM],
        scratch_shapes=[
            pltpu.VMEM((group, RIM, part), x.dtype),
            pltpu.SemaphoreType.DMA,
            dma(links),
            dma(links),
            pltpu.SemaphoreType.DMA,
            pltpu.SemaphoreType.DMA,
        ],
        compiler_params=pltpu.CompilerParams(collective_id=ident, has_side_effects=True),
        cost_estimate=pl.CostEstimate(flops=0, bytes_accessed=90_000_000, transcendentals=0),
    )(x)


def swap_back(x, tail, rim, small, ident):
    rows, count = lax.axis_size("dp"), lax.axis_size("zq")
    group, length, part = x.shape
    links = 2 * rows - 1
    return pl.pallas_call(
        partial(swap_back_kernel, rows, count),
        out_shape=jax.ShapeDtypeStruct((group, length, part + small.shape[1]), x.dtype),
        in_specs=[ANY, IN_VMEM, ANY, ANY],
        out_specs=ANY,
        scratch_shapes=[
            pltpu.VMEM((group, RIM, part), x.dtype),
            pltpu.VMEM((group, RIM, part), x.dtype),
            dma(3),
            dma(3, links),
            dma(3, links),
            pltpu.SemaphoreType.DMA,
            pltpu.SemaphoreType.DMA,
        ],
        compiler_params=pltpu.CompilerParams(collective_id=ident, has_side_effects=True),
        cost_estimate=pl.CostEstimate(flops=0, bytes_accessed=90_000_000, transcendentals=0),
    )(x, tail, rim, small)


def begin(hidden, grad, gain, decay, beta, weights, ident):
    rows, count = lax.axis_size("dp"), lax.axis_size("zq")
    group, links = 2 * rows, 2 * rows - 1
    owned = decay.shape[0]
    parts = [weight.shape[1] // group for weight in weights]
    wide = sum(parts[:4]) + LANES
    cut = (group, owned, wide)
    side_shapes = [(group, owned, sum(parts[4:6])), (group, owned, sum(parts[6:]))]
    assert count > 2
    tokens = jax.ShapeDtypeStruct(hidden.shape, BF16)
    everyone = jax.ShapeDtypeStruct((group,) + hidden.shape, BF16)
    return pl.pallas_call(
        partial(start_kernel, rows, count),
        out_shape=[jax.ShapeDtypeStruct((count,) + cut, BF16)]
        + [jax.ShapeDtypeStruct(shape, BF16) for shape in side_shapes]
        + [everyone] * 2
        + [tokens] * 3,
        in_specs=[IN_VMEM] * 5 + [IN_HBM] * 8,
        out_specs=[ANY] * 5 + [IN_VMEM] * 3,
        scratch_shapes=[pltpu.VMEM(weight.shape, F32) for weight in weights]
        + [pltpu.VMEM(cut, BF16)]
        + [pltpu.VMEM(shape, BF16) for shape in side_shapes]
        + [
            dma(8),
            dma(5),
            dma(links),
            dma(links),
            dma(2, links),
            dma(2, links),
            dma(2, rows - 1),
            dma(2, rows - 1),
            dma(2, rows),
            dma(2, rows),
        ]
        + [dma(count - 1, group)] * 4,
        compiler_params=pltpu.CompilerParams(
            collective_id=ident, has_side_effects=True
        ),
        cost_estimate=pl.CostEstimate(
            flops=0, bytes_accessed=300_000_000, transcendentals=0
        ),
    )(hidden, grad, gain, decay, beta, *weights)


def column(x, ident):
    count = lax.axis_size("zq")
    return comm_call(
        partial(column_kernel, count),
        jax.ShapeDtypeStruct((count,) + x.shape, x.dtype),
        [pltpu.SemaphoreType.DMA, dma(count - 1), dma(count - 1)],
        ident,
        (x,),
    )


def hop(x, forward, ident):
    count = lax.axis_size("zq")
    return comm_call(
        partial(hop_kernel, count, forward),
        jax.ShapeDtypeStruct(x.shape, x.dtype),
        [pltpu.SemaphoreType.DMA, pltpu.SemaphoreType.DMA],
        ident,
        (x,),
        IN_VMEM,
    )


def chain(high, low, add, sides, forward, ident):
    rows, count = lax.axis_size("dp"), lax.axis_size("zq")
    heads, key_size, value_size = add.shape
    links = 2 * rows - 1
    pieces = (heads * PIECES, key_size, value_size // PIECES)
    return pl.pallas_call(
        partial(chain_kernel, count, rows, heads, len(sides), forward),
        out_shape=[jax.ShapeDtypeStruct(add.shape, BF16)]
        + [jax.ShapeDtypeStruct(side.shape, side.dtype) for side in sides],
        in_specs=[IN_VMEM] * 3 + [ANY] * len(sides),
        out_specs=[IN_VMEM] + [ANY] * len(sides),
        scratch_shapes=[
            pltpu.VMEM(pieces, BF16),
            pltpu.VMEM(pieces, BF16),
            dma(heads * PIECES),
            dma(heads * PIECES),
            dma(len(sides)),
            dma(len(sides), links),
            dma(len(sides), links),
        ],
        compiler_params=pltpu.CompilerParams(collective_id=ident, has_side_effects=True),
        cost_estimate=pl.CostEstimate(
            flops=0, bytes_accessed=200_000_000, transcendentals=0
        ),
    )(high, low, add, *sides)


def unit_lower_inverses(lows):
    shape = lows[0].shape
    row = lax.broadcasted_iota(jnp.int32, shape, 0)
    col = lax.broadcasted_iota(jnp.int32, shape, 1)

    def same(width):
        shift = width.bit_length() - 1
        return (row >> shift) == (col >> shift)

    def products(lefts, rights):
        return [exact(left, right) for left, right in zip(lefts, rights)]

    eye = (row == col).astype(F32)
    width = 8
    near = [jnp.where(same(width), low, 0.0) for low in lows]
    square = products(near, near)
    inverse = [eye - block for block in near]
    inverse = [x + y for x, y in zip(inverse, products(inverse, square))]
    square = products(square, square)
    inverse = [x + y for x, y in zip(inverse, products(inverse, square))]
    while width < shape[0]:
        picked = same(2 * width) & jnp.logical_not(same(width))
        cross = [jnp.where(picked, low, 0.0) for low in lows]
        inverse = [
            x - y for x, y in zip(inverse, products(inverse, products(cross, inverse)))
        ]
        width *= 2
    return inverse


def unit_parts(values):
    scale = lax.rsqrt(jnp.sum(values * values, axis=-1, keepdims=True) + EPSILON)
    return values * scale, scale


def unit_back(unit, scale, grad):
    return scale * (grad - unit * jnp.sum(unit * grad, axis=-1, keepdims=True))


def strict_lower(size):
    row = lax.broadcasted_iota(jnp.int32, (size, size), 0)
    col = lax.broadcasted_iota(jnp.int32, (size, size), 1)
    return (row > col).astype(F32)


def convolve(x_ref, rim_ref, taps_ref, same_ref, ext):
    size = x_ref.shape[1]
    ext[:RIM] = rim_ref[0].astype(F32)
    ext[RIM:] = x_ref[0].astype(F32)
    mixed = taps_ref[0:1] * ext[RIM:]
    for lag in range(1, CONV):
        mixed = mixed + taps_ref[lag : lag + 1] * ext[RIM - lag : RIM - lag + size] * (
            same_ref[:, lag : lag + 1]
        )
    return mixed


def convolve_back(grad, taps_ref, same_ref, ext, back):
    size = grad.shape[0]
    back[:RIM] = jnp.zeros((RIM, grad.shape[1]), F32)
    back[RIM:] = taps_ref[0:1] * grad
    sums = [jnp.sum(grad * ext[RIM:], axis=0, keepdims=True)]
    for lag in range(1, CONV):
        kept = grad * same_ref[:, lag : lag + 1]
        sums.append(
            jnp.sum(kept * ext[RIM - lag : RIM - lag + size], axis=0, keepdims=True)
        )
        back[RIM - lag : RIM - lag + size] += taps_ref[lag : lag + 1] * kept
    return jnp.concatenate(sums, axis=0)


def silu_parts(values):
    sig = jax.nn.sigmoid(values)
    return values * sig, sig * (1.0 + values * (1.0 - sig))


def chunk_forward_kernel(step, *refs):
    count = 4 * step
    pre_refs, rim_refs, tap_refs = refs[:count], refs[count : 2 * count], refs[2 * count : 3 * count]
    same_ref, lines_ref, decay_ref = refs[3 * count : 3 * count + 3]
    (
        inverse_ref,
        scores_ref,
        own_ref,
        effect_ref,
        offset_ref,
        high_ref,
        low_ref,
        back_high_ref,
        back_low_ref,
    ) = refs[3 * count + 3 : 3 * count + 12]
    ext = refs[3 * count + 12]
    heads, lows = [], []
    for u in range(step):
        active = []
        for i in range(4 * u, 4 * u + 4):
            mixed = convolve(pre_refs[i], rim_refs[i], tap_refs[i], same_ref, ext.at[i])
            active.append(silu_parts(mixed)[0])
        size, key_size = active[0].shape
        columns = lines_ref[u].T
        beta, start, tail = columns[:, 0:1], columns[:, 1:2], columns[:, 2:3]
        decay = decay_ref[u]
        query = unit_parts(active[0])[0] * key_size ** (-0.5)
        key = unit_parts(active[1])[0]
        values = jnp.concatenate(active[2:], axis=1)
        inner = exact(key, key, (1, 1))
        lows.append(beta * inner * (decay * strict_lower(size)))
        heads.append((query, key, values, beta, start, tail, decay))
    inverses = unit_lower_inverses(lows)
    row = lax.broadcasted_iota(jnp.int32, (key_size, key_size), 0)
    col = lax.broadcasted_iota(jnp.int32, (key_size, key_size), 1)
    for u in range(step):
        query, key, values, beta, start, tail, decay = heads[u]
        inverse = inverses[u]
        width = values.shape[1]
        scores = exact(query, key, (1, 1)) * decay
        update = exact(inverse, beta * values)
        reach = exact(inverse, (beta * start) * key)
        inverse_ref[u] = inverse
        scores_ref[u] = scores
        own_ref[:, u * width : (u + 1) * width] = exact(scores, update)
        effect_ref[u] = start * query - exact(scores, reach)
        last = tail * key
        offset_ref[u] = exact(last, update, (0, 0))
        transfer = jnp.where(row == col, start[size - 1 :, :], 0.0) - exact(
            last, reach, (0, 0)
        )
        for matrix, top_ref, rest_ref in (
            (transfer, high_ref, low_ref),
            (transfer.T, back_high_ref, back_low_ref),
        ):
            top = matrix.astype(BF16)
            top_ref[u] = top
            rest_ref[u] = (matrix - top.astype(F32)).astype(BF16)


def gate_forward_kernel(own_ref, effect_ref, state_ref, gate_ref, gain_ref, mixed_ref, gated_ref):
    mixed = own_ref[...] + exact(effect_ref[0], state_ref[0].astype(F32))
    mixed_ref[...] = mixed
    gate = gate_ref[...].astype(F32)
    gated_ref[...] = (
        rms_scale(mixed) * gain_ref[...] * (gate * jax.nn.sigmoid(gate))
    ).astype(BF16)


def gate_backward_kernel(
    mixed_ref, gate_ref, gain_ref, grad_ref, effect_ref, out_ref, gate_grad_ref, gain_grad_ref, add_ref
):
    mixed = mixed_ref[...]
    gate = gate_ref[...].astype(F32)
    grad = grad_ref[...].astype(F32)
    gain = gain_ref[...]
    scale = lax.rsqrt(jnp.mean(mixed * mixed, axis=-1, keepdims=True) + EPSILON)
    normed = mixed * scale
    sig = jax.nn.sigmoid(gate)
    act = gate * sig
    gain_grad_ref[0] = jnp.sum(grad * normed * act, axis=0, keepdims=True)
    gate_grad_ref[...] = (
        grad * normed * gain * (sig * (1.0 + gate * (1.0 - sig)))
    ).astype(BF16)
    inner = grad * gain * act
    mixed_grad = scale * (inner - normed * jnp.mean(inner * normed, axis=-1, keepdims=True))
    out_ref[...] = mixed_grad
    add_ref[0] = exact(effect_ref[0], mixed_grad, (0, 0))


def chunk_backward_kernel(heads, *refs):
    pre_refs, rim_refs, tap_refs = refs[:4], refs[4:8], refs[8:12]
    same_ref, lines_ref, decay_ref = refs[12:15]
    inverse_ref, scores_ref, state_ref, mixed_ref, ending_ref = refs[15:20]
    (
        grad_ref,
        grad_tail_ref,
        grad_rim_ref,
        taps_grad_ref,
        dlines_ref,
        ddecay_ref,
    ) = refs[20:26]
    ext, back = refs[26:]
    active, slopes = [], []
    for i in range(4):
        mixed = convolve(pre_refs[i], rim_refs[i], tap_refs[i], same_ref, ext.at[i])
        value, slope = silu_parts(mixed)
        active.append(value)
        slopes.append(slope)
    size, key_size = active[0].shape
    values = jnp.concatenate(active[2:], axis=1)
    columns = lines_ref[0].T
    beta, start, tail = columns[:, 0:1], columns[:, 1:2], columns[:, 2:3]
    decay, inverse, scores = decay_ref[0], inverse_ref[0], scores_ref[0]
    state = state_ref[0].astype(F32)
    ending = ending_ref[0].astype(F32)
    mixed_grad = mixed_ref[...]
    unit_q, scale_q = unit_parts(active[0])
    query = unit_q * key_size ** (-0.5)
    key, scale_k = unit_parts(active[1])
    below = strict_lower(size)
    inner = exact(key, key, (1, 1))
    raw = exact(query, key, (1, 1))
    recalled = exact(key, state)
    miss = values - start * recalled
    update = exact(inverse, beta * miss)
    mixed_state = exact(mixed_grad, state, (1, 1))
    last = tail * key
    dupdate = exact(scores, mixed_grad, (0, 0)) + exact(last, ending)
    dscores = exact(mixed_grad, update, (1, 1))
    dlast = exact(update, ending, (1, 1))
    dright = exact(inverse, dupdate, (0, 0))
    dlower = -exact(dright, update, (1, 1)) * below
    dscaled = dscores * decay
    dquery = start * mixed_state + exact(dscaled, key)
    dinner = beta * dlower * decay
    dkey = (
        tail * dlast
        + exact(dscaled, query, (0, 0))
        - exact((beta * start) * dright, state, (1, 1))
        + exact(dinner, key)
        + exact(dinner, key, (0, 0))
    )
    right_recalled = jnp.sum(dright * recalled, axis=-1, keepdims=True)
    dbeta = jnp.sum(dright * miss, axis=-1, keepdims=True) + jnp.sum(
        dlower * inner * decay, axis=-1, keepdims=True
    )
    final = jnp.sum(jnp.sum(ending * state, axis=-1, keepdims=True), axis=0, keepdims=True)
    row = lax.broadcasted_iota(jnp.int32, (size, 1), 0)
    dstart = (
        jnp.sum(query * mixed_state, axis=-1, keepdims=True)
        - beta * right_recalled
        + jnp.where(row == size - 1, final, 0.0)
    )
    dtail = jnp.sum(key * dlast, axis=-1, keepdims=True)
    dlines_ref[0] = jnp.concatenate(
        [dbeta, dstart, dtail, jnp.zeros((size, 5), F32)], axis=1
    ).T
    ddecay_ref[0] = dscores * raw + beta * dlower * inner
    dvalues = beta * dright
    grads = [
        unit_back(unit_q, scale_q, dquery * key_size ** (-0.5)),
        unit_back(key, scale_k, dkey),
        dvalues[:, :key_size],
        dvalues[:, key_size:],
    ]
    head = pl.program_id(0)
    per = grad_ref.shape[2] // key_size
    for i, block in enumerate((head, heads + head, 2 * heads + 2 * head, 2 * heads + 2 * head + 1)):
        sums = convolve_back(grads[i] * slopes[i], tap_refs[i], same_ref, ext.at[i], back)
        slab = block // per
        columns = pl.ds(pl.multiple_of((block % per) * key_size, key_size), key_size)
        grad_ref[slab, :, columns] = back[RIM:].astype(BF16)
        grad_tail_ref[slab, :, columns] = back[size:]
        grad_rim_ref[slab, :, columns] = back[:RIM].astype(BF16)
        taps_grad_ref[slab, 0:CONV, columns] = sums


def by_head(*shape):
    return pl.BlockSpec((1,) + shape, lambda h: (h, 0, 0))


def by_heads(step, *shape):
    return pl.BlockSpec((step,) + shape, lambda h: (h, 0, 0))


def by_columns(rows, width, offset=0):
    return pl.BlockSpec((rows, width), lambda h: (0, h + offset))


def head_call(body, heads, in_specs, out_specs, out_shape, operands, flops, scratch=()):
    return pl.pallas_call(
        body,
        scratch_shapes=scratch,
        grid=(heads,),
        in_specs=in_specs,
        out_specs=out_specs,
        out_shape=out_shape,
        cost_estimate=pl.CostEstimate(flops=flops, bytes_accessed=20_000_000, transcendentals=0),
    )(*operands)


def shaped(*shape, dtype=F32):
    return jax.ShapeDtypeStruct(shape, dtype)


def decays(segment, before, decay_pre, beta_pre, a_log):
    length = segment.shape[0]
    beta = jax.nn.sigmoid(beta_pre)
    decay_log = -jnp.exp(a_log) * jax.nn.softplus(decay_pre)
    order = jnp.arange(length)
    lower = order[:, None] >= order[None, :]
    running = exact(lower.astype(F32), decay_log).T
    live = (segment[:, None] == segment[None, :]) & lower
    gap = running[:, :, None] - running[:, None, :]
    decay = jnp.where(live, jnp.exp(jnp.where(live, gap, 0.0)), 0.0)
    start = jnp.exp(running) * (segment == before).astype(F32)
    live_last = segment == segment[-1]
    last_gap = running[:, -1:] - running
    tail = jnp.where(live_last, jnp.exp(jnp.where(live_last, last_gap, 0.0)), 0.0)
    filler = jnp.zeros((5,) + start.shape, F32)
    return jnp.moveaxis(jnp.concatenate([jnp.stack([beta.T, start, tail]), filler]), 0, 1), decay


def local(
    hidden_in,
    segment_ids,
    grad_out,
    attn_gain,
    w_query,
    w_key,
    w_value,
    w_decay,
    w_beta,
    w_outgate,
    a_log,
    conv_query,
    conv_key,
    conv_value,
    out_gain,
    w_output,
    mlp_gain,
    w_gate,
    w_up,
    w_down,
):
    rows, count = lax.axis_size("dp"), lax.axis_size("zq")
    group = 2 * rows
    segment = segment_ids[0]
    length, width = hidden_in.shape[1:]
    heads = a_log.shape[0]
    key_width, value_width = w_query.shape[1], w_value.shape[1]
    key_size, value_size = key_width // heads, out_gain.shape[0]
    mixer_width = 2 * key_width + value_width
    hidden_width = w_gate.shape[1]
    owned = w_query.shape[0]
    margin = CONV - 1
    me = lax.axis_index("dp") * 2 + lax.axis_index("c")
    mixer_part = mixer_width // group
    back_width = value_width // group
    ffn_width = hidden_width // group

    def shuffled(values):
        return (
            values.reshape(-1, rows, count, 2 * owned).swapaxes(1, 2).reshape(-1, width)
        )

    def unshuffled(values):
        return (
            values.reshape(-1, count, rows, 2 * owned).swapaxes(1, 2).reshape(-1, width)
        )

    def cut(values):
        return values.astype(BF16).reshape(owned, group, -1).swapaxes(0, 1)

    def joined(values):
        return values.swapaxes(0, 1).reshape(values.shape[1], -1)

    def gathered(values):
        return lax.all_gather(values.reshape(group * owned, -1), "zq", axis=0, tiled=True)

    def scattered(values):
        return lax.psum_scatter(
            values, "zq", scatter_dimension=0, tiled=True
        ).reshape(group, owned, -1)

    def blocks(values):
        return values.astype(BF16).reshape(group, length, -1)

    (
        mixer_weights,
        first_own,
        gate_up_own,
        normed_all,
        grad_all,
        hidden_low,
        normed_low,
        grad_low,
    ) = begin(
        hidden_in[0],
        grad_out[0],
        attn_gain[None],
        w_decay,
        w_beta,
        (w_query, w_key, w_value, w_outgate, w_output, w_down, w_gate, w_up),
        0,
    )
    mixer_weights = mixer_weights.reshape(width, -1)
    normed_all = normed_all.reshape(-1, width)
    grad_all = grad_all.reshape(-1, width)
    project = mixer_weights[:, : mixer_part + back_width]
    small_weights = mixer_weights[:, mixer_part + back_width :]
    first_weights = gathered(first_own)
    output_weights, down = first_weights[:, :back_width], first_weights[:, back_width:]

    inputs = hidden_low.astype(F32)
    attn_row, mlp_row = shuffled(attn_gain[None]), shuffled(mlp_gain[None])
    normed, norm_pull = jax.vjp(rms_scale, inputs)
    pre_all = mm(normed_all, project[:, :mixer_part])
    gate_all = mm(normed_all, project[:, mixer_part:])
    pre, rim = swap_on(blocks(pre_all), 3)
    small_pre = mm(normed_low, small_weights)
    decay_pre, beta_pre = small_pre[:, :heads], small_pre[:, heads : 2 * heads]
    rim_ids = lax.ppermute(
        segment[-margin:],
        ("zq", "c"),
        [(i, i + 1) for i in range(2 * count - 1)],
    )
    seg_ext = jnp.concatenate([rim_ids, segment])
    same = jnp.stack(
        [
            (segment == seg_ext[margin - lag : margin - lag + length]).astype(F32)
            for lag in range(CONV)
        ],
        axis=1,
    )
    (lines, decay), decay_pull = jax.vjp(
        partial(decays, segment, seg_ext[margin - 1]), decay_pre, beta_pre, a_log
    )
    slabs, slab = group, mixer_part
    if slab % key_size:
        slabs, slab = mixer_width // (3 * key_size), 3 * key_size
        pre, rim = [
            joined(part).reshape(-1, slabs, slab).swapaxes(0, 1) for part in (pre, rim)
        ]
    per = slab // key_size
    taps = jnp.concatenate([conv_query, conv_key, conv_value], axis=1)
    channel_blocks = [
        lambda h: h,
        lambda h: heads + h,
        lambda h: 2 * heads + 2 * h,
        lambda h: 2 * heads + 2 * h + 1,
    ]

    step = 3 if heads % 3 == 0 else 1

    def at_blocks(make, step):
        return [
            make(lambda h, b=b, u=u: b(step * h + u)) for u in range(step) for b in channel_blocks
        ]

    def token_specs(step):
        def in_slab(lines):
            return lambda at: pl.BlockSpec(
                (1, lines, key_size), lambda h: (at(h) // per, 0, at(h) % per)
            )

        return (
            at_blocks(in_slab(length), step)
            + at_blocks(in_slab(RIM), step)
            + at_blocks(lambda at: pl.BlockSpec((CONV, key_size), lambda h: (0, at(h))), step)
            + [pl.BlockSpec((length, CONV), lambda h: (0, 0))]
            + [by_heads(step, 8, length), by_heads(step, length, length)]
        )

    def token_args(step):
        blocks = 4 * step
        return (pre,) * blocks + (rim,) * blocks + (taps,) * blocks + (same, lines, decay)

    values_spec = by_columns(length, value_size)
    state_spec = by_head(key_size, value_size)
    inverse, scores, own, effect, offset, high, low, back_high, back_low = head_call(
        partial(chunk_forward_kernel, step),
        heads // step,
        token_specs(step),
        [
            by_heads(step, length, length),
            by_heads(step, length, length),
            by_columns(length, step * value_size),
            by_heads(step, length, key_size),
            by_heads(step, key_size, value_size),
        ]
        + [by_heads(step, key_size, key_size)] * 4,
        [
            shaped(heads, length, length),
            shaped(heads, length, length),
            shaped(length, value_width),
            shaped(heads, length, key_size),
            shaped(heads, key_size, value_size),
        ]
        + [shaped(heads, key_size, key_size, dtype=BF16)] * 4,
        token_args(step),
        6_000_000_000,
        [pltpu.VMEM((4 * step, RIM + length, key_size), F32)],
    )
    state, gate_back = chain(high, low, offset, (gate_all.reshape(group, length, -1),), True, 5)
    gate_pre = joined(gate_back)
    gate_up_own, state, first_weights = lax.optimization_barrier(
        (gate_up_own, state, first_weights)
    )
    gate_up = gathered(gate_up_own)
    gain_spec = pl.BlockSpec((1, value_size), lambda h: (0, 0))
    gain_row = out_gain[None]
    mixed, gated = head_call(
        gate_forward_kernel,
        heads,
        [values_spec, by_head(length, key_size), state_spec, values_spec, gain_spec],
        [values_spec, values_spec],
        [shaped(length, value_width), shaped(length, value_width, dtype=BF16)],
        (own, effect, state, gate_pre, gain_row),
        1_000_000_000,
    )
    gated_cut = gated.reshape(length, group, back_width).swapaxes(0, 1)
    gated_all = swap(gated_cut, 6).reshape(-1, back_width)
    middle, normed_two_all = turn(
        mm(gated_all, output_weights, (1, 1)).reshape(group, length, width),
        mlp_row,
        inputs,
        (),
        4,
    )
    normed_two_all = normed_two_all.reshape(-1, width)

    both = mm(normed_two_all, gate_up)
    hidden, swiglu_pull = jax.vjp(swiglu, both[:, :ffn_width], both[:, ffn_width:])
    hidden_low = hidden.astype(BF16)
    grad_gate, grad_up = swiglu_pull(mm(grad_all, down))
    both_grad_low = jnp.concatenate([grad_gate, grad_up], axis=1).astype(BF16)
    grad_normed_two_parts = mm(both_grad_low, gate_up, (1, 1)).reshape(group, length, width)
    mlp_parts = blocks(mm(hidden_low, down, (1, 1)))
    gate_up_rows = mm(normed_two_all, both_grad_low, (0, 0)).astype(BF16)
    grad_normed_two_parts, gate_up_rows = lax.optimization_barrier(
        (grad_normed_two_parts, gate_up_rows)
    )
    gate_up_rows = scattered(gate_up_rows)
    grad_middle, attended_grad_all, grad_mlp_gain, mlp_pairs = turn(
        grad_normed_two_parts, mlp_row, grad_low, (middle, mlp_parts), 2
    )
    attended_grad_all = attended_grad_all.reshape(-1, width)

    grad_gated = joined(swap(blocks(mm(attended_grad_all, output_weights)), 6))
    output_rows = mm(attended_grad_all, gated_all, (0, 0)).astype(BF16)
    down_rows = mm(grad_all, hidden_low, (0, 0)).astype(BF16)
    mixed_grad, gate_pre_grad, gain_grad, state_add = head_call(
        gate_backward_kernel,
        heads,
        [values_spec, values_spec, gain_spec, values_spec, by_head(length, key_size)],
        [values_spec, values_spec, by_head(1, value_size), state_spec],
        [
            shaped(length, value_width),
            shaped(length, value_width, dtype=BF16),
            shaped(heads, 1, value_size),
            shaped(heads, key_size, value_size),
        ],
        (mixed, gate_pre, gain_row, grad_gated, effect),
        1_000_000_000,
    )
    grad_out_gain = jnp.sum(gain_grad, axis=(0, 1))
    side_rows = jnp.concatenate([down_rows, output_rows], axis=1)
    state_add, gate_up_rows, side_rows = lax.optimization_barrier(
        (state_add, gate_up_rows, side_rows)
    )
    ending, gate_grad_back, mlp_back = chain(
        back_high,
        back_low,
        state_add,
        (gate_pre_grad.reshape(length, group, back_width).swapaxes(0, 1), mlp_pairs),
        False,
        8,
    )
    gate_grad_all = gate_grad_back.reshape(-1, back_width)
    side_rows, ending = lax.optimization_barrier((side_rows, ending))
    side_rows = scattered(side_rows)
    gate_up_back = lax.all_to_all(gate_up_rows, ("dp", "c"), 0, 0, tiled=True)
    whole = lambda *shape: pl.BlockSpec(shape, lambda h: (0, 0, 0))
    grad_pre, grad_tail, grad_rim, grad_taps, dlines, ddecay = head_call(
        partial(chunk_backward_kernel, heads),
        heads,
        token_specs(1)
        + [
            by_head(length, length),
            by_head(length, length),
            state_spec,
            values_spec,
            state_spec,
        ],
        [
            whole(slabs, length, slab),
            whole(slabs, RIM, slab),
            whole(slabs, RIM, slab),
            whole(slabs, 2 * CONV, slab),
        ]
        + [by_head(8, length), by_head(length, length)],
        [
            shaped(slabs, length, slab, dtype=BF16),
            shaped(slabs, RIM, slab),
            shaped(slabs, RIM, slab, dtype=BF16),
            shaped(slabs, 2 * CONV, slab),
            shaped(heads, 8, length),
            shaped(heads, length, length),
        ],
        token_args(1) + (inverse, scores, state, mixed_grad, ending),
        12_000_000_000,
        [pltpu.VMEM((4, RIM + length, key_size), F32), pltpu.VMEM((RIM + length, key_size), F32)],
    )
    grad_decay, grad_beta, grad_alog = decay_pull((dlines, ddecay))
    grad_taps = joined(grad_taps)[:CONV]
    grad_conv_one = grad_taps[:, :key_width]
    grad_conv_two = grad_taps[:, key_width : 2 * key_width]
    grad_conv_three = grad_taps[:, 2 * key_width :]
    small_grad = jnp.concatenate([grad_decay, grad_beta], axis=1).astype(BF16)
    small_grad = jnp.pad(small_grad, ((0, 0), (0, LANES - 2 * heads)))
    if slabs != group:
        grad_pre, grad_tail, grad_rim = [
            joined(part).reshape(-1, group, mixer_part).swapaxes(0, 1)
            for part in (grad_pre, grad_tail, grad_rim)
        ]
    grad_pre, gate_up_back = lax.optimization_barrier((grad_pre, gate_up_back))
    grads_all = swap_back(grad_pre, grad_tail, grad_rim, small_grad, 10).reshape(
        group * length, -1
    )
    mixer_parts = jnp.concatenate(
        [
            mm(normed_all, grads_all, (0, 0)).astype(BF16),
            mm(normed_all, gate_grad_all, (0, 0)).astype(BF16),
        ],
        axis=1,
    )
    mixer_parts, side_rows = lax.optimization_barrier((mixer_parts, side_rows))
    mixer_rows = scattered(mixer_parts)
    combined = fold(
        blocks(
            mm(
                jnp.concatenate([grads_all[:, :mixer_part], gate_grad_all], axis=1),
                project,
                (1, 1),
            )
        ),
        7,
    )
    mlp_part = jnp.sum(mlp_back.astype(F32), axis=0)
    result = (middle + mlp_part).astype(BF16)
    combined = combined + mm(small_grad, small_weights, (1, 1))
    grad_attn_gain = jnp.sum(combined * normed, axis=0)
    grad_inputs = grad_middle + norm_pull(combined * attn_row)[0]

    side_back = lax.all_to_all(side_rows, ("dp", "c"), 0, 0, tiled=True).astype(F32)
    gate_grad = joined(gate_up_back[:, :, :ffn_width].astype(F32))
    up_grad = joined(gate_up_back[:, :, ffn_width:].astype(F32))
    down_grad = joined(side_back[:, :, :ffn_width])
    output_grad = joined(side_back[:, :, ffn_width:])

    pieces = (
        grad_attn_gain,
        grad_alog,
        grad_conv_one,
        grad_conv_two,
        grad_conv_three,
        grad_out_gain,
        grad_mlp_gain,
    )
    flat = jnp.concatenate([piece.reshape(-1) for piece in pieces])
    lines = -(-flat.shape[0] // (group * 8 * LANES)) * 8
    flat = jnp.pad(flat, (0, group * lines * LANES - flat.shape[0])).reshape(group, lines, LANES)
    flat = jnp.sum(swap(flat, 11), axis=0)
    flat = jnp.sum(column(flat, 12), axis=0)
    flat = spread(flat, 16).reshape(-1)
    mixer_rows, _ = lax.optimization_barrier((mixer_rows, (flat, grad_inputs)))
    mixer_swapped = swap(
        jnp.concatenate(
            [mixer_rows[:, :, :mixer_part], mixer_rows[:, :, mixer_part + LANES :]], axis=2
        ),
        15,
    ).astype(F32)
    mixer_back = joined(mixer_swapped[:, :, :mixer_part])
    outgate_grad = joined(mixer_swapped[:, :, mixer_part:])
    small_rows = lax.dynamic_index_in_dim(mixer_rows, me, 0, keepdims=False)
    small_rows = small_rows[:, mixer_part : mixer_part + LANES].astype(F32)
    summed, at = [], 0
    for piece in pieces:
        summed.append(flat[at : at + piece.size].reshape(piece.shape))
        at += piece.size

    return (
        unshuffled(result)[None],
        unshuffled(grad_inputs.astype(BF16))[None],
        unshuffled(summed[0][None])[0],
        mixer_back[:, :key_width],
        mixer_back[:, key_width : 2 * key_width],
        mixer_back[:, 2 * key_width :],
        small_rows[:, :heads],
        small_rows[:, heads : 2 * heads],
        outgate_grad,
        summed[1],
        summed[2],
        summed[3],
        summed[4],
        summed[5],
        output_grad,
        unshuffled(summed[6][None])[0],
        gate_grad,
        up_grad,
        down_grad,
    )


def solution(mesh):
    rows, places = mesh.shape["dp"], mesh.shape["seq"]
    fine = Mesh(mesh.devices.reshape(rows, places // 2, 2), ("dp", "zq", "c"))
    tokens = P("dp", ("zq", "c"), None)
    owned = P(("dp", "zq", "c"), None)
    return jax.shard_map(
        local,
        mesh=fine,
        in_specs=(tokens, P("dp", ("zq", "c")), tokens, P())
        + (owned,) * 6
        + (P(),) * 5
        + (owned, P(), owned, owned, owned),
        out_specs=(tokens, tokens, P())
        + (owned,) * 6
        + (P(),) * 5
        + (owned, P(), owned, owned, owned),
        check_vma=False,
    )
```
